256 devices in a mesh: section: 16 (over z_hi, y, core), seq: 16 (over x, z_lo).
Axes of the slice: x: 4, y: 4, z: 8 (z_hi: 2, z_lo: 4; z = z_hi * 4 + z_lo), core: 2. Of those that a mesh axis runs over, the one named last changes fastest.
Arguments:
- base_ids: int32 [2, 2048], P(None, 'seq'), may hold values from 0 to 3
- stem_weight: bfloat16 [15, 4, 768], replicated, may hold values from -1.5 to 1.5
- conv_weight: bfloat16 [16, 5, 768, 768], P('section'), may hold values from -0.09375 to 0.09375
- block_gain: float32 [16, 768], P('section'), may hold values from 0.1 to 1.9
- cotangent: bfloat16 [2, 2048, 768], P(None, 'seq'), may hold values from -0.29882812 to 0.29882812
Outputs:
- conv_grad: bfloat16 [16, 5, 768, 768], P('section', None, 'seq')
- gain_grad: float32 [16, 768], P('section', 'seq')
The draws below stay inside these ranges and needn't reach their ends.
All inputs are finite; a program needn't handle non-finite values.
Results may differ from the reference program's by a relative error of at most 0.035.
Values may be sent and summed in bfloat16 or wider, within the bound.
No kernel may reach another device: no remote copies, remote signals or barrier semaphores. Data moves between devices by JAX's collectives and lax.ppermute only.
A program may use at most 128 MiB of HBM per device.

```python
import jax
import jax.numpy as jnp
from jax import lax

C = 768
KERNEL = 5
STEM_K = 15
BASES = 4
MICRO = 2
TOK_DEV = 128
TOKENS = 2048
N_SECTION = 16
N_SEQ = 16


def plant(values, stream_key, least, largest):
    longest = values.shape.index(max(values.shape))
    spots = []
    for shift in (0, 1):
        where = [jax.random.randint(jax.random.fold_in(stream_key, axis), (), 0, length) for axis, length in enumerate(values.shape)]
        where[longest] = (where[longest] + shift) % values.shape[longest]
        spots.append(tuple(where))
    return values.at[spots[0]].set(least).at[spots[1]].set(largest)


def block_scale(rng, dims, cuts, low, largest):
    factor_of, own = 1.0, jax.random.fold_in(rng, 6)
    for position, blocks in cuts:
        heights = jnp.exp(jax.random.uniform(jax.random.fold_in(own, position), (blocks,), jnp.float32, low / len(cuts), largest / len(cuts)))
        factor_of = factor_of * jnp.repeat(heights, dims[position] // blocks).reshape([-1 if axis == position else 1 for axis in range(len(dims))])
    return factor_of


def bell_draw(key, shape, deviation, reach, split=(), kind=jnp.bfloat16):
    level = block_scale(key, shape, split, -0.22, 0.18) if split else 1.0
    result = jax.random.normal(key, shape, jnp.float32) * deviation * level
    return jnp.minimum(jnp.maximum(result, -reach), reach).astype(kind)


def setup_inputs(seed: int = 0) -> dict:
    key_of = jax.random.split(jax.random.key(seed), 6)
    return {
        "base_ids": plant(jax.random.randint(key_of[0], (MICRO, TOKENS), 0, 4), jax.random.fold_in(key_of[0], 1), 0, 3).astype(jnp.int32),
        "stem_weight": bell_draw(key_of[1], (STEM_K, BASES, C), STEM_K ** -0.5, 1.5),
        "conv_weight": bell_draw(key_of[2], (N_SECTION, KERNEL, C, C), (KERNEL * C) ** -0.5, 0.09375, ((0, 16),)),
        "block_gain": jnp.clip(1.0 + 0.18 * jax.random.normal(key_of[3], (N_SECTION, C), jnp.float32), 0.1, 1.9),
        "cotangent": bell_draw(key_of[4], (MICRO, TOKENS, C), 0.05, 0.29882812, ((1, 16),)),
    }


def activate(block_sum, gain_row):
    scale = lax.rsqrt(lax.optimization_barrier(jnp.mean(block_sum * block_sum, axis=-1, keepdims=True)) + 1e-06)
    return jax.nn.gelu(block_sum * scale * gain_row)

def rounded_sum(partials):
    held = lax.optimization_barrier(partials.astype(jnp.bfloat16))
    return lax.optimization_barrier(jnp.sum(held.astype(jnp.float32), axis=0))

def conv_apply(activated, filters):
    row_count = activated.shape[1]
    conv_reach = (KERNEL - 1) // 2
    padded = jnp.pad(activated, ((0, 0), (conv_reach, conv_reach), (0, 0))).astype(jnp.float32)
    summed = jnp.zeros(activated.shape, jnp.float32)
    for offset in range(KERNEL):
        summed = summed + jnp.einsum('mtc,cd->mtd', padded[:, offset:offset + row_count], filters[offset].astype(jnp.float32))
    return summed

def conv_back(grad_out, filters):
    row_count = grad_out.shape[1]
    conv_reach = (KERNEL - 1) // 2
    padded = jnp.pad(grad_out, ((0, 0), (conv_reach, conv_reach), (0, 0))).astype(jnp.float32)
    summed = jnp.zeros(grad_out.shape, jnp.float32)
    for offset in range(KERNEL):
        start = 2 * conv_reach - offset
        summed = summed + jnp.einsum('mtd,cd->mtc', padded[:, start:start + row_count], filters[offset].astype(jnp.float32))
    return summed

def reference(base_ids, stem_weight, conv_weight, block_gain, cotangent):
    micro_count = base_ids.shape[0]
    total_rows = base_ids.shape[1]
    section_count = conv_weight.shape[0]
    half_count = section_count // 2
    conv_reach = (KERNEL - 1) // 2
    stem_reach = (STEM_K - 1) // 2
    padded_ids = jnp.pad(base_ids + 1, ((0, 0), (stem_reach, stem_reach)))
    letters = jnp.arange(1, BASES + 1, dtype=jnp.int32)
    stem_sum = jnp.zeros((micro_count, total_rows, C), jnp.float32)
    for offset in range(STEM_K):
        onehot = (padded_ids[:, offset:offset + total_rows, None] == letters).astype(jnp.float32)
        stem_sum = stem_sum + jnp.einsum('mtb,bc->mtc', onehot, stem_weight[offset].astype(jnp.float32))
    stream = stem_sum.astype(jnp.bfloat16)
    skip_list = []
    saved = []
    for block_index in range(section_count):
        block_sum = stream.astype(jnp.float32)
        if block_index >= half_count:
            block_sum = block_sum + skip_list[section_count - 1 - block_index].astype(jnp.float32)
        activated = activate(block_sum, block_gain[block_index]).astype(jnp.bfloat16)
        stream = (block_sum + conv_apply(activated, conv_weight[block_index])).astype(jnp.bfloat16)
        saved.append((block_sum, activated))
        if block_index < half_count:
            skip_list.append(stream)
    grad_flow = cotangent
    skip_grads = [None] * half_count
    kernel_grads = [None] * section_count
    gain_grads = [None] * section_count
    shape_four = (micro_count, N_SEQ, TOK_DEV, C)
    for block_index in reversed(range(section_count)):
        block_sum, activated = saved[block_index]
        from_next = grad_flow.astype(jnp.float32)
        if block_index < half_count:
            from_next = from_next + skip_grads[block_index].astype(jnp.float32)
        grad_out = from_next.astype(jnp.bfloat16)
        grad_act = conv_back(grad_out, conv_weight[block_index])
        padded = jnp.pad(activated, ((0, 0), (conv_reach, conv_reach), (0, 0))).astype(jnp.float32)
        grad_four = grad_out.astype(jnp.float32).reshape(shape_four)
        per_offset = []
        for offset in range(KERNEL):
            window = padded[:, offset:offset + total_rows].reshape(shape_four)
            per_offset.append(rounded_sum(jnp.einsum('mqtc,mqtd->qcd', window, grad_four)))
        kernel_grads[block_index] = jnp.stack(per_offset)

        def blockwise(sum_four, gain_rows):
            return activate(sum_four, gain_rows[None, :, None, :])
        gain_rows = jnp.broadcast_to(block_gain[block_index], (N_SEQ, C))
        unused_out, pullback = jax.vjp(blockwise, block_sum.reshape(shape_four), gain_rows)
        grad_norm_in, grad_gain = pullback(grad_act.reshape(shape_four))
        gain_grads[block_index] = rounded_sum(grad_gain)
        grad_in = (grad_out.astype(jnp.float32) + grad_norm_in.reshape(block_sum.shape)).astype(jnp.bfloat16)
        if block_index >= half_count:
            skip_grads[section_count - 1 - block_index] = grad_in
        grad_flow = grad_in
    conv_grad = jnp.stack(kernel_grads).astype(jnp.bfloat16)
    gain_grad = jnp.stack(gain_grads)
    return (conv_grad, gain_grad)
```

```python
import functools

import jax
import jax.numpy as jnp
from jax import lax
from jax.experimental import pallas as pl
from jax.experimental.pallas import tpu as pltpu
from jax.sharding import PartitionSpec as P

KERNEL = 5
STEM_K = 15
BASES = 4
C = 768
ROWS = 128
HALO = 8
WIDE = ROWS + 2 * HALO
PAD = WIDE + 16
STAGES = 8
BLOCKS = 16
SPAN = 4
TOKENS = BLOCKS * ROWS
AXES = ("section", "seq")
BF16 = jnp.bfloat16
F32 = jnp.float32
GELU_A = 0.7978845608028654
GELU_B = 0.044715
VMEM_SPEC = pl.BlockSpec(memory_space=pltpu.VMEM)
SMEM_SPEC = pl.BlockSpec(memory_space=pltpu.SMEM)
ANY_SPEC = pl.BlockSpec(memory_space=pl.ANY)


def place(stage, core, block):
    x, z = block // SPAN, block % SPAN
    column = x * SPAN + (SPAN - 1 - z if stage >= STAGES // 2 else z)
    return (2 * stage + core) * BLOCKS + column


def moved(array, source, target, shift=0):
    route = [
        (place(source, core, block), place(target, core, block + shift))
        for core in range(2)
        for block in range(BLOCKS)
        if 0 <= block + shift < BLOCKS
    ]
    return lax.ppermute(array, AXES, route)


def swapped(array):
    return lax.ppermute(array, "section", [(i, i ^ 1) for i in range(2 * STAGES)])


def turned_x(array, distance):
    route = [
        (x * SPAN + z, (x + distance) % SPAN * SPAN + z) for x in range(SPAN) for z in range(SPAN)
    ]
    return lax.ppermute(array, "seq", route)


def turned_z(array, distance):
    route = [
        (x * SPAN + z, x * SPAN + (z + distance) % SPAN) for x in range(SPAN) for z in range(SPAN)
    ]
    return lax.ppermute(array, "seq", route)


def hop(pieces, source, target):
    main, first, last = pieces
    return (
        moved(main, source, target),
        moved(last, source, target, 1),
        moved(first, source, target, -1),
    )


def params(mib):
    return pltpu.CompilerParams(vmem_limit_bytes=mib << 20)


def row_mask(block):
    row = lax.broadcasted_iota(jnp.int32, (WIDE, 1), 0) + (block * ROWS - HALO)
    return (row >= 0) & (row < TOKENS)


def normed(total):
    scale = lax.rsqrt(jnp.mean(total * total, axis=-1, keepdims=True) + 1e-06)
    return total * scale, scale


def forward_kernel(tick, info, *refs):
    skips = tick >= STAGES // 2
    last = tick == STAGES - 1
    refs = list(refs)
    main, left, right = refs[:3]
    refs = refs[3:]
    own_skip = refs.pop(0) if tick > STAGES // 2 else None
    skip_b = refs.pop(0) if skips else None
    filters, gains, whole, middle, act_a, act_b, sum_a, sum_b = refs[:8]
    out, first_rows, last_rows = refs[8:11] if not last else (None, None, None)
    pad = refs[-1]

    @pl.when(info[0] == tick)
    def _():
        keep = row_mask(info[1])
        whole[0:HALO, :] = left[...]
        whole[HALO : HALO + ROWS, :] = main[...]
        whole[HALO + ROWS : WIDE, :] = right[...]
        pad[0:8, :] = jnp.zeros((8, C), F32)
        pad[PAD - 8 : PAD, :] = jnp.zeros((8, C), F32)

        def activated(total, which, act):
            value, _ = normed(total)
            value = jax.nn.gelu(value * gains[which : which + 1, :])
            rounded = jnp.where(keep, value, 0.0).astype(BF16)
            act[...] = rounded
            pad[8 : 8 + WIDE, :] = rounded.astype(F32)

        def conv(total, which):
            for tap in range(KERNEL):
                start = 6 + tap
                total = total + jnp.dot(
                    pad[start : start + WIDE, :].astype(BF16),
                    filters[which, tap],
                    preferred_element_type=F32,
                )
            return total

        total = whole[...].astype(F32)
        if tick == STAGES // 2:
            total = total + total
        elif skips:
            total = total + own_skip[...].astype(F32)
        sum_a[...] = total
        activated(total, 0, act_a)
        value = conv(total, 0).astype(BF16)
        middle[...] = value
        total = value.astype(F32)
        if skips:
            total = total + skip_b[...].astype(F32)
        sum_b[...] = total
        activated(total, 1, act_b)
        if not last:
            value = conv(total, 1)
            out[...] = value[HALO : HALO + ROWS].astype(BF16)
            first_rows[...] = value[HALO : 2 * HALO].astype(BF16)
            last_rows[...] = value[ROWS : HALO + ROWS].astype(BF16)


def forward(tick, info, pieces, skip_a, skip_b, filters, gains):
    last = tick == STAGES - 1
    args = list(pieces)
    if skip_a is not None:
        args.append(skip_a)
    if skip_b is not None:
        args.append(skip_b)
    wide = jax.ShapeDtypeStruct((WIDE, C), BF16)
    total = jax.ShapeDtypeStruct((WIDE, C), F32)
    edge = jax.ShapeDtypeStruct((HALO, C), BF16)
    shapes = [wide, wide, wide, wide, total, total]
    if not last:
        shapes += [jax.ShapeDtypeStruct((ROWS, C), BF16), edge, edge]
    return pl.pallas_call(
        functools.partial(forward_kernel, tick),
        out_shape=shapes,
        in_specs=[SMEM_SPEC] + [VMEM_SPEC] * (len(args) + 2),
        out_specs=[VMEM_SPEC] * len(shapes),
        scratch_shapes=[pltpu.VMEM((PAD, C), F32)],
        compiler_params=params(16),
        name="forward_stage",
    )(info, *args, filters, gains)


def backward_kernel(tick, info, *refs):
    joined = tick < STAGES // 2
    refs = list(refs)
    main, left, right = refs[:3]
    refs = refs[3:]
    skip_a = refs.pop(0) if tick < STAGES // 2 - 1 else None
    skip_b = refs.pop(0) if joined else None
    sum_a, sum_b, filters, gains, whole, middle, grad_a, grad_b, gain_out = refs[:9]
    out, first_rows, last_rows = refs[9:12] if tick else (None, None, None)
    pad = refs[-1]

    @pl.when(info[0] == tick)
    def _():
        keep = row_mask(info[1])
        whole[0:HALO, :] = left[...]
        whole[HALO : HALO + ROWS, :] = main[...]
        whole[HALO + ROWS : WIDE, :] = right[...]
        pad[0:8, :] = jnp.zeros((8, C), F32)
        pad[PAD - 8 : PAD, :] = jnp.zeros((8, C), F32)

        def pull(grad, total_ref, which, grad_ref, last):
            grad_ref[...] = grad[HALO : HALO + ROWS].astype(BF16)
            pad[8 : 8 + WIDE, :] = grad
            grad_act = jnp.zeros((WIDE, C), F32)
            for tap in range(KERNEL):
                start = 10 - tap
                grad_act = grad_act + lax.dot_general(
                    pad[start : start + WIDE, :].astype(BF16),
                    filters[which, tap],
                    (((1,), (1,)), ((), ())),
                    preferred_element_type=F32,
                )
            total = total_ref[...]
            gain = gains[which : which + 1, :]
            value, scale = normed(total)
            inner = value * gain
            square = inner * inner
            tanh = jnp.tanh(GELU_A * (inner + GELU_B * (square * inner)))
            slope = 0.5 * (1.0 + tanh) + (0.5 * GELU_A) * inner * (1.0 - tanh * tanh) * (
                1.0 + (3.0 * GELU_B) * square
            )
            grad_inner = grad_act * slope
            product = (grad_inner * value)[HALO : HALO + ROWS]
            gain_out[which : which + 1, :] = jnp.sum(product, axis=0, keepdims=True)
            if last:
                return None
            grad_value = grad_inner * gain
            mean = jnp.mean(grad_value * value, axis=-1, keepdims=True)
            result = grad + scale * (grad_value - value * mean)
            return jnp.where(keep, result, 0.0).astype(BF16)

        grad = whole[...].astype(F32)
        if tick == STAGES // 2 - 1:
            grad = grad + grad
        elif joined:
            grad = grad + skip_a[...].astype(F32)
        grad = grad.astype(BF16).astype(F32)
        value = pull(grad, sum_b, 1, grad_b, False)
        middle[...] = value
        grad = value.astype(F32)
        if joined:
            grad = (grad + skip_b[...].astype(F32)).astype(BF16).astype(F32)
        value = pull(grad, sum_a, 0, grad_a, tick == 0)
        if tick:
            value = value.astype(F32)
            out[...] = value[HALO : HALO + ROWS].astype(BF16)
            first_rows[...] = value[HALO : 2 * HALO].astype(BF16)
            last_rows[...] = value[ROWS : HALO + ROWS].astype(BF16)


def backward(tick, info, pieces, skip_a, skip_b, sums, filters, gains):
    args = list(pieces)
    if skip_a is not None:
        args.append(skip_a)
    if skip_b is not None:
        args.append(skip_b)
    wide = jax.ShapeDtypeStruct((WIDE, C), BF16)
    own = jax.ShapeDtypeStruct((ROWS, C), BF16)
    edge = jax.ShapeDtypeStruct((HALO, C), BF16)
    shapes = [wide, wide, own, own, jax.ShapeDtypeStruct((2, C), F32)]
    if tick:
        shapes += [own, edge, edge]
    return pl.pallas_call(
        functools.partial(backward_kernel, tick),
        out_shape=shapes,
        in_specs=[SMEM_SPEC] + [VMEM_SPEC] * (len(args) + 4),
        out_specs=[VMEM_SPEC] * len(shapes),
        scratch_shapes=[pltpu.VMEM((PAD, C), F32)],
        compiler_params=params(16),
        name="backward_stage",
    )(info, *args, *sums, filters, gains)


def pair_kernel(info, own, other, pair, sems):
    core = info[2]
    copies = [
        pltpu.make_async_copy(own.at[0], pair.at[core], sems.at[0]),
        pltpu.make_async_copy(other.at[0], pair.at[1 - core], sems.at[1]),
    ]
    for copy in copies:
        copy.start()
    for copy in copies:
        copy.wait()


def paired(info, own, other):
    return pl.pallas_call(
        pair_kernel,
        out_shape=pltpu.VMEM((2, *own.shape[1:]), own.dtype),
        in_specs=[SMEM_SPEC, ANY_SPEC, ANY_SPEC],
        out_specs=VMEM_SPEC,
        scratch_shapes=[pltpu.SemaphoreType.DMA((2,))],
        compiler_params=params(14),
        name="weight_pair",
    )(info, own, other)


def product_kernel(rows_t, *refs):
    pieces, outs, total = refs[:SPAN], refs[SPAN : 2 * SPAN], refs[-1]
    count = 2 * ROWS
    for index, piece in enumerate(pieces):
        term = jnp.dot(
            rows_t[:, index * count : (index + 1) * count],
            piece[0:count, :],
            preferred_element_type=F32,
        )
        total[...] = term if index == 0 else total[...] + term
    gain = sum(piece[count : count + 8, :].astype(F32) for piece in pieces).astype(BF16)
    height = total.shape[0] // SPAN
    for index, out in enumerate(outs):
        out[0:height, :] = total[index * height : (index + 1) * height, :].astype(BF16)
        out[height : height + 8, :] = gain


def product(rows_t, pieces):
    height = rows_t.shape[0] // SPAN + 8
    return pl.pallas_call(
        product_kernel,
        out_shape=[jax.ShapeDtypeStruct((height, C), BF16)] * SPAN,
        in_specs=[VMEM_SPEC] * (1 + SPAN),
        out_specs=[VMEM_SPEC] * SPAN,
        scratch_shapes=[pltpu.VMEM((rows_t.shape[0], C), F32)],
        compiler_params=params(24),
        name="kernel_grad",
    )(rows_t, *pieces)


def chosen(stage, arrays):
    result = arrays[0]
    for index, array in enumerate(arrays[1:], 1):
        result = jnp.where(stage == index, array, result)
    return result


def shards(base_ids, stem_weight, conv_weight, block_gain, cotangent):
    section = lax.axis_index("section")
    column = lax.axis_index("seq")
    stage, core = section // 2, section % 2
    x, z = column // SPAN, column % SPAN
    late = stage >= STAGES // 2
    block = x * SPAN + jnp.where(late, SPAN - 1 - z, z)
    info = jnp.stack([stage, block, core]).astype(jnp.int32)

    filters = paired(info, conv_weight, swapped(conv_weight))
    other_gain = swapped(block_gain)
    gains = jnp.where(
        core == 0,
        jnp.concatenate([block_gain, other_gain], 0),
        jnp.concatenate([other_gain, block_gain], 0),
    )

    reach = HALO + STEM_K // 2
    ids = base_ids + 1
    ids = jnp.concatenate(
        [moved(ids[:, -reach:], 0, 0, 1), ids, moved(ids[:, :reach], 0, 0, -1)], 1
    )
    ids = lax.dynamic_index_in_dim(ids, core, 0, keepdims=False)
    letters = jnp.arange(1, BASES + 1, dtype=jnp.int32)
    onehot = jnp.concatenate(
        [ids[offset : offset + WIDE, None] == letters for offset in range(STEM_K)], axis=1
    ).astype(BF16)
    stem = jnp.dot(
        onehot, stem_weight.reshape(STEM_K * BASES, C), preferred_element_type=F32
    ).astype(BF16)

    last = STAGES - 1
    cot = lax.dynamic_index_in_dim(cotangent, core, 0, keepdims=False)

    def cot_moved(rows, shift):
        route = [
            ((2 * last + c) * BLOCKS + b, place(last, c, b + shift))
            for c in range(2)
            for b in range(BLOCKS)
            if 0 <= b + shift < BLOCKS
        ]
        return lax.ppermute(rows, AXES, route)

    cot_pieces = (
        cot_moved(cot, 0),
        cot_moved(cot[ROWS - HALO :], 1),
        cot_moved(cot[:HALO], -1),
    )

    pieces = (stem[HALO : HALO + ROWS], stem[:HALO], stem[HALO + ROWS :])
    skip_whole, skip_middle, sums, acts = {}, {}, [], []
    half = STAGES // 2
    for tick in range(STAGES):
        results = forward(
            tick,
            info,
            pieces,
            skip_whole.get(tick),
            skip_middle.get(tick),
            filters,
            gains,
        )
        whole, middle, act_a, act_b, sum_a, sum_b = results[:6]
        sums.append((sum_a, sum_b))
        acts.append((act_a, act_b))
        if tick < last:
            pieces = hop(results[6:], tick, tick + 1)
        if tick < half:
            skip_middle[last - tick] = moved(middle, tick, last - tick)
            if tick:
                skip_whole[STAGES - tick] = moved(whole, tick, STAGES - tick)

    keep = chosen(stage, [jnp.where(core == 0, a, b) for a, b in acts])
    give = chosen(stage, [jnp.where(core == 0, b, a) for a, b in acts])
    both = jnp.stack([keep, swapped(give)])
    width = C // SPAN
    split = both.reshape(2, WIDE, SPAN, width).transpose(2, 0, 1, 3)

    def slice_for(distance):
        return lax.dynamic_index_in_dim(split, (x + distance) % SPAN, 0, keepdims=False)

    gathered = jnp.stack(
        [slice_for(0)] + [turned_x(slice_for(d), d) for d in range(1, SPAN)]
    )
    taps = jnp.stack(
        [gathered[:, :, HALO - 2 + k : HALO - 2 + k + ROWS] for k in range(KERNEL)]
    )
    share = width // SPAN
    rows_t = taps.reshape(KERNEL, SPAN * 2 * ROWS, SPAN, share).transpose(2, 0, 3, 1)
    rows_t = jnp.concatenate(
        [
            lax.dynamic_index_in_dim(rows_t, (z + d) % SPAN, 0, keepdims=False)
            for d in range(SPAN)
        ],
        0,
    ).reshape(SPAN * KERNEL * share, SPAN * 2 * ROWS)

    pieces = cot_pieces
    skip_whole, skip_middle, grads, gain_parts = {}, {}, [None] * STAGES, [None] * STAGES
    for tick in reversed(range(STAGES)):
        results = backward(
            tick,
            info,
            pieces,
            skip_whole.get(tick),
            skip_middle.get(tick),
            sums[tick],
            filters,
            gains,
        )
        whole, middle, grad_a, grad_b, gain_part = results[:5]
        grads[tick] = (grad_a, grad_b)
        gain_parts[tick] = gain_part
        if tick:
            pieces = hop(results[5:], tick, tick - 1)
        if tick >= half:
            skip_middle[last - tick] = moved(middle, tick, last - tick)
            if tick < last:
                skip_whole[last - 1 - tick] = moved(whole, tick, last - 1 - tick)

    gain_part = chosen(stage, gain_parts)
    keep = chosen(stage, [jnp.where(core == 0, a, b) for a, b in grads])
    give = chosen(stage, [jnp.where(core == 0, b, a) for a, b in grads])
    keep_gain = jnp.where(core == 0, gain_part[0:1], gain_part[1:2])
    give_gain = jnp.where(core == 0, gain_part[1:2], gain_part[0:1])
    none = jnp.zeros((7, C), BF16)
    got = swapped(jnp.concatenate([give, give_gain.astype(BF16), none], 0))
    total_gain = keep_gain + got[ROWS : ROWS + 1].astype(F32)
    both = jnp.concatenate([keep, got[:ROWS], total_gain.astype(BF16), none], 0)
    parts = product(rows_t, [both] + [turned_x(both, d) for d in range(1, SPAN)])
    total = parts[0].astype(F32)
    for d in range(1, SPAN):
        total = total + turned_z(parts[d], d).astype(F32)
    height = KERNEL * share
    kernel_grad = total[:height].astype(BF16).reshape(1, KERNEL, share, C)
    gain_grad = lax.dynamic_slice_in_dim(total[height], column * share, share)
    return kernel_grad, gain_grad[None]


def solution(mesh):
    placed = (
        P(None, "seq"),
        P(),
        P("section", None, None, None),
        P("section", None),
        P(None, "seq", None),
    )
    return jax.shard_map(
        shards,
        mesh=mesh,
        in_specs=placed,
        out_specs=(P("section", None, "seq", None), P("section", "seq")),
        check_vma=False,
    )
```

```python
import functools

import jax
import jax.numpy as jnp
from jax import lax
from jax.experimental import pallas as pl
from jax.experimental.pallas import tpu as pltpu
from jax.sharding import PartitionSpec as P

KERNEL = 5
STEM_K = 15
BASES = 4
C = 768
ROWS = 128
HALO = 8
WIDE = ROWS + 2 * HALO
PAD = WIDE + 16
STAGES = 8
BLOCKS = 16
SPAN = 4
TOKENS = BLOCKS * ROWS
AXES = ("section", "seq")
BF16 = jnp.bfloat16
F32 = jnp.float32
GELU_A = 0.7978845608028654
GELU_B = 0.044715
VMEM_SPEC = pl.BlockSpec(memory_space=pltpu.VMEM)
SMEM_SPEC = pl.BlockSpec(memory_space=pltpu.SMEM)
HBM_SPEC = pl.BlockSpec(memory_space=pltpu.HBM)


def place(stage, core, block):
    x, z = block // SPAN, block % SPAN
    column = x * SPAN + (SPAN - 1 - z if stage >= STAGES // 2 else z)
    return (2 * stage + core) * BLOCKS + column


def moved(array, source, target, shift=0):
    route = [
        (place(source, core, block), place(target, core, block + shift))
        for core in range(2)
        for block in range(BLOCKS)
        if 0 <= block + shift < BLOCKS
    ]
    return lax.ppermute(array, AXES, route)


def swapped(array):
    return lax.ppermute(array, "section", [(i, i ^ 1) for i in range(2 * STAGES)])


def beside(array, shift):
    route = [(b, b + shift) for b in range(BLOCKS) if 0 <= b + shift < BLOCKS]
    return lax.ppermute(array, "seq", route)


def turned_x(array, distance):
    route = [
        (x * SPAN + z, (x + distance) % SPAN * SPAN + z) for x in range(SPAN) for z in range(SPAN)
    ]
    return lax.ppermute(array, "seq", route)


def turned_z(array, distance):
    route = [
        (x * SPAN + z, x * SPAN + (z + distance) % SPAN) for x in range(SPAN) for z in range(SPAN)
    ]
    return lax.ppermute(array, "seq", route)


def everywhere(array, step, shift=0):
    route = [
        (place(stage, core, block), place(stage + step, core, block + shift))
        for stage in range(STAGES)
        for core in range(2)
        for block in range(BLOCKS)
        if 0 <= stage + step < STAGES and 0 <= block + shift < BLOCKS
    ]
    return lax.ppermute(array, AXES, route)


def hop(pieces, step):
    main, first, last = pieces
    return (
        everywhere(main, step),
        everywhere(last, step, 1),
        everywhere(first, step, -1),
    )


def after(array, event):
    return lax.optimization_barrier((array, event))[0]


def params(mib):
    return pltpu.CompilerParams(vmem_limit_bytes=mib << 20)


def row_mask(block):
    row = lax.broadcasted_iota(jnp.int32, (WIDE, 1), 0) + (block * ROWS - HALO)
    return (row >= 0) & (row < TOKENS)


def normed(total):
    scale = lax.rsqrt(jnp.mean(total * total, axis=-1, keepdims=True) + 1e-06)
    return total * scale, scale


def load_filters(core, own, other, held, sems, order):
    def start(first, second):
        for which in order:
            source = (first, second)[which]
            for tap in range(KERNEL):
                pltpu.make_async_copy(
                    source.at[0, tap], held.at[which, tap], sems.at[which, tap]
                ).start()

    @pl.when(core == 0)
    def _():
        start(own, other)

    @pl.when(core != 0)
    def _():
        start(other, own)


def wait_filter(own, held, sems, which, tap):
    pltpu.make_async_copy(own.at[0, tap], held.at[which, tap], sems.at[which, tap]).wait()


def forward_kernel(tick, info, *refs):
    skips = tick >= STAGES // 2
    last = tick == STAGES - 1
    refs = list(refs)
    main, left, right = refs[:3]
    refs = refs[3:]
    own_skip = refs.pop(0) if tick > STAGES // 2 else None
    skip_b = refs.pop(0) if skips else None
    own, other, gains, _, sums_out, acts_out = refs[:6]
    refs = refs[6:]
    out, first_rows, last_rows = (refs.pop(0), refs.pop(0), refs.pop(0)) if not last else (None,) * 3
    middle = refs.pop(0) if not skips else None
    whole_out = refs.pop(0) if 0 < tick < STAGES // 2 else None
    whole, pad, sums, acts, held, filter_sems, sems = refs

    @pl.when(info[0] == tick)
    def _():
        core = info[2]
        load_filters(core, own, other, held, filter_sems, (0, 1))
        keep = row_mask(info[1])
        whole[0:HALO, :] = left[...]
        whole[HALO : HALO + ROWS, :] = main[...]
        whole[HALO + ROWS : WIDE, :] = right[...]
        pad[0:8, :] = jnp.zeros((8, C), F32)
        pad[PAD - 8 : PAD, :] = jnp.zeros((8, C), F32)
        if whole_out is not None:
            whole_out[...] = whole[...]
        sum_copies = [
            pltpu.make_async_copy(sums.at[i], sums_out.at[i], sems.at[i]) for i in range(2)
        ]
        act_copies = [
            pltpu.make_async_copy(acts.at[0], acts_out.at[core], sems.at[2]),
            pltpu.make_async_copy(acts.at[1], acts_out.at[1 - core], sems.at[3]),
        ]

        def activated(total, which):
            sums[which] = total
            sum_copies[which].start()
            value, _ = normed(total)
            value = jax.nn.gelu(value * gains[which : which + 1, :])
            rounded = jnp.where(keep, value, 0.0).astype(BF16)
            acts[which] = rounded
            act_copies[which].start()
            pad[8 : 8 + WIDE, :] = rounded.astype(F32)

        def conv(total, which):
            for tap in range(KERNEL):
                start = 6 + tap
                rows = pad[start : start + WIDE, :].astype(BF16)
                wait_filter(own, held, filter_sems, which, tap)
                total = total + jnp.dot(rows, held[which, tap], preferred_element_type=F32)
            return total

        total = whole[...].astype(F32)
        if tick == STAGES // 2:
            total = total + total
        elif skips:
            total = total + own_skip[...].astype(F32)
        activated(total, 0)
        value = conv(total, 0).astype(BF16)
        if middle is not None:
            middle[...] = value
        total = value.astype(F32)
        if skips:
            total = total + skip_b[...].astype(F32)
        activated(total, 1)
        if last:
            for tap in range(KERNEL):
                wait_filter(own, held, filter_sems, 1, tap)
        else:
            value = conv(total, 1)
            out[...] = value[HALO : HALO + ROWS].astype(BF16)
            first_rows[...] = value[HALO : 2 * HALO].astype(BF16)
            last_rows[...] = value[ROWS : HALO + ROWS].astype(BF16)
        for copy in sum_copies + act_copies:
            copy.wait()


def forward(tick, info, pieces, skip_a, skip_b, own, other, gains, kept):
    last = tick == STAGES - 1
    half = STAGES // 2
    args = list(pieces)
    if skip_a is not None:
        args.append(skip_a)
    if skip_b is not None:
        args.append(skip_b)
    wide = jax.ShapeDtypeStruct((WIDE, C), BF16)
    edge = jax.ShapeDtypeStruct((HALO, C), BF16)
    shapes = [
        jax.ShapeDtypeStruct((2, WIDE, C), F32),
        jax.ShapeDtypeStruct(kept.shape, kept.dtype),
    ]
    specs = [HBM_SPEC, HBM_SPEC]
    vmem_shapes = [] if last else [jax.ShapeDtypeStruct((ROWS, C), BF16), edge, edge]
    if tick < half:
        vmem_shapes.append(wide)
    if 0 < tick < half:
        vmem_shapes.append(wide)
    count = 1 + len(args)
    return pl.pallas_call(
        functools.partial(forward_kernel, tick),
        out_shape=shapes + vmem_shapes,
        in_specs=[SMEM_SPEC]
        + [VMEM_SPEC] * len(args)
        + [HBM_SPEC, HBM_SPEC, VMEM_SPEC, HBM_SPEC],
        out_specs=specs + [VMEM_SPEC] * len(vmem_shapes),
        scratch_shapes=[
            pltpu.VMEM((WIDE, C), BF16),
            pltpu.VMEM((PAD, C), F32),
            pltpu.VMEM((2, WIDE, C), F32),
            pltpu.VMEM((2, WIDE, C), BF16),
            pltpu.VMEM((2, KERNEL, C, C), BF16),
            pltpu.SemaphoreType.DMA((2, KERNEL)),
            pltpu.SemaphoreType.DMA((4,)),
        ],
        input_output_aliases={count + 3: 1},
        compiler_params=params(24),
        name="forward_stage",
    )(info, *args, own, other, gains, kept)


def backward_kernel(tick, info, *refs):
    half = STAGES // 2
    joined = tick < half
    refs = list(refs)
    main, left, right = refs[:3]
    refs = refs[3:]
    skip_a = refs.pop(0) if tick < half - 1 else None
    skip_b = refs.pop(0) if joined else None
    sums_in, own, other, gains, _, grads_out = refs[:6]
    refs = refs[6:]
    out, first_rows, last_rows = (refs.pop(0), refs.pop(0), refs.pop(0)) if tick else (None,) * 3
    middle = refs.pop(0) if not joined else None
    whole_out = refs.pop(0) if half <= tick < STAGES - 1 else None
    whole, pad, sums, grads, held, filter_sems, sems = refs

    @pl.when(info[0] == tick)
    def _():
        core = info[2]
        sum_copies = [
            pltpu.make_async_copy(sums_in.at[i], sums.at[i], sems.at[i]) for i in range(2)
        ]
        sum_copies[1].start()
        load_filters(core, own, other, held, filter_sems, (1, 0))
        sum_copies[0].start()
        grad_copies = [
            pltpu.make_async_copy(grads.at[0], grads_out.at[core], sems.at[2]),
            pltpu.make_async_copy(grads.at[1], grads_out.at[1 - core], sems.at[3]),
        ]
        keep = row_mask(info[1])
        whole[0:HALO, :] = left[...]
        whole[HALO : HALO + ROWS, :] = main[...]
        whole[HALO + ROWS : WIDE, :] = right[...]
        pad[0:8, :] = jnp.zeros((8, C), F32)
        pad[PAD - 8 : PAD, :] = jnp.zeros((8, C), F32)
        if whole_out is not None:
            whole_out[...] = whole[...]

        def pull(grad, which, last):
            grads[which, 0:ROWS, :] = grad[HALO : HALO + ROWS].astype(BF16)
            pad[8 : 8 + WIDE, :] = grad
            grad_act = jnp.zeros((WIDE, C), F32)
            for tap in range(KERNEL):
                start = 10 - tap
                rows = pad[start : start + WIDE, :].astype(BF16)
                wait_filter(own, held, filter_sems, which, tap)
                grad_act = grad_act + lax.dot_general(
                    rows,
                    held[which, tap],
                    (((1,), (1,)), ((), ())),
                    preferred_element_type=F32,
                )
            sum_copies[which].wait()
            gain = gains[which : which + 1, :]
            value, scale = normed(sums[which])
            inner = value * gain
            square = inner * inner
            tanh = jnp.tanh(GELU_A * (inner + GELU_B * (square * inner)))
            slope = 0.5 * (1.0 + tanh) + (0.5 * GELU_A) * inner * (1.0 - tanh * tanh) * (
                1.0 + (3.0 * GELU_B) * square
            )
            grad_inner = grad_act * slope
            product = (grad_inner * value)[HALO : HALO + ROWS]
            grad_gain = jnp.sum(product, axis=0, keepdims=True)
            grads[which, ROWS : ROWS + 8, :] = jnp.broadcast_to(grad_gain, (8, C)).astype(BF16)
            grad_copies[which].start()
            if last:
                return None
            grad_value = grad_inner * gain
            mean = jnp.mean(grad_value * value, axis=-1, keepdims=True)
            result = grad + scale * (grad_value - value * mean)
            return jnp.where(keep, result, 0.0).astype(BF16)

        grad = whole[...].astype(F32)
        if tick == half - 1:
            grad = grad + grad
        elif joined:
            grad = grad + skip_a[...].astype(F32)
        grad = grad.astype(BF16).astype(F32)
        value = pull(grad, 1, False)
        if middle is not None:
            middle[...] = value
        grad = value.astype(F32)
        if joined:
            grad = (grad + skip_b[...].astype(F32)).astype(BF16).astype(F32)
        value = pull(grad, 0, tick == 0)
        if tick:
            value = value.astype(F32)
            out[...] = value[HALO : HALO + ROWS].astype(BF16)
            first_rows[...] = value[HALO : 2 * HALO].astype(BF16)
            last_rows[...] = value[ROWS : HALO + ROWS].astype(BF16)
        for copy in grad_copies:
            copy.wait()


def backward(tick, info, pieces, skip_a, skip_b, sums, own, other, gains, kept):
    half = STAGES // 2
    args = list(pieces)
    if skip_a is not None:
        args.append(skip_a)
    if skip_b is not None:
        args.append(skip_b)
    wide = jax.ShapeDtypeStruct((WIDE, C), BF16)
    edge = jax.ShapeDtypeStruct((HALO, C), BF16)
    shapes = [jax.ShapeDtypeStruct(kept.shape, kept.dtype)]
    vmem_shapes = [jax.ShapeDtypeStruct((ROWS, C), BF16), edge, edge] if tick else []
    if tick >= half:
        vmem_shapes.append(wide)
    if half <= tick < STAGES - 1:
        vmem_shapes.append(wide)
    count = 1 + len(args)
    return pl.pallas_call(
        functools.partial(backward_kernel, tick),
        out_shape=shapes + vmem_shapes,
        in_specs=[SMEM_SPEC]
        + [VMEM_SPEC] * len(args)
        + [HBM_SPEC, HBM_SPEC, HBM_SPEC, VMEM_SPEC, HBM_SPEC],
        out_specs=[HBM_SPEC] + [VMEM_SPEC] * len(vmem_shapes),
        scratch_shapes=[
            pltpu.VMEM((WIDE, C), BF16),
            pltpu.VMEM((PAD, C), F32),
            pltpu.VMEM((2, WIDE, C), F32),
            pltpu.VMEM((2, ROWS + 8, C), BF16),
            pltpu.VMEM((2, KERNEL, C, C), BF16),
            pltpu.SemaphoreType.DMA((2, KERNEL)),
            pltpu.SemaphoreType.DMA((4,)),
        ],
        input_output_aliases={count + 4: 0},
        compiler_params=params(24),
        name="backward_stage",
    )(info, *args, sums, own, other, gains, kept)


def product_kernel(rows_t, *refs):
    pieces, outs, total = refs[:SPAN], refs[SPAN : 2 * SPAN], refs[-1]
    height = ROWS + 8
    gain = jnp.zeros((8, C), F32)
    for index, piece in enumerate(pieces):
        for micro in range(2):
            column = (2 * index + micro) * ROWS
            start = micro * height
            term = jnp.dot(
                rows_t[:, column : column + ROWS],
                piece[start : start + ROWS, :],
                preferred_element_type=F32,
            )
            total[...] = term if column == 0 else total[...] + term
            gain = gain + piece[start + ROWS : start + height, :].astype(F32)
    gain = gain.astype(BF16)
    height = total.shape[0] // SPAN
    for index, out in enumerate(outs):
        out[0:height, :] = total[index * height : (index + 1) * height, :].astype(BF16)
        out[height : height + 8, :] = gain


def product(rows_t, pieces):
    height = rows_t.shape[0] // SPAN + 8
    return pl.pallas_call(
        product_kernel,
        out_shape=[jax.ShapeDtypeStruct((height, C), BF16)] * SPAN,
        in_specs=[VMEM_SPEC] * (1 + SPAN),
        out_specs=[VMEM_SPEC] * SPAN,
        scratch_shapes=[pltpu.VMEM((rows_t.shape[0], C), F32)],
        compiler_params=params(24),
        name="kernel_grad",
    )(rows_t, *pieces)


def shards(base_ids, stem_weight, conv_weight, block_gain, cotangent):
    section = lax.axis_index("section")
    column = lax.axis_index("seq")
    stage, core = section // 2, section % 2
    x, z = column // SPAN, column % SPAN
    late = stage >= STAGES // 2
    block = x * SPAN + jnp.where(late, SPAN - 1 - z, z)
    info = jnp.stack([stage, block, core]).astype(jnp.int32)
    half = STAGES // 2
    last = STAGES - 1

    other_filters = swapped(conv_weight)
    other_gain = swapped(block_gain)
    gains = jnp.where(
        core == 0,
        jnp.concatenate([block_gain, other_gain], 0),
        jnp.concatenate([other_gain, block_gain], 0),
    )

    reach = HALO + STEM_K // 2
    ids = base_ids + 1
    ids = jnp.concatenate(
        [beside(ids[:, -reach:], 1), ids, beside(ids[:, :reach], -1)], 1
    )
    ids = lax.dynamic_index_in_dim(ids, core, 0, keepdims=False)
    letters = jnp.arange(1, BASES + 1, dtype=jnp.int32)
    onehot = jnp.concatenate(
        [ids[offset : offset + WIDE, None] == letters for offset in range(STEM_K)], axis=1
    ).astype(BF16)
    stem = jnp.dot(
        onehot, stem_weight.reshape(STEM_K * BASES, C), preferred_element_type=F32
    ).astype(BF16)

    pieces = (stem[HALO : HALO + ROWS], stem[:HALO], stem[HALO + ROWS :])
    skip_whole, skip_middle, sums = {}, {}, []
    waiting = []
    kept = jnp.zeros((2, WIDE, C), BF16)
    for tick in range(STAGES):
        results = forward(
            tick,
            info,
            pieces,
            skip_whole.get(tick),
            skip_middle.get(tick),
            conv_weight,
            other_filters,
            gains,
            kept,
        )
        kept = results[1]
        sums.append(results[0])
        if tick < last:
            pieces = hop(results[2:5], 1)
            for store, target, array, source in waiting:
                store[target] = moved(after(array, results[2]), source, target)
            waiting = []
        if tick < half:
            entry = (skip_middle, last - tick, results[5], tick)
            if tick == half - 1:
                skip_middle[last - tick] = moved(results[5], tick, last - tick)
            else:
                waiting.append(entry)
            if tick:
                waiting.append((skip_whole, STAGES - tick, results[6], tick))

    both = jnp.stack([kept[0], swapped(kept[1])])
    width = C // SPAN
    split = both.reshape(2, WIDE, SPAN, width).transpose(2, 0, 1, 3)

    def slice_for(distance):
        return lax.dynamic_index_in_dim(split, (x + distance) % SPAN, 0, keepdims=False)

    gathered = jnp.stack(
        [slice_for(0)] + [turned_x(slice_for(d), d) for d in range(1, SPAN)]
    )
    taps = jnp.stack(
        [gathered[:, :, HALO - 2 + k : HALO - 2 + k + ROWS] for k in range(KERNEL)]
    )
    share = width // SPAN
    rows_t = taps.reshape(KERNEL, SPAN * 2 * ROWS, SPAN, share).transpose(2, 0, 3, 1)
    rows_t = jnp.concatenate(
        [
            lax.dynamic_index_in_dim(rows_t, (z + d) % SPAN, 0, keepdims=False)
            for d in range(SPAN)
        ],
        0,
    ).reshape(SPAN * KERNEL * share, SPAN * 2 * ROWS)

    cot = lax.dynamic_index_in_dim(cotangent, core, 0, keepdims=False)
    cot = jnp.concatenate(
        [beside(cot[ROWS - HALO :], 1), cot, beside(cot[:HALO], -1)], 0
    )
    cot = lax.ppermute(
        cot,
        AXES,
        [
            ((2 * last + c) * BLOCKS + b, place(last, c, b))
            for c in range(2)
            for b in range(BLOCKS)
        ],
    )
    pieces = (cot[HALO : HALO + ROWS], cot[:HALO], cot[HALO + ROWS :])
    skip_whole, skip_middle, waiting = {}, {}, []
    kept = jnp.zeros((2, ROWS + 8, C), BF16)
    for tick in reversed(range(STAGES)):
        results = backward(
            tick,
            info,
            pieces,
            skip_whole.get(tick),
            skip_middle.get(tick),
            sums[tick],
            conv_weight,
            other_filters,
            gains,
            kept,
        )
        kept = results[0]
        if tick:
            pieces = hop(results[1:4], -1)
            for store, target, array, source in waiting:
                store[target] = moved(after(array, results[1]), source, target)
            waiting = []
        if tick >= half:
            if tick == half:
                skip_middle[last - tick] = moved(results[4], tick, last - tick)
            else:
                waiting.append((skip_middle, last - tick, results[4], tick))
            if tick < last:
                waiting.append((skip_whole, last - 1 - tick, results[5], tick))

    both = jnp.concatenate([kept[0], swapped(kept[1])], 0)
    parts = product(rows_t, [both] + [turned_x(both, d) for d in range(1, SPAN)])
    total = parts[0].astype(F32)
    for d in range(1, SPAN):
        total = total + turned_z(parts[d], d).astype(F32)
    height = KERNEL * share
    kernel_grad = total[:height].astype(BF16).reshape(1, KERNEL, share, C)
    gain_grad = lax.dynamic_slice_in_dim(total[height], column * share, share)
    return kernel_grad, gain_grad[None]


def solution(mesh):
    placed = (
        P(None, "seq"),
        P(),
        P("section", None, None, None),
        P("section", None),
        P(None, "seq", None),
    )
    return jax.shard_map(
        shards,
        mesh=mesh,
        in_specs=placed,
        out_specs=(P("section", None, "seq", None), P("section", "seq")),
        check_vma=False,
    )
```

```python
import functools

import jax
import jax.numpy as jnp
from jax import lax
from jax.experimental import pallas as pl
from jax.experimental.pallas import tpu as pltpu
from jax.sharding import PartitionSpec as P

KERNEL = 5
STEM_K = 15
BASES = 4
C = 768
ROWS = 128
HALO = 8
WIDE = ROWS + 2 * HALO
PAD = WIDE + 16
STAGES = 8
BLOCKS = 16
SPAN = 4
TOKENS = BLOCKS * ROWS
AXES = ("section", "seq")
BF16 = jnp.bfloat16
F32 = jnp.float32
GELU_A = 0.7978845608028654
GELU_B = 0.044715
VMEM_SPEC = pl.BlockSpec(memory_space=pltpu.VMEM)
SMEM_SPEC = pl.BlockSpec(memory_space=pltpu.SMEM)
HBM_SPEC = pl.BlockSpec(memory_space=pltpu.HBM)


def place(stage, core, block):
    x, z = block // SPAN, block % SPAN
    column = x * SPAN + (SPAN - 1 - z if stage >= STAGES // 2 else z)
    return (2 * stage + core) * BLOCKS + column


def moved(array, source, target, shift=0):
    route = [
        (place(source, core, block), place(target, core, block + shift))
        for core in range(2)
        for block in range(BLOCKS)
        if 0 <= block + shift < BLOCKS
    ]
    return lax.ppermute(array, AXES, route)


def swapped(array):
    return lax.ppermute(array, "section", [(i, i ^ 1) for i in range(2 * STAGES)])


def beside(array, shift):
    route = [(b, b + shift) for b in range(BLOCKS) if 0 <= b + shift < BLOCKS]
    return lax.ppermute(array, "seq", route)


def turned_x(array, distance):
    route = [
        (x * SPAN + z, (x + distance) % SPAN * SPAN + z) for x in range(SPAN) for z in range(SPAN)
    ]
    return lax.ppermute(array, "seq", route)


def turned_z(array, distance):
    route = [
        (x * SPAN + z, x * SPAN + (z + distance) % SPAN) for x in range(SPAN) for z in range(SPAN)
    ]
    return lax.ppermute(array, "seq", route)


def parity(array, tick, step, shift=0):
    route = [
        (place(stage, core, block), place(stage + step, core, block + shift))
        for stage in range(tick % 2, STAGES, 2)
        for core in range(2)
        for block in range(BLOCKS)
        if 0 <= stage + step < STAGES and 0 <= block + shift < BLOCKS
    ]
    return lax.ppermute(array, AXES, route)


def hop(pieces, tick, step):
    main, first, last = pieces
    return (
        parity(main, tick, step),
        parity(last, tick, step, 1),
        parity(first, tick, step, -1),
    )


def after(array, event):
    return lax.optimization_barrier((array, event))[0]


def params(mib):
    return pltpu.CompilerParams(vmem_limit_bytes=mib << 20)


def row_mask(block):
    row = lax.broadcasted_iota(jnp.int32, (WIDE, 1), 0) + (block * ROWS - HALO)
    return (row >= 0) & (row < TOKENS)


def normed(total):
    scale = lax.rsqrt(jnp.mean(total * total, axis=-1, keepdims=True) + 1e-06)
    return total * scale, scale


def send_pair(core, source, first, second, sems):
    def start(one, two):
        pltpu.make_async_copy(source.at[0], one, sems.at[0]).start()
        pltpu.make_async_copy(source.at[1], two, sems.at[1]).start()

    pl.when(core == 0)(lambda: start(first, second))
    pl.when(core != 0)(lambda: start(second, first))


def wait_pair(source, first, sems):
    for index in range(2):
        pltpu.make_async_copy(source.at[index], first, sems.at[index]).wait()


def hbm(shape, dtype):
    return pltpu.HBM(shape, dtype)


def forward_kernel(tick, info, *refs):
    half = STAGES // 2
    skips = tick >= half
    last = tick == STAGES - 1
    refs = list(refs)
    main, left, right = refs[:3]
    refs = refs[3:]
    own_skip = refs.pop(0) if tick > half else None
    skip_b = refs.pop(0) if skips else None
    filters, gains = refs[:2]
    refs = refs[4 if skips else 6 :]
    sums_out, keep_out, give_out = refs[:3]
    refs = refs[3:]
    middle_out, whole_out = (refs.pop(0), refs.pop(0)) if not skips else (None, None)
    out, first_rows, last_rows = (refs.pop(0), refs.pop(0), refs.pop(0)) if not last else (None,) * 3
    whole, middle, pad, sums, acts, sems = refs

    @pl.when(info[0] == tick)
    def _():
        core = info[2]
        keep = row_mask(info[1])
        whole[0:HALO, :] = left[...]
        whole[HALO : HALO + ROWS, :] = main[...]
        whole[HALO + ROWS : WIDE, :] = right[...]
        pad[0:8, :] = jnp.zeros((8, C), F32)
        pad[PAD - 8 : PAD, :] = jnp.zeros((8, C), F32)
        copies = []
        if not skips:
            copies = [
                pltpu.make_async_copy(whole, whole_out, sems.at[4]),
                pltpu.make_async_copy(middle, middle_out, sems.at[5]),
            ]
            copies[0].start()
        sum_copies = [
            pltpu.make_async_copy(sums.at[i], sums_out.at[i], sems.at[i]) for i in range(2)
        ]

        def activated(total, which):
            sums[which] = total
            sum_copies[which].start()
            value, _ = normed(total)
            value = jax.nn.gelu(value * gains[which : which + 1, :])
            rounded = jnp.where(keep, value, 0.0).astype(BF16)
            acts[which] = rounded
            pad[8 : 8 + WIDE, :] = rounded.astype(F32)

        def conv(total, which):
            for tap in range(KERNEL):
                start = 6 + tap
                rows = pad[start : start + WIDE, :].astype(BF16)
                total = total + jnp.dot(rows, filters[which, tap], preferred_element_type=F32)
            return total

        total = whole[...].astype(F32)
        if tick == half:
            total = total + total
        elif skips:
            total = total + own_skip[...].astype(F32)
        activated(total, 0)
        value = conv(total, 0).astype(BF16)
        if not skips:
            middle[...] = value
            copies[1].start()
        total = value.astype(F32)
        if skips:
            total = total + skip_b[...].astype(F32)
        activated(total, 1)
        send_pair(core, acts, keep_out, give_out, sems.at[pl.ds(2, 2)])
        if not last:
            value = conv(total, 1)
            out[...] = value[HALO : HALO + ROWS].astype(BF16)
            first_rows[...] = value[HALO : 2 * HALO].astype(BF16)
            last_rows[...] = value[ROWS : HALO + ROWS].astype(BF16)
        for copy in sum_copies + copies:
            copy.wait()
        wait_pair(acts, keep_out, sems.at[pl.ds(2, 2)])


def forward(tick, info, pieces, skip_a, skip_b, filters, gains, kept, passed):
    last = tick == STAGES - 1
    skips = tick >= STAGES // 2
    args = list(pieces)
    if skip_a is not None:
        args.append(skip_a)
    if skip_b is not None:
        args.append(skip_b)
    edge = jax.ShapeDtypeStruct((HALO, C), BF16)
    held = list(kept) + ([] if skips else list(passed))
    shapes = [hbm((2, WIDE, C), F32)] + [hbm(a.shape, a.dtype) for a in held]
    vmem_shapes = [] if last else [jax.ShapeDtypeStruct((ROWS, C), BF16), edge, edge]
    count = 3 + len(args)
    return pl.pallas_call(
        functools.partial(forward_kernel, tick),
        out_shape=shapes + vmem_shapes,
        in_specs=[SMEM_SPEC] + [VMEM_SPEC] * (len(args) + 2) + [HBM_SPEC] * len(held),
        out_specs=[HBM_SPEC] * len(shapes) + [VMEM_SPEC] * len(vmem_shapes),
        scratch_shapes=[
            pltpu.VMEM((WIDE, C), BF16),
            pltpu.VMEM((WIDE, C), BF16),
            pltpu.VMEM((PAD, C), F32),
            pltpu.VMEM((2, WIDE, C), F32),
            pltpu.VMEM((2, WIDE, C), BF16),
            pltpu.SemaphoreType.DMA((6,)),
        ],
        input_output_aliases={count + i: 1 + i for i in range(len(held))},
        compiler_params=params(12),
        name="forward_stage",
    )(info, *args, filters, gains, *held)


def backward_kernel(tick, info, *refs):
    half = STAGES // 2
    joined = tick < half
    refs = list(refs)
    main, left, right = refs[:3]
    refs = refs[3:]
    skip_a = refs.pop(0) if tick < half - 1 else None
    skip_b = refs.pop(0) if joined else None
    filters, gains, sums_in = refs[:3]
    refs = refs[5 if joined else 7 :]
    keep_out, give_out = refs[:2]
    refs = refs[2:]
    middle_out, whole_out = (refs.pop(0), refs.pop(0)) if not joined else (None, None)
    out, first_rows, last_rows = (refs.pop(0), refs.pop(0), refs.pop(0)) if tick else (None,) * 3
    whole, middle, pad, sums, grads, sems = refs

    @pl.when(info[0] == tick)
    def _():
        core = info[2]
        sum_copies = [
            pltpu.make_async_copy(sums_in.at[i], sums.at[i], sems.at[i]) for i in range(2)
        ]
        sum_copies[1].start()
        sum_copies[0].start()
        keep = row_mask(info[1])
        whole[0:HALO, :] = left[...]
        whole[HALO : HALO + ROWS, :] = main[...]
        whole[HALO + ROWS : WIDE, :] = right[...]
        pad[0:8, :] = jnp.zeros((8, C), F32)
        pad[PAD - 8 : PAD, :] = jnp.zeros((8, C), F32)
        copies = []
        if not joined:
            copies = [
                pltpu.make_async_copy(whole, whole_out, sems.at[4]),
                pltpu.make_async_copy(middle, middle_out, sems.at[5]),
            ]
            copies[0].start()

        def pull(grad, which, last):
            grads[which, 0:ROWS, :] = grad[HALO : HALO + ROWS].astype(BF16)
            pad[8 : 8 + WIDE, :] = grad
            grad_act = jnp.zeros((WIDE, C), F32)
            for tap in range(KERNEL):
                start = 10 - tap
                rows = pad[start : start + WIDE, :].astype(BF16)
                grad_act = grad_act + lax.dot_general(
                    rows,
                    filters[which, tap],
                    (((1,), (1,)), ((), ())),
                    preferred_element_type=F32,
                )
            sum_copies[which].wait()
            gain = gains[which : which + 1, :]
            value, scale = normed(sums[which])
            inner = value * gain
            square = inner * inner
            tanh = jnp.tanh(GELU_A * (inner + GELU_B * (square * inner)))
            slope = 0.5 * (1.0 + tanh) + (0.5 * GELU_A) * inner * (1.0 - tanh * tanh) * (
                1.0 + (3.0 * GELU_B) * square
            )
            grad_inner = grad_act * slope
            product = (grad_inner * value)[HALO : HALO + ROWS]
            grad_gain = jnp.sum(product, axis=0, keepdims=True)
            grads[which, ROWS : ROWS + 8, :] = jnp.broadcast_to(grad_gain, (8, C)).astype(BF16)
            if last:
                return None
            grad_value = grad_inner * gain
            mean = jnp.mean(grad_value * value, axis=-1, keepdims=True)
            result = grad + scale * (grad_value - value * mean)
            return jnp.where(keep, result, 0.0).astype(BF16)

        grad = whole[...].astype(F32)
        if tick == half - 1:
            grad = grad + grad
        elif joined:
            grad = grad + skip_a[...].astype(F32)
        grad = grad.astype(BF16).astype(F32)
        value = pull(grad, 1, False)
        if not joined:
            middle[...] = value
            copies[1].start()
        grad = value.astype(F32)
        if joined:
            grad = (grad + skip_b[...].astype(F32)).astype(BF16).astype(F32)
        value = pull(grad, 0, tick == 0)
        send_pair(core, grads, keep_out, give_out, sems.at[pl.ds(2, 2)])
        if tick:
            value = value.astype(F32)
            out[...] = value[HALO : HALO + ROWS].astype(BF16)
            first_rows[...] = value[HALO : 2 * HALO].astype(BF16)
            last_rows[...] = value[ROWS : HALO + ROWS].astype(BF16)
        for copy in copies:
            copy.wait()
        wait_pair(grads, keep_out, sems.at[pl.ds(2, 2)])


def backward(tick, info, pieces, skip_a, skip_b, sums, filters, gains, kept, passed):
    joined = tick < STAGES // 2
    args = list(pieces)
    if skip_a is not None:
        args.append(skip_a)
    if skip_b is not None:
        args.append(skip_b)
    edge = jax.ShapeDtypeStruct((HALO, C), BF16)
    held = list(kept) + ([] if joined else list(passed))
    shapes = [hbm(a.shape, a.dtype) for a in held]
    vmem_shapes = [jax.ShapeDtypeStruct((ROWS, C), BF16), edge, edge] if tick else []
    count = 4 + len(args)
    return pl.pallas_call(
        functools.partial(backward_kernel, tick),
        out_shape=shapes + vmem_shapes,
        in_specs=[SMEM_SPEC] + [VMEM_SPEC] * (len(args) + 2) + [HBM_SPEC] * (1 + len(held)),
        out_specs=[HBM_SPEC] * len(shapes) + [VMEM_SPEC] * len(vmem_shapes),
        scratch_shapes=[
            pltpu.VMEM((WIDE, C), BF16),
            pltpu.VMEM((WIDE, C), BF16),
            pltpu.VMEM((PAD, C), F32),
            pltpu.VMEM((2, WIDE, C), F32),
            pltpu.VMEM((2, ROWS + 8, C), BF16),
            pltpu.SemaphoreType.DMA((6,)),
        ],
        input_output_aliases={count + i: i for i in range(len(held))},
        compiler_params=params(12),
        name="backward_stage",
    )(info, *args, filters, gains, sums, *held)


def pair_kernel(info, own, other, pair, sems):
    core = info[2]
    copies = [
        pltpu.make_async_copy(own.at[0], pair.at[core], sems.at[0]),
        pltpu.make_async_copy(other.at[0], pair.at[1 - core], sems.at[1]),
    ]
    for copy in copies:
        copy.start()
    for copy in copies:
        copy.wait()


def paired(info, own, other):
    return pl.pallas_call(
        pair_kernel,
        out_shape=pltpu.VMEM((2, *own.shape[1:]), own.dtype),
        in_specs=[SMEM_SPEC, HBM_SPEC, HBM_SPEC],
        out_specs=VMEM_SPEC,
        scratch_shapes=[pltpu.SemaphoreType.DMA((2,))],
        compiler_params=params(12),
        name="weight_pair",
    )(info, own, other)


def split_kernel(info, keep, got, *outs):
    width = C // SPAN
    for index, array in enumerate((keep, got)):
        for part in range(SPAN):
            piece = array[:, part * width : (part + 1) * width]
            for distance, out in enumerate(outs):

                @pl.when(lax.rem(info[3] + distance, SPAN) == part)
                def _():
                    out[index] = piece


def split(info, keep, got):
    return pl.pallas_call(
        split_kernel,
        out_shape=[jax.ShapeDtypeStruct((2, WIDE, C // SPAN), BF16)] * SPAN,
        in_specs=[SMEM_SPEC, VMEM_SPEC, VMEM_SPEC],
        out_specs=[VMEM_SPEC] * SPAN,
        compiler_params=params(8),
        name="split_rows",
    )(info, keep, got)


def turn_kernel(*refs):
    pieces, out = refs[:SPAN], refs[SPAN]
    width = C // SPAN
    for index, piece in enumerate(pieces):
        for micro in range(2):
            rows = piece[micro].astype(F32).T
            column = (2 * index + micro) * ROWS
            for tap in range(KERNEL):
                start = HALO - 2 + tap
                out[tap * width : (tap + 1) * width, column : column + ROWS] = rows[
                    :, start : start + ROWS
                ].astype(BF16)


def turned(pieces):
    width = C // SPAN
    return pl.pallas_call(
        turn_kernel,
        out_shape=jax.ShapeDtypeStruct((KERNEL * width, SPAN * 2 * ROWS), BF16),
        in_specs=[VMEM_SPEC] * SPAN,
        out_specs=VMEM_SPEC,
        compiler_params=params(12),
        name="turn_rows",
    )(*pieces)


def product_kernel(info, rows_t, *refs):
    count = 2 * SPAN
    pieces, outs, total = refs[:count], refs[count : count + SPAN], refs[-1]
    gain = jnp.zeros((8, C), F32)
    for index, piece in enumerate(pieces):
        term = jnp.dot(
            rows_t[:, index * ROWS : (index + 1) * ROWS],
            piece[0:ROWS, :],
            preferred_element_type=F32,
        )
        total[...] = term if index == 0 else total[...] + term
        gain = gain + piece[ROWS : ROWS + 8, :].astype(F32)
    gain = gain.astype(BF16)
    width = C // SPAN
    share = width // SPAN
    for distance, out in enumerate(outs):
        target = lax.rem(info[4] + distance, SPAN)
        for tap in range(KERNEL):
            start = pl.multiple_of(tap * width + target * share, 8)
            out[tap * share : (tap + 1) * share, :] = total[pl.ds(start, share), :].astype(BF16)
        out[KERNEL * share : KERNEL * share + 8, :] = gain


def product(info, rows_t, pieces):
    height = rows_t.shape[0] // SPAN + 8
    return pl.pallas_call(
        product_kernel,
        out_shape=[jax.ShapeDtypeStruct((height, C), BF16)] * SPAN,
        in_specs=[SMEM_SPEC] + [VMEM_SPEC] * (1 + 2 * SPAN),
        out_specs=[VMEM_SPEC] * SPAN,
        scratch_shapes=[pltpu.VMEM((rows_t.shape[0], C), F32)],
        compiler_params=params(24),
        name="kernel_grad",
    )(info, rows_t, *pieces)


def mirrored(array, step):
    half = STAGES // 2
    sources = range(half) if step >= 0 else range(half, STAGES)
    route = [
        (place(stage, core, block), place(target, core, block))
        for stage in sources
        for target in [STAGES - 1 - stage + (abs(step) - 1 if step > 0 else 1 - abs(step))]
        for core in range(2)
        for block in range(BLOCKS)
        if 0 <= target < STAGES and target != stage and (target < half) != (stage < half)
    ]
    return lax.ppermute(array, AXES, route)


def shards(base_ids, stem_weight, conv_weight, block_gain, cotangent):
    section = lax.axis_index("section")
    column = lax.axis_index("seq")
    stage, core = section // 2, section % 2
    x, z = column // SPAN, column % SPAN
    late = stage >= STAGES // 2
    block = x * SPAN + jnp.where(late, SPAN - 1 - z, z)
    info = jnp.stack([stage, block, core, x, z]).astype(jnp.int32)
    half = STAGES // 2
    last = STAGES - 1

    filters = paired(info, conv_weight, swapped(conv_weight))
    other_gain = swapped(block_gain)
    gains = jnp.where(
        core == 0,
        jnp.concatenate([block_gain, other_gain], 0),
        jnp.concatenate([other_gain, block_gain], 0),
    )

    reach = HALO + STEM_K // 2
    ids = base_ids + 1
    ids = jnp.concatenate(
        [beside(ids[:, -reach:], 1), ids, beside(ids[:, :reach], -1)], 1
    )
    ids = lax.dynamic_index_in_dim(ids, core, 0, keepdims=False)
    letters = jnp.arange(1, BASES + 1, dtype=jnp.int32)
    onehot = jnp.concatenate(
        [ids[offset : offset + WIDE, None] == letters for offset in range(STEM_K)], axis=1
    ).astype(BF16)
    stem = jnp.dot(
        onehot, stem_weight.reshape(STEM_K * BASES, C), preferred_element_type=F32
    ).astype(BF16)
    pieces = (stem[HALO : HALO + ROWS], stem[:HALO], stem[HALO + ROWS :])

    cot = lax.dynamic_index_in_dim(cotangent, core, 0, keepdims=False)

    def cot_moved(rows, shift):
        route = [
            ((2 * last + c) * BLOCKS + b, place(last, c, b + shift))
            for c in range(2)
            for b in range(BLOCKS)
            if 0 <= b + shift < BLOCKS
        ]
        return lax.ppermute(rows, AXES, route)

    cot_pieces = (
        cot_moved(cot, 0),
        cot_moved(cot[ROWS - HALO :], 1),
        cot_moved(cot[:HALO], -1),
    )

    wide = jnp.zeros((WIDE, C), BF16)
    skip_a = skip_b = None
    sums = []
    kept, passed = (wide, wide), (wide, wide)
    for tick in range(STAGES):
        results = forward(
            tick,
            info,
            pieces,
            skip_a if tick > half else None,
            skip_b,
            filters,
            gains,
            kept,
            passed,
        )
        sums.append(results[0])
        kept = results[1:3]
        if tick < half:
            passed = results[3:5]
        if tick < last:
            pieces = hop(results[-3:], tick, 1)
        if tick == half - 1:
            skip_b = mirrored(passed[0], 1)
            skip_a = mirrored(passed[1], 2)

    parts = split(info, kept[0], swapped(kept[1]))
    rows_t = turned([parts[0]] + [turned_x(parts[d], d) for d in range(1, SPAN)])

    pieces = cot_pieces
    skip_a = skip_b = None
    own = jnp.zeros((ROWS + 8, C), BF16)
    kept, passed = (own, own), (wide, wide)
    for tick in reversed(range(STAGES)):
        results = backward(
            tick,
            info,
            pieces,
            skip_a if tick < half - 1 else None,
            skip_b,
            sums[tick],
            filters,
            gains,
            kept,
            passed,
        )
        kept = results[:2]
        if tick >= half:
            passed = results[2:4]
        if tick:
            pieces = hop(results[-3:], tick, -1)
        if tick == half:
            skip_b = mirrored(passed[0], -1)
            skip_a = mirrored(passed[1], -2)

    keep, got = kept[0], swapped(kept[1])
    grads = [keep, got]
    for d in range(1, SPAN):
        grads += [turned_x(keep, d), turned_x(got, d)]
    parts = product(info, rows_t, grads)
    total = parts[0].astype(F32)
    for d in range(1, SPAN):
        total = total + turned_z(parts[d], d).astype(F32)
    share = C // BLOCKS
    height = KERNEL * share
    kernel_grad = total[:height].astype(BF16).reshape(1, KERNEL, share, C)
    gain_grad = lax.dynamic_slice_in_dim(total[height], column * share, share)
    return kernel_grad, gain_grad[None]


def solution(mesh):
    placed = (
        P(None, "seq"),
        P(),
        P("section", None, None, None),
        P("section", None),
        P(None, "seq", None),
    )
    return jax.shard_map(
        shards,
        mesh=mesh,
        in_specs=placed,
        out_specs=(P("section", None, "seq", None), P("section", "seq")),
        check_vma=False,
    )
```

```python
import functools

import jax
import jax.numpy as jnp
from jax import lax
from jax.experimental import pallas as pl
from jax.experimental.pallas import tpu as pltpu
from jax.sharding import PartitionSpec as P

KERNEL = 5
STEM_K = 15
BASES = 4
C = 768
ROWS = 128
HALO = 8
WIDE = ROWS + 2 * HALO
PAD = WIDE + 16
STAGES = 8
BLOCKS = 16
SPAN = 4
TOKENS = BLOCKS * ROWS
AXES = ("section", "seq")
BF16 = jnp.bfloat16
F32 = jnp.float32
GELU_A = 0.7978845608028654
GELU_B = 0.044715
VMEM_SPEC = pl.BlockSpec(memory_space=pltpu.VMEM)
SMEM_SPEC = pl.BlockSpec(memory_space=pltpu.SMEM)
HBM_SPEC = pl.BlockSpec(memory_space=pltpu.HBM)


def place(stage, core, block):
    x, z = block // SPAN, block % SPAN
    column = x * SPAN + (SPAN - 1 - z if stage >= STAGES // 2 else z)
    return (2 * stage + core) * BLOCKS + column


def swapped(array):
    return lax.ppermute(array, "section", [(i, i ^ 1) for i in range(2 * STAGES)])


def beside(array, shift):
    route = [(b, b + shift) for b in range(BLOCKS) if 0 <= b + shift < BLOCKS]
    return lax.ppermute(array, "seq", route)


def turned_x(array, distance):
    route = [
        (x * SPAN + z, (x + distance) % SPAN * SPAN + z) for x in range(SPAN) for z in range(SPAN)
    ]
    return lax.ppermute(array, "seq", route)


def turned_z(array, distance):
    route = [
        (x * SPAN + z, x * SPAN + (z + distance) % SPAN) for x in range(SPAN) for z in range(SPAN)
    ]
    return lax.ppermute(array, "seq", route)


def parity(array, tick, step, shift=0):
    route = [
        (place(stage, core, block), place(stage + step, core, block + shift))
        for stage in range(tick % 2, STAGES, 2)
        for core in range(2)
        for block in range(BLOCKS)
        if 0 <= stage + step < STAGES and 0 <= block + shift < BLOCKS
    ]
    return lax.ppermute(array, AXES, route)


def hop(pieces, tick, step):
    main, first, last = pieces
    return (
        parity(main, tick, step),
        parity(last, tick, step, 1),
        parity(first, tick, step, -1),
    )


def after(array, event):
    return lax.optimization_barrier((array, event))[0]


def params(mib):
    return pltpu.CompilerParams(vmem_limit_bytes=mib << 20)


def row_mask(block):
    row = lax.broadcasted_iota(jnp.int32, (WIDE, 1), 0) + (block * ROWS - HALO)
    return (row >= 0) & (row < TOKENS)


def normed(total):
    scale = lax.rsqrt(jnp.mean(total * total, axis=-1, keepdims=True) + 1e-06)
    return total * scale, scale


def send_pair(core, source, first, second, sems):
    def start(one, two):
        pltpu.make_async_copy(source.at[0], one, sems.at[0]).start()
        pltpu.make_async_copy(source.at[1], two, sems.at[1]).start()

    pl.when(core == 0)(lambda: start(first, second))
    pl.when(core != 0)(lambda: start(second, first))


def wait_pair(source, first, sems):
    for index in range(2):
        pltpu.make_async_copy(source.at[index], first, sems.at[index]).wait()


def hbm(shape, dtype):
    return pltpu.HBM(shape, dtype)


def forward_kernel(tick, info, *refs):
    half = STAGES // 2
    skips = tick >= half
    last = tick == STAGES - 1
    refs = list(refs)
    main, left, right = refs[:3]
    refs = refs[3:]
    own_skip = refs.pop(0) if tick > half else None
    skip_b = refs.pop(0) if skips else None
    filters, gains = refs[:2]
    refs = refs[4 if skips else 6 :]
    sums_out, keep_out, give_out = refs[:3]
    refs = refs[3:]
    middle_out, whole_out = (refs.pop(0), refs.pop(0)) if not skips else (None, None)
    out, first_rows, last_rows = (refs.pop(0), refs.pop(0), refs.pop(0)) if not last else (None,) * 3
    whole, middle, pad, sums, acts, sems = refs

    @pl.when(info[0] == tick)
    def _():
        core = info[2]
        keep = row_mask(info[1])
        whole[0:HALO, :] = left[...]
        whole[HALO : HALO + ROWS, :] = main[...]
        whole[HALO + ROWS : WIDE, :] = right[...]
        pad[0:8, :] = jnp.zeros((8, C), F32)
        pad[PAD - 8 : PAD, :] = jnp.zeros((8, C), F32)
        copies = []
        if not skips:
            copies = [
                pltpu.make_async_copy(whole, whole_out, sems.at[4]),
                pltpu.make_async_copy(middle, middle_out, sems.at[5]),
            ]
            copies[0].start()
        sum_copies = [
            pltpu.make_async_copy(sums.at[i], sums_out.at[i], sems.at[i]) for i in range(2)
        ]

        def activated(total, which):
            sums[which] = total
            sum_copies[which].start()
            value, _ = normed(total)
            value = jax.nn.gelu(value * gains[which : which + 1, :])
            rounded = jnp.where(keep, value, 0.0).astype(BF16)
            acts[which] = rounded
            pad[8 : 8 + WIDE, :] = rounded.astype(F32)

        def conv(total, which):
            for tap in range(KERNEL):
                start = 6 + tap
                rows = pad[start : start + WIDE, :].astype(BF16)
                total = total + jnp.dot(rows, filters[which, tap], preferred_element_type=F32)
            return total

        total = whole[...].astype(F32)
        if tick == half:
            total = total + total
        elif skips:
            total = total + own_skip[...].astype(F32)
        activated(total, 0)
        value = conv(total, 0).astype(BF16)
        if not skips:
            middle[...] = value
            copies[1].start()
        total = value.astype(F32)
        if skips:
            total = total + skip_b[...].astype(F32)
        activated(total, 1)
        send_pair(core, acts, keep_out, give_out, sems.at[pl.ds(2, 2)])
        if not last:
            value = conv(total, 1)
            out[...] = value[HALO : HALO + ROWS].astype(BF16)
            first_rows[...] = value[HALO : 2 * HALO].astype(BF16)
            last_rows[...] = value[ROWS : HALO + ROWS].astype(BF16)
        for copy in sum_copies + copies:
            copy.wait()
        wait_pair(acts, keep_out, sems.at[pl.ds(2, 2)])


def forward(tick, info, pieces, skip_a, skip_b, filters, gains, kept, passed):
    last = tick == STAGES - 1
    skips = tick >= STAGES // 2
    args = list(pieces)
    if skip_a is not None:
        args.append(skip_a)
    if skip_b is not None:
        args.append(skip_b)
    edge = jax.ShapeDtypeStruct((HALO, C), BF16)
    held = list(kept) + ([] if skips else list(passed))
    shapes = [hbm((2, WIDE, C), F32)] + [hbm(a.shape, a.dtype) for a in held]
    vmem_shapes = [] if last else [jax.ShapeDtypeStruct((ROWS, C), BF16), edge, edge]
    count = 3 + len(args)
    return pl.pallas_call(
        functools.partial(forward_kernel, tick),
        out_shape=shapes + vmem_shapes,
        in_specs=[SMEM_SPEC] + [VMEM_SPEC] * (len(args) + 2) + [HBM_SPEC] * len(held),
        out_specs=[HBM_SPEC] * len(shapes) + [VMEM_SPEC] * len(vmem_shapes),
        scratch_shapes=[
            pltpu.VMEM((WIDE, C), BF16),
            pltpu.VMEM((WIDE, C), BF16),
            pltpu.VMEM((PAD, C), F32),
            pltpu.VMEM((2, WIDE, C), F32),
            pltpu.VMEM((2, WIDE, C), BF16),
            pltpu.SemaphoreType.DMA((6,)),
        ],
        input_output_aliases={count + i: 1 + i for i in range(len(held))},
        compiler_params=params(12),
        name="forward_stage",
    )(info, *args, filters, gains, *held)


def backward_kernel(tick, info, *refs):
    half = STAGES // 2
    joined = tick < half
    refs = list(refs)
    main, left, right = refs[:3]
    refs = refs[3:]
    skip_a = refs.pop(0) if tick < half - 1 else None
    skip_b = refs.pop(0) if joined else None
    filters, gains, sums_in = refs[:3]
    refs = refs[5 if joined else 7 :]
    keep_out, give_out = refs[:2]
    refs = refs[2:]
    middle_out, whole_out = (refs.pop(0), refs.pop(0)) if not joined else (None, None)
    out, first_rows, last_rows = (refs.pop(0), refs.pop(0), refs.pop(0)) if tick else (None,) * 3
    whole, middle, pad, sums, grads, sems = refs

    @pl.when(info[0] == tick)
    def _():
        core = info[2]
        sum_copies = [
            pltpu.make_async_copy(sums_in.at[i], sums.at[i], sems.at[i]) for i in range(2)
        ]
        sum_copies[1].start()
        sum_copies[0].start()
        keep = row_mask(info[1])
        whole[0:HALO, :] = left[...]
        whole[HALO : HALO + ROWS, :] = main[...]
        whole[HALO + ROWS : WIDE, :] = right[...]
        pad[0:8, :] = jnp.zeros((8, C), F32)
        pad[PAD - 8 : PAD, :] = jnp.zeros((8, C), F32)
        copies = []
        if not joined:
            copies = [
                pltpu.make_async_copy(whole, whole_out, sems.at[4]),
                pltpu.make_async_copy(middle, middle_out, sems.at[5]),
            ]
            copies[0].start()

        def pull(grad, which, last):
            grads[which, 0:ROWS, :] = grad[HALO : HALO + ROWS].astype(BF16)
            pad[8 : 8 + WIDE, :] = grad
            grad_act = jnp.zeros((WIDE, C), F32)
            for tap in range(KERNEL):
                start = 10 - tap
                rows = pad[start : start + WIDE, :].astype(BF16)
                grad_act = grad_act + lax.dot_general(
                    rows,
                    filters[which, tap],
                    (((1,), (1,)), ((), ())),
                    preferred_element_type=F32,
                )
            sum_copies[which].wait()
            gain = gains[which : which + 1, :]
            value, scale = normed(sums[which])
            inner = value * gain
            square = inner * inner
            tanh = jnp.tanh(GELU_A * (inner + GELU_B * (square * inner)))
            slope = 0.5 * (1.0 + tanh) + (0.5 * GELU_A) * inner * (1.0 - tanh * tanh) * (
                1.0 + (3.0 * GELU_B) * square
            )
            grad_inner = grad_act * slope
            product = (grad_inner * value)[HALO : HALO + ROWS]
            grad_gain = jnp.sum(product, axis=0, keepdims=True)
            grads[which, ROWS : ROWS + 8, :] = jnp.broadcast_to(grad_gain, (8, C)).astype(BF16)
            if last:
                return None
            grad_value = grad_inner * gain
            mean = jnp.mean(grad_value * value, axis=-1, keepdims=True)
            result = grad + scale * (grad_value - value * mean)
            return jnp.where(keep, result, 0.0).astype(BF16)

        grad = whole[...].astype(F32)
        if tick == half - 1:
            grad = grad + grad
        elif joined:
            grad = grad + skip_a[...].astype(F32)
        grad = grad.astype(BF16).astype(F32)
        value = pull(grad, 1, False)
        if not joined:
            middle[...] = value
            copies[1].start()
        grad = value.astype(F32)
        if joined:
            grad = (grad + skip_b[...].astype(F32)).astype(BF16).astype(F32)
        value = pull(grad, 0, tick == 0)
        send_pair(core, grads, keep_out, give_out, sems.at[pl.ds(2, 2)])
        if tick:
            value = value.astype(F32)
            out[...] = value[HALO : HALO + ROWS].astype(BF16)
            first_rows[...] = value[HALO : 2 * HALO].astype(BF16)
            last_rows[...] = value[ROWS : HALO + ROWS].astype(BF16)
        for copy in copies:
            copy.wait()
        wait_pair(grads, keep_out, sems.at[pl.ds(2, 2)])


def backward(tick, info, pieces, skip_a, skip_b, sums, filters, gains, kept, passed):
    joined = tick < STAGES // 2
    args = list(pieces)
    if skip_a is not None:
        args.append(skip_a)
    if skip_b is not None:
        args.append(skip_b)
    edge = jax.ShapeDtypeStruct((HALO, C), BF16)
    held = list(kept) + ([] if joined else list(passed))
    shapes = [hbm(a.shape, a.dtype) for a in held]
    vmem_shapes = [jax.ShapeDtypeStruct((ROWS, C), BF16), edge, edge] if tick else []
    count = 4 + len(args)
    return pl.pallas_call(
        functools.partial(backward_kernel, tick),
        out_shape=shapes + vmem_shapes,
        in_specs=[SMEM_SPEC] + [VMEM_SPEC] * (len(args) + 2) + [HBM_SPEC] * (1 + len(held)),
        out_specs=[HBM_SPEC] * len(shapes) + [VMEM_SPEC] * len(vmem_shapes),
        scratch_shapes=[
            pltpu.VMEM((WIDE, C), BF16),
            pltpu.VMEM((WIDE, C), BF16),
            pltpu.VMEM((PAD, C), F32),
            pltpu.VMEM((2, WIDE, C), F32),
            pltpu.VMEM((2, ROWS + 8, C), BF16),
            pltpu.SemaphoreType.DMA((6,)),
        ],
        input_output_aliases={count + i: i for i in range(len(held))},
        compiler_params=params(12),
        name="backward_stage",
    )(info, *args, filters, gains, sums, *held)


def pair_kernel(info, own, other, pair, *refs):
    core, sems = info[2], refs[-1]
    copies = [
        pltpu.make_async_copy(own.at[0], pair.at[core], sems.at[0]),
        pltpu.make_async_copy(other.at[0], pair.at[1 - core], sems.at[1]),
    ]
    for copy in copies:
        copy.start()
    for copy in copies:
        copy.wait()


def paired(info, own, other, blanks):
    return pl.pallas_call(
        pair_kernel,
        out_shape=[pltpu.VMEM((2, *own.shape[1:]), own.dtype)]
        + [hbm(shape, BF16) for shape in blanks],
        in_specs=[SMEM_SPEC, HBM_SPEC, HBM_SPEC],
        out_specs=[VMEM_SPEC] + [HBM_SPEC] * len(blanks),
        scratch_shapes=[pltpu.SemaphoreType.DMA((2,))],
        compiler_params=params(44),
        name="weight_pair",
    )(info, own, other)


def split_kernel(info, keep, got, *outs):
    width = C // SPAN
    for index, array in enumerate((keep, got)):
        for part in range(SPAN):
            piece = array[:, part * width : (part + 1) * width]
            for distance, out in enumerate(outs):

                @pl.when(lax.rem(info[3] + distance, SPAN) == part)
                def _():
                    out[index] = piece


def split(info, keep, got):
    return pl.pallas_call(
        split_kernel,
        out_shape=[jax.ShapeDtypeStruct((2, WIDE, C // SPAN), BF16)] * SPAN,
        in_specs=[SMEM_SPEC, VMEM_SPEC, VMEM_SPEC],
        out_specs=[VMEM_SPEC] * SPAN,
        compiler_params=params(8),
        name="split_rows",
    )(info, keep, got)


def turn_kernel(*refs):
    pieces, out = refs[:SPAN], refs[SPAN]
    width = C // SPAN
    for index, piece in enumerate(pieces):
        for micro in range(2):
            rows = piece[micro].astype(F32).T
            column = (2 * index + micro) * ROWS
            for tap in range(KERNEL):
                start = HALO - 2 + tap
                out[tap * width : (tap + 1) * width, column : column + ROWS] = rows[
                    :, start : start + ROWS
                ].astype(BF16)


def turned(pieces):
    width = C // SPAN
    return pl.pallas_call(
        turn_kernel,
        out_shape=jax.ShapeDtypeStruct((KERNEL * width, SPAN * 2 * ROWS), BF16),
        in_specs=[VMEM_SPEC] * SPAN,
        out_specs=VMEM_SPEC,
        compiler_params=params(12),
        name="turn_rows",
    )(*pieces)


def product_kernel(info, rows_t, *refs):
    count = 2 * SPAN
    pieces, outs, total = refs[:count], refs[count : count + SPAN], refs[-1]
    gain = jnp.zeros((8, C), F32)
    for index, piece in enumerate(pieces):
        term = jnp.dot(
            rows_t[:, index * ROWS : (index + 1) * ROWS],
            piece[0:ROWS, :],
            preferred_element_type=F32,
        )
        total[...] = term if index == 0 else total[...] + term
        gain = gain + piece[ROWS : ROWS + 8, :].astype(F32)
    gain = gain.astype(BF16)
    width = C // SPAN
    share = width // SPAN
    for distance, out in enumerate(outs):
        target = lax.rem(info[4] + distance, SPAN)
        for tap in range(KERNEL):
            start = pl.multiple_of(tap * width + target * share, 8)
            out[tap * share : (tap + 1) * share, :] = total[pl.ds(start, share), :].astype(BF16)
        out[KERNEL * share : KERNEL * share + 8, :] = gain


def product(info, rows_t, pieces):
    height = rows_t.shape[0] // SPAN + 8
    return pl.pallas_call(
        product_kernel,
        out_shape=[jax.ShapeDtypeStruct((height, C), BF16)] * SPAN,
        in_specs=[SMEM_SPEC] + [VMEM_SPEC] * (1 + 2 * SPAN),
        out_specs=[VMEM_SPEC] * SPAN,
        scratch_shapes=[pltpu.VMEM((rows_t.shape[0], C), F32)],
        compiler_params=params(24),
        name="kernel_grad",
    )(info, rows_t, *pieces)


def mirrored(array, pairs):
    route = [
        (place(source, core, block), place(target, core, block))
        for source, target in pairs
        for core in range(2)
        for block in range(BLOCKS)
    ]
    return lax.ppermute(array, AXES, route)


def shards(base_ids, stem_weight, conv_weight, block_gain, cotangent):
    section = lax.axis_index("section")
    column = lax.axis_index("seq")
    stage, core = section // 2, section % 2
    x, z = column // SPAN, column % SPAN
    late = stage >= STAGES // 2
    block = x * SPAN + jnp.where(late, SPAN - 1 - z, z)
    info = jnp.stack([stage, block, core, x, z]).astype(jnp.int32)
    half = STAGES // 2
    last = STAGES - 1

    wide, own = (WIDE, C), (ROWS + 8, C)
    other_filters = swapped(conv_weight)
    other_gain = swapped(block_gain)
    gains = jnp.where(
        core == 0,
        jnp.concatenate([block_gain, other_gain], 0),
        jnp.concatenate([other_gain, block_gain], 0),
    )

    reach = HALO + STEM_K // 2
    ids = base_ids + 1
    ids = jnp.concatenate(
        [beside(ids[:, -reach:], 1), ids, beside(ids[:, :reach], -1)], 1
    )
    ids = lax.dynamic_index_in_dim(ids, core, 0, keepdims=False)
    letters = jnp.arange(1, BASES + 1, dtype=jnp.int32)
    onehot = jnp.concatenate(
        [ids[offset : offset + WIDE, None] == letters for offset in range(STEM_K)], axis=1
    ).astype(BF16)
    stem = jnp.dot(
        onehot, stem_weight.reshape(STEM_K * BASES, C), preferred_element_type=F32
    ).astype(BF16)
    pieces = (stem[HALO : HALO + ROWS], stem[:HALO], stem[HALO + ROWS :])

    cot = lax.dynamic_index_in_dim(cotangent, core, 0, keepdims=False)

    def cot_moved(rows, shift):
        route = [
            ((2 * last + c) * BLOCKS + b, place(last, c, b + shift))
            for c in range(2)
            for b in range(BLOCKS)
            if 0 <= b + shift < BLOCKS
        ]
        return lax.ppermute(rows, AXES, route)

    cot_pieces = (
        cot_moved(cot, 0),
        cot_moved(cot[ROWS - HALO :], 1),
        cot_moved(cot[:HALO], -1),
    )

    pieces, cot_pieces, gains = lax.optimization_barrier((pieces, cot_pieces, gains))
    info = after(info, (pieces, gains))
    filters, *blanks = paired(info, conv_weight, other_filters, [wide] * 6 + [own] * 2)
    skip_near = skip_far = skip_whole = None
    sums = []
    kept, passed = blanks[0:2], blanks[2:4]
    for tick in range(STAGES):
        results = forward(
            tick,
            info,
            pieces,
            skip_whole if tick > half else None,
            skip_near if tick == half else skip_far,
            filters,
            gains,
            kept,
            passed,
        )
        sums.append(results[0])
        kept = results[1:3]
        if tick < half:
            passed = results[3:5]
        if tick < last:
            pieces = hop(results[-3:], tick, 1)
        if tick == half - 1:
            skip_near = mirrored(passed[0], [(half - 1, half)])
            late = after(tuple(passed), pieces)
            skip_whole = mirrored(late[1], [(t, STAGES - t) for t in range(1, half)])
            skip_far = mirrored(late[0], [(t, last - t) for t in range(half - 1)])

    acts = kept
    pieces = cot_pieces
    skip_near = skip_far = skip_whole = None
    kept, passed = blanks[6:8], blanks[4:6]
    for tick in reversed(range(STAGES)):
        results = backward(
            tick,
            info,
            pieces,
            skip_whole if tick < half - 1 else None,
            skip_near if tick == half - 1 else skip_far,
            sums[tick],
            filters,
            gains,
            kept,
            passed,
        )
        kept = results[:2]
        event = results[-1]
        if tick == last:
            got = swapped(after(acts[1], event))
            info = after(info, got)
        elif tick == last - 1:
            keep, got = after((acts[0], got), event)
            parts = split(info, keep, got)
            info = after(info, parts[0])
        elif tick == last - 2:
            parts = after(tuple(parts), event)
            parts = [parts[0]] + [turned_x(parts[d], d) for d in range(1, SPAN)]
            info = after(info, parts[1:])
        elif tick == last - 3:
            rows_t = turned(after(tuple(parts), event))
            info = after(info, rows_t)
        if tick >= half:
            passed = results[2:4]
        if tick:
            pieces = hop(results[-3:], tick, -1)
        if tick == half:
            skip_near = mirrored(passed[0], [(half, half - 1)])
            late = after(tuple(passed), pieces)
            skip_whole = mirrored(late[1], [(t, last - 1 - t) for t in range(half, last)])
            skip_far = mirrored(late[0], [(t, last - t) for t in range(half + 1, STAGES)])

    keep, got = kept[0], swapped(kept[1])
    grads = [keep, got]
    for d in range(1, SPAN):
        grads += [turned_x(keep, d), turned_x(got, d)]
    parts = product(info, rows_t, grads)
    total = parts[0].astype(F32)
    for d in range(1, SPAN):
        total = total + turned_z(parts[d], d).astype(F32)
    share = C // BLOCKS
    height = KERNEL * share
    kernel_grad = total[:height].astype(BF16).reshape(1, KERNEL, share, C)
    gain_grad = lax.dynamic_slice_in_dim(total[height], column * share, share)
    return kernel_grad, gain_grad[None]


def solution(mesh):
    placed = (
        P(None, "seq"),
        P(),
        P("section", None, None, None),
        P("section", None),
        P(None, "seq", None),
    )
    return jax.shard_map(
        shards,
        mesh=mesh,
        in_specs=placed,
        out_specs=(P("section", None, "seq", None), P("section", "seq")),
        check_vma=False,
    )
```

```python
import functools

import jax
import jax.numpy as jnp
from jax import lax
from jax.experimental import pallas as pl
from jax.experimental.pallas import tpu as pltpu
from jax.sharding import PartitionSpec as P

KERNEL = 5
STEM_K = 15
BASES = 4
C = 768
ROWS = 128
HALO = 8
WIDE = ROWS + 2 * HALO
PAD = WIDE + 16
STAGES = 8
BLOCKS = 16
SPAN = 4
TOKENS = BLOCKS * ROWS
AXES = ("section", "seq")
BF16 = jnp.bfloat16
F32 = jnp.float32
GELU_A = 0.7978845608028654
GELU_B = 0.044715
VMEM_SPEC = pl.BlockSpec(memory_space=pltpu.VMEM)
SMEM_SPEC = pl.BlockSpec(memory_space=pltpu.SMEM)
HBM_SPEC = pl.BlockSpec(memory_space=pltpu.HBM)


def place(stage, core, block):
    x, z = block // SPAN, block % SPAN
    column = x * SPAN + (SPAN - 1 - z if stage >= STAGES // 2 else z)
    return (2 * stage + core) * BLOCKS + column


def swapped(array):
    return lax.ppermute(array, "section", [(i, i ^ 1) for i in range(2 * STAGES)])


def beside(array, shift):
    route = [(b, b + shift) for b in range(BLOCKS) if 0 <= b + shift < BLOCKS]
    return lax.ppermute(array, "seq", route)


def turned_x(array, distance):
    route = [
        (x * SPAN + z, (x + distance) % SPAN * SPAN + z) for x in range(SPAN) for z in range(SPAN)
    ]
    return lax.ppermute(array, "seq", route)


def turned_z(array, distance):
    route = [
        (x * SPAN + z, x * SPAN + (z + distance) % SPAN) for x in range(SPAN) for z in range(SPAN)
    ]
    return lax.ppermute(array, "seq", route)


def parity(array, tick, step, shift=0):
    route = [
        (place(stage, core, block), place(stage + step, core, block + shift))
        for stage in range(tick % 2, STAGES, 2)
        for core in range(2)
        for block in range(BLOCKS)
        if 0 <= stage + step < STAGES and 0 <= block + shift < BLOCKS
    ]
    return lax.ppermute(array, AXES, route)


def hop(pieces, tick, step):
    main, first, last = pieces
    return (
        parity(main, tick, step),
        parity(last, tick, step, 1),
        parity(first, tick, step, -1),
    )


def after(array, event):
    return lax.optimization_barrier((array, event))[0]


def params(mib):
    return pltpu.CompilerParams(vmem_limit_bytes=mib << 20)


def row_mask(block):
    row = lax.broadcasted_iota(jnp.int32, (WIDE, 1), 0) + (block * ROWS - HALO)
    return (row >= 0) & (row < TOKENS)


def joined_rows(parts):
    return jnp.concatenate([part[...].astype(F32) for part in parts], axis=0)


def normed(total):
    scale = lax.rsqrt(jnp.mean(total * total, axis=-1, keepdims=True) + 1e-06)
    return total * scale, scale


def send_pair(core, source, first, second, sems):
    def start(one, two):
        pltpu.make_async_copy(source.at[0], one, sems.at[0]).start()
        pltpu.make_async_copy(source.at[1], two, sems.at[1]).start()

    pl.when(core == 0)(lambda: start(first, second))
    pl.when(core != 0)(lambda: start(second, first))


def wait_pair(source, first, sems):
    for index in range(2):
        pltpu.make_async_copy(source.at[index], first, sems.at[index]).wait()


def hbm(shape, dtype):
    return pltpu.HBM(shape, dtype)


def forward_kernel(tick, info, *refs):
    half = STAGES // 2
    skips = tick >= half
    last = tick == STAGES - 1
    refs = list(refs)
    main, left, right = refs[:3]
    refs = refs[3:]
    own_skip = refs.pop(0) if tick > half else None
    skip_b = [refs.pop(0) for _ in range(2 if tick == half else 1)] if skips else None
    filters, gains = refs[:2]
    refs = refs[4 if skips else 6 :]
    sums_out, keep_out, give_out = refs[:3]
    refs = refs[3:]
    middle_out, whole_out = (refs.pop(0), refs.pop(0)) if not skips else (None, None)
    out, first_rows, last_rows = (refs.pop(0), refs.pop(0), refs.pop(0)) if not last else (None,) * 3
    near = [refs.pop(0), refs.pop(0)] if tick == half - 1 else None
    whole, middle, pad, sums, acts, sems = refs

    @pl.when(info[0] == tick)
    def _():
        core = info[2]
        keep = row_mask(info[1])
        whole[0:HALO, :] = left[...]
        whole[HALO : HALO + ROWS, :] = main[...]
        whole[HALO + ROWS : WIDE, :] = right[...]
        pad[0:8, :] = jnp.zeros((8, C), F32)
        pad[PAD - 8 : PAD, :] = jnp.zeros((8, C), F32)
        copies = []
        if not skips:
            copies = [pltpu.make_async_copy(whole, whole_out, sems.at[4])]
            copies[0].start()
            if near is None:
                copies.append(pltpu.make_async_copy(middle, middle_out, sems.at[5]))
        sum_copies = [
            pltpu.make_async_copy(sums.at[i], sums_out.at[i], sems.at[i]) for i in range(2)
        ]

        def activated(total, which):
            sums[which] = total
            sum_copies[which].start()
            value, _ = normed(total)
            value = jax.nn.gelu(value * gains[which : which + 1, :])
            rounded = jnp.where(keep, value, 0.0).astype(BF16)
            acts[which] = rounded
            pad[8 : 8 + WIDE, :] = rounded.astype(F32)

        def conv(total, which):
            for tap in range(KERNEL):
                start = 6 + tap
                rows = pad[start : start + WIDE, :].astype(BF16)
                total = total + jnp.dot(rows, filters[which, tap], preferred_element_type=F32)
            return total

        total = whole[...].astype(F32)
        if tick == half:
            total = total + total
        elif skips:
            total = total + own_skip[...].astype(F32)
        activated(total, 0)
        value = conv(total, 0).astype(BF16)
        if near is not None:
            near[0][...] = value[: WIDE // 2]
            near[1][...] = value[WIDE // 2 :]
        elif not skips:
            middle[...] = value
            copies[1].start()
        total = value.astype(F32)
        if skips:
            total = total + joined_rows(skip_b)
        activated(total, 1)
        send_pair(core, acts, keep_out, give_out, sems.at[pl.ds(2, 2)])
        if not last:
            value = conv(total, 1)
            out[...] = value[HALO : HALO + ROWS].astype(BF16)
            first_rows[...] = value[HALO : 2 * HALO].astype(BF16)
            last_rows[...] = value[ROWS : HALO + ROWS].astype(BF16)
        for copy in sum_copies + copies:
            copy.wait()
        wait_pair(acts, keep_out, sems.at[pl.ds(2, 2)])


def forward(tick, info, pieces, skip_a, skip_b, filters, gains, kept, passed):
    last = tick == STAGES - 1
    skips = tick >= STAGES // 2
    args = list(pieces)
    if skip_a is not None:
        args.append(skip_a)
    if skip_b is not None:
        args += skip_b
    edge = jax.ShapeDtypeStruct((HALO, C), BF16)
    held = list(kept) + ([] if skips else list(passed))
    shapes = [hbm((2, WIDE, C), F32)] + [hbm(a.shape, a.dtype) for a in held]
    vmem_shapes = [] if last else [jax.ShapeDtypeStruct((ROWS, C), BF16), edge, edge]
    if tick == STAGES // 2 - 1:
        vmem_shapes += [jax.ShapeDtypeStruct((WIDE // 2, C), BF16)] * 2
    count = 3 + len(args)
    return pl.pallas_call(
        functools.partial(forward_kernel, tick),
        out_shape=shapes + vmem_shapes,
        in_specs=[SMEM_SPEC] + [VMEM_SPEC] * (len(args) + 2) + [HBM_SPEC] * len(held),
        out_specs=[HBM_SPEC] * len(shapes) + [VMEM_SPEC] * len(vmem_shapes),
        scratch_shapes=[
            pltpu.VMEM((WIDE, C), BF16),
            pltpu.VMEM((WIDE, C), BF16),
            pltpu.VMEM((PAD, C), F32),
            pltpu.VMEM((2, WIDE, C), F32),
            pltpu.VMEM((2, WIDE, C), BF16),
            pltpu.SemaphoreType.DMA((6,)),
        ],
        input_output_aliases={count + i: 1 + i for i in range(len(held))},
        compiler_params=params(12),
        name="forward_stage",
    )(info, *args, filters, gains, *held)


def backward_kernel(tick, info, *refs):
    half = STAGES // 2
    joined = tick < half
    refs = list(refs)
    main, left, right = refs[:3]
    refs = refs[3:]
    skip_a = refs.pop(0) if tick < half - 1 else None
    skip_b = [refs.pop(0) for _ in range(2 if tick == half - 1 else 1)] if joined else None
    filters, gains, sums_in = refs[:3]
    refs = refs[5 if joined else 7 :]
    keep_out, give_out = refs[:2]
    refs = refs[2:]
    middle_out, whole_out = (refs.pop(0), refs.pop(0)) if not joined else (None, None)
    out, first_rows, last_rows = (refs.pop(0), refs.pop(0), refs.pop(0)) if tick else (None,) * 3
    near = [refs.pop(0), refs.pop(0)] if tick == half else None
    whole, middle, pad, sums, grads, sems = refs

    @pl.when(info[0] == tick)
    def _():
        core = info[2]
        sum_copies = [
            pltpu.make_async_copy(sums_in.at[i], sums.at[i], sems.at[i]) for i in range(2)
        ]
        sum_copies[1].start()
        sum_copies[0].start()
        keep = row_mask(info[1])
        whole[0:HALO, :] = left[...]
        whole[HALO : HALO + ROWS, :] = main[...]
        whole[HALO + ROWS : WIDE, :] = right[...]
        pad[0:8, :] = jnp.zeros((8, C), F32)
        pad[PAD - 8 : PAD, :] = jnp.zeros((8, C), F32)
        copies = []
        if not joined:
            copies = [pltpu.make_async_copy(whole, whole_out, sems.at[4])]
            copies[0].start()
            if near is None:
                copies.append(pltpu.make_async_copy(middle, middle_out, sems.at[5]))

        def pull(grad, which, last):
            grads[which, 0:ROWS, :] = grad[HALO : HALO + ROWS].astype(BF16)
            pad[8 : 8 + WIDE, :] = grad
            grad_act = jnp.zeros((WIDE, C), F32)
            for tap in range(KERNEL):
                start = 10 - tap
                rows = pad[start : start + WIDE, :].astype(BF16)
                grad_act = grad_act + jnp.dot(
                    rows, filters[which, tap], preferred_element_type=F32
                )
            sum_copies[which].wait()
            gain = gains[which : which + 1, :]
            value, scale = normed(sums[which])
            inner = value * gain
            square = inner * inner
            tanh = jnp.tanh(GELU_A * (inner + GELU_B * (square * inner)))
            slope = 0.5 * (1.0 + tanh) + (0.5 * GELU_A) * inner * (1.0 - tanh * tanh) * (
                1.0 + (3.0 * GELU_B) * square
            )
            grad_inner = grad_act * slope
            product = (grad_inner * value)[HALO : HALO + ROWS]
            grad_gain = jnp.sum(product, axis=0, keepdims=True)
            grads[which, ROWS : ROWS + 8, :] = jnp.broadcast_to(grad_gain, (8, C)).astype(BF16)
            if last:
                return None
            grad_value = grad_inner * gain
            mean = jnp.mean(grad_value * value, axis=-1, keepdims=True)
            result = grad + scale * (grad_value - value * mean)
            return jnp.where(keep, result, 0.0).astype(BF16)

        grad = whole[...].astype(F32)
        if tick == half - 1:
            grad = grad + grad
        elif joined:
            grad = grad + skip_a[...].astype(F32)
        grad = grad.astype(BF16).astype(F32)
        value = pull(grad, 1, False)
        if near is not None:
            near[0][...] = value[: WIDE // 2]
            near[1][...] = value[WIDE // 2 :]
        elif not joined:
            middle[...] = value
            copies[1].start()
        grad = value.astype(F32)
        if joined:
            grad = (grad + joined_rows(skip_b)).astype(BF16).astype(F32)
        value = pull(grad, 0, tick == 0)
        send_pair(core, grads, keep_out, give_out, sems.at[pl.ds(2, 2)])
        if tick:
            value = value.astype(F32)
            out[...] = value[HALO : HALO + ROWS].astype(BF16)
            first_rows[...] = value[HALO : 2 * HALO].astype(BF16)
            last_rows[...] = value[ROWS : HALO + ROWS].astype(BF16)
        for copy in copies:
            copy.wait()
        wait_pair(grads, keep_out, sems.at[pl.ds(2, 2)])


def backward(tick, info, pieces, skip_a, skip_b, sums, filters, gains, kept, passed):
    joined = tick < STAGES // 2
    args = list(pieces)
    if skip_a is not None:
        args.append(skip_a)
    if skip_b is not None:
        args += skip_b
    edge = jax.ShapeDtypeStruct((HALO, C), BF16)
    held = list(kept) + ([] if joined else list(passed))
    shapes = [hbm(a.shape, a.dtype) for a in held]
    vmem_shapes = [jax.ShapeDtypeStruct((ROWS, C), BF16), edge, edge] if tick else []
    if tick == STAGES // 2:
        vmem_shapes += [jax.ShapeDtypeStruct((WIDE // 2, C), BF16)] * 2
    count = 4 + len(args)
    return pl.pallas_call(
        functools.partial(backward_kernel, tick),
        out_shape=shapes + vmem_shapes,
        in_specs=[SMEM_SPEC] + [VMEM_SPEC] * (len(args) + 2) + [HBM_SPEC] * (1 + len(held)),
        out_specs=[HBM_SPEC] * len(shapes) + [VMEM_SPEC] * len(vmem_shapes),
        scratch_shapes=[
            pltpu.VMEM((WIDE, C), BF16),
            pltpu.VMEM((WIDE, C), BF16),
            pltpu.VMEM((PAD, C), F32),
            pltpu.VMEM((2, WIDE, C), F32),
            pltpu.VMEM((2, ROWS + 8, C), BF16),
            pltpu.SemaphoreType.DMA((6,)),
        ],
        input_output_aliases={count + i: i for i in range(len(held))},
        compiler_params=params(12),
        name="backward_stage",
    )(info, *args, filters, gains, sums, *held)


def pair_kernel(info, own, other, pair, *refs):
    core, sems = info[2], refs[-1]
    copies = [
        pltpu.make_async_copy(own.at[0], pair.at[core], sems.at[0]),
        pltpu.make_async_copy(other.at[0], pair.at[1 - core], sems.at[1]),
    ]
    for copy in copies:
        copy.start()
    for copy in copies:
        copy.wait()


def transpose_kernel(own, out, source, result, sems_in, sems_out):
    def load(tap, slot):
        return pltpu.make_async_copy(own.at[0, tap], source.at[slot], sems_in.at[slot])

    def save(tap, slot):
        return pltpu.make_async_copy(result.at[slot], out.at[0, tap], sems_out.at[slot])

    load(0, 0).start()
    for tap in range(KERNEL):
        slot = tap % 2
        if tap + 1 < KERNEL:
            load(tap + 1, 1 - slot).start()
        load(tap, slot).wait()
        if tap >= 2:
            save(tap - 2, slot).wait()

        def part(index, _):
            rows = pl.ds(pl.multiple_of(index * 256, 256), 256)
            row = lax.broadcasted_iota(jnp.int32, (256, C), 0) + index * 256
            eye = (row == lax.broadcasted_iota(jnp.int32, (256, C), 1)).astype(BF16)
            result[slot, rows, :] = lax.dot_general(
                eye, source[slot], (((1,), (1,)), ((), ())), preferred_element_type=F32
            ).astype(BF16)
            return 0

        lax.fori_loop(0, C // 256, part, 0)
        save(tap, slot).start()
    for tap in range(KERNEL - 2, KERNEL):
        save(tap, tap % 2).wait()


def transposed(own):
    return pl.pallas_call(
        transpose_kernel,
        out_shape=hbm(own.shape, own.dtype),
        in_specs=[HBM_SPEC],
        out_specs=HBM_SPEC,
        scratch_shapes=[
            pltpu.VMEM((2, C, C), BF16),
            pltpu.VMEM((2, C, C), BF16),
            pltpu.SemaphoreType.DMA((2,)),
            pltpu.SemaphoreType.DMA((2,)),
        ],
        compiler_params=params(12),
        name="turn_filters",
    )(own)


def paired(info, own, other, blanks, mib):
    return pl.pallas_call(
        pair_kernel,
        out_shape=[pltpu.VMEM((2, *own.shape[1:]), own.dtype)]
        + [hbm(shape, BF16) for shape in blanks],
        in_specs=[SMEM_SPEC, HBM_SPEC, HBM_SPEC],
        out_specs=[VMEM_SPEC] + [HBM_SPEC] * len(blanks),
        scratch_shapes=[pltpu.SemaphoreType.DMA((2,))],
        compiler_params=params(mib),
        name="weight_pair",
    )(info, own, other)


def split_kernel(info, keep, got, *outs):
    width = C // SPAN
    for index, array in enumerate((keep, got)):
        for part in range(SPAN):
            piece = array[:, part * width : (part + 1) * width]
            for distance, out in enumerate(outs):

                @pl.when(lax.rem(info[3] + distance, SPAN) == part)
                def _():
                    out[index] = piece


def split(info, keep, got):
    return pl.pallas_call(
        split_kernel,
        out_shape=[jax.ShapeDtypeStruct((2, WIDE, C // SPAN), BF16)] * SPAN,
        in_specs=[SMEM_SPEC, VMEM_SPEC, VMEM_SPEC],
        out_specs=[VMEM_SPEC] * SPAN,
        compiler_params=params(8),
        name="split_rows",
    )(info, keep, got)


def turn_kernel(*refs):
    pieces, out = refs[:SPAN], refs[SPAN]
    width = C // SPAN
    for index, piece in enumerate(pieces):
        for micro in range(2):
            rows = piece[micro].astype(F32).T
            column = (2 * index + micro) * ROWS
            for tap in range(KERNEL):
                start = HALO - 2 + tap
                out[tap * width : (tap + 1) * width, column : column + ROWS] = rows[
                    :, start : start + ROWS
                ].astype(BF16)


def turned(pieces):
    width = C // SPAN
    return pl.pallas_call(
        turn_kernel,
        out_shape=jax.ShapeDtypeStruct((KERNEL * width, SPAN * 2 * ROWS), BF16),
        in_specs=[VMEM_SPEC] * SPAN,
        out_specs=VMEM_SPEC,
        compiler_params=params(12),
        name="turn_rows",
    )(*pieces)


def product_kernel(info, rows_t, *refs):
    count = 2 * SPAN
    pieces, outs, total = refs[:count], refs[count : count + SPAN], refs[-1]
    gain = jnp.zeros((8, C), F32)
    for index, piece in enumerate(pieces):
        term = jnp.dot(
            rows_t[:, index * ROWS : (index + 1) * ROWS],
            piece[0:ROWS, :],
            preferred_element_type=F32,
        )
        total[...] = term if index == 0 else total[...] + term
        gain = gain + piece[ROWS : ROWS + 8, :].astype(F32)
    gain = gain.astype(BF16)
    width = C // SPAN
    share = width // SPAN
    for distance, out in enumerate(outs):
        target = lax.rem(info[4] + distance, SPAN)
        for tap in range(KERNEL):
            start = pl.multiple_of(tap * width + target * share, 8)
            out[tap * share : (tap + 1) * share, :] = total[pl.ds(start, share), :].astype(BF16)
        out[KERNEL * share : KERNEL * share + 8, :] = gain


def product(info, rows_t, pieces):
    height = rows_t.shape[0] // SPAN + 8
    return pl.pallas_call(
        product_kernel,
        out_shape=[jax.ShapeDtypeStruct((height, C), BF16)] * SPAN,
        in_specs=[SMEM_SPEC] + [VMEM_SPEC] * (1 + 2 * SPAN),
        out_specs=[VMEM_SPEC] * SPAN,
        scratch_shapes=[pltpu.VMEM((rows_t.shape[0], C), F32)],
        compiler_params=params(24),
        name="kernel_grad",
    )(info, rows_t, *pieces)


def mirrored(array, pairs):
    route = [
        (place(source, core, block), place(target, core, block))
        for source, target in pairs
        for core in range(2)
        for block in range(BLOCKS)
    ]
    return lax.ppermute(array, AXES, route)


def nearest(halves):
    half, last = STAGES // 2, STAGES - 1
    outer = mirrored(halves[1], [(half - 1, 0), (half, last)])
    return [
        mirrored(halves[0], [(half - 1, half), (half, half - 1)]),
        mirrored(outer, [(0, half), (last, half - 1)]),
    ]


def shards(base_ids, stem_weight, conv_weight, block_gain, cotangent):
    section = lax.axis_index("section")
    column = lax.axis_index("seq")
    stage, core = section // 2, section % 2
    x, z = column // SPAN, column % SPAN
    late = stage >= STAGES // 2
    block = x * SPAN + jnp.where(late, SPAN - 1 - z, z)
    info = jnp.stack([stage, block, core, x, z]).astype(jnp.int32)
    half = STAGES // 2
    last = STAGES - 1

    wide, own = (WIDE, C), (ROWS + 8, C)
    other_filters = swapped(conv_weight)
    other_gain = swapped(block_gain)
    gains = jnp.where(
        core == 0,
        jnp.concatenate([block_gain, other_gain], 0),
        jnp.concatenate([other_gain, block_gain], 0),
    )

    reach = HALO + STEM_K // 2
    ids = base_ids + 1
    ids = jnp.concatenate(
        [beside(ids[:, -reach:], 1), ids, beside(ids[:, :reach], -1)], 1
    )
    ids = lax.dynamic_index_in_dim(ids, core, 0, keepdims=False)
    letters = jnp.arange(1, BASES + 1, dtype=jnp.int32)
    onehot = jnp.concatenate(
        [ids[offset : offset + WIDE, None] == letters for offset in range(STEM_K)], axis=1
    ).astype(BF16)
    stem = jnp.dot(
        onehot, stem_weight.reshape(STEM_K * BASES, C), preferred_element_type=F32
    ).astype(BF16)
    pieces = (stem[HALO : HALO + ROWS], stem[:HALO], stem[HALO + ROWS :])

    cot = lax.dynamic_index_in_dim(cotangent, core, 0, keepdims=False)

    def cot_moved(rows, shift):
        route = [
            ((2 * last + c) * BLOCKS + b, place(last, c, b + shift))
            for c in range(2)
            for b in range(BLOCKS)
            if 0 <= b + shift < BLOCKS
        ]
        return lax.ppermute(rows, AXES, route)

    cot_pieces = (
        cot_moved(cot, 0),
        cot_moved(cot[ROWS - HALO :], 1),
        cot_moved(cot[:HALO], -1),
    )

    pieces, cot_pieces, gains = lax.optimization_barrier((pieces, cot_pieces, gains))
    info = after(info, (pieces, gains))
    filters, *blanks = paired(info, conv_weight, other_filters, [wide] * 6 + [own] * 2, 44)
    skip_near = skip_far = skip_whole = None
    sums = []
    kept, passed = blanks[0:2], blanks[2:4]
    for tick in range(STAGES):
        results = forward(
            tick,
            info,
            pieces,
            skip_whole if tick > half else None,
            skip_near if tick == half else skip_far,
            filters,
            gains,
            kept,
            passed,
        )
        if tick == 0:
            turned_own = transposed(after(conv_weight, results[-1]))
            info = after(info, turned_own)
        elif tick == 1:
            turned_other = swapped(after(turned_own, results[-1]))
        elif tick == 2:
            turned_pair = after((turned_own, turned_other), results[-1])
            (back_filters,) = paired(info, *turned_pair, [], 12)
            info = after(info, back_filters)
        sums.append(results[0])
        kept = results[1:3]
        if tick < half:
            passed = results[3:5]
        if tick == half - 1:
            skip_near = nearest(results[-2:])
            pieces = hop(results[-5:-2], tick, 1)
            late = after(tuple(passed), pieces)
            skip_whole = mirrored(late[1], [(t, STAGES - t) for t in range(1, half)])
            skip_far = [mirrored(late[0], [(t, last - t) for t in range(half - 1)])]
        elif tick < last:
            pieces = hop(results[-3:], tick, 1)

    acts = kept
    pieces = cot_pieces
    skip_near = skip_far = skip_whole = None
    kept, passed = blanks[6:8], blanks[4:6]
    for tick in reversed(range(STAGES)):
        results = backward(
            tick,
            info,
            pieces,
            skip_whole if tick < half - 1 else None,
            skip_near if tick == half - 1 else skip_far,
            sums[tick],
            back_filters,
            gains,
            kept,
            passed,
        )
        kept = results[:2]
        event = results[-1]
        if tick == last:
            got = swapped(after(acts[1], event))
            info = after(info, got)
        elif tick == last - 1:
            keep, got = after((acts[0], got), event)
            parts = split(info, keep, got)
            info = after(info, parts[0])
        elif tick == last - 2:
            parts = after(tuple(parts), event)
            parts = [parts[0]] + [turned_x(parts[d], d) for d in range(1, SPAN)]
            info = after(info, parts[1:])
        elif tick == last - 3:
            rows_t = turned(after(tuple(parts), event))
            info = after(info, rows_t)
        if tick >= half:
            passed = results[2:4]
        if tick == half:
            skip_near = nearest(results[-2:])
            pieces = hop(results[-5:-2], tick, -1)
            late = after(tuple(passed), pieces)
            skip_whole = mirrored(late[1], [(t, last - 1 - t) for t in range(half, last)])
            skip_far = [mirrored(late[0], [(t, last - t) for t in range(half + 1, STAGES)])]
        elif tick:
            pieces = hop(results[-3:], tick, -1)

    keep, got = kept[0], swapped(kept[1])
    grads = [keep, got]
    for d in range(1, SPAN):
        grads += [turned_x(keep, d), turned_x(got, d)]
    parts = product(info, rows_t, grads)
    total = parts[0].astype(F32)
    for d in range(1, SPAN):
        total = total + turned_z(parts[d], d).astype(F32)
    share = C // BLOCKS
    height = KERNEL * share
    kernel_grad = total[:height].astype(BF16).reshape(1, KERNEL, share, C)
    gain_grad = lax.dynamic_slice_in_dim(total[height], column * share, share)
    return kernel_grad, gain_grad[None]


def solution(mesh):
    placed = (
        P(None, "seq"),
        P(),
        P("section", None, None, None),
        P("section", None),
        P(None, "seq", None),
    )
    return jax.shard_map(
        shards,
        mesh=mesh,
        in_specs=placed,
        out_specs=(P("section", None, "seq", None), P("section", "seq")),
        check_vma=False,
    )
```

```python
import functools

import jax
import jax.numpy as jnp
from jax import lax
from jax.experimental import pallas as pl
from jax.experimental.pallas import tpu as pltpu
from jax.sharding import PartitionSpec as P

KERNEL = 5
STEM_K = 15
BASES = 4
C = 768
ROWS = 128
HALO = 8
WIDE = ROWS + 2 * HALO
PAD = WIDE + 16
STAGES = 8
BLOCKS = 16
SPAN = 4
TOKENS = BLOCKS * ROWS
AXES = ("section", "seq")
BF16 = jnp.bfloat16
F32 = jnp.float32
GELU_A = 0.7978845608028654
GELU_B = 0.044715
VMEM_SPEC = pl.BlockSpec(memory_space=pltpu.VMEM)
SMEM_SPEC = pl.BlockSpec(memory_space=pltpu.SMEM)
HBM_SPEC = pl.BlockSpec(memory_space=pltpu.HBM)


def place(stage, core, block):
    x, z = block // SPAN, block % SPAN
    column = x * SPAN + (SPAN - 1 - z if stage >= STAGES // 2 else z)
    return (2 * stage + core) * BLOCKS + column


def swapped(array):
    return lax.ppermute(array, "section", [(i, i ^ 1) for i in range(2 * STAGES)])


def beside(array, shift):
    route = [(b, b + shift) for b in range(BLOCKS) if 0 <= b + shift < BLOCKS]
    return lax.ppermute(array, "seq", route)


def turned_x(array, distance):
    route = [
        (x * SPAN + z, (x + distance) % SPAN * SPAN + z) for x in range(SPAN) for z in range(SPAN)
    ]
    return lax.ppermute(array, "seq", route)


def turned_z(array, distance):
    route = [
        (x * SPAN + z, x * SPAN + (z + distance) % SPAN) for x in range(SPAN) for z in range(SPAN)
    ]
    return lax.ppermute(array, "seq", route)


def parity(array, tick, step, shift=0):
    route = [
        (place(stage, core, block), place(stage + step, core, block + shift))
        for stage in range(tick % 2, STAGES, 2)
        for core in range(2)
        for block in range(BLOCKS)
        if 0 <= stage + step < STAGES and 0 <= block + shift < BLOCKS
    ]
    return lax.ppermute(array, AXES, route)


def hop(pieces, tick, step):
    main, first, last = pieces
    return (
        parity(main, tick, step),
        parity(last, tick, step, 1),
        parity(first, tick, step, -1),
    )


def after(array, event):
    return lax.optimization_barrier((array, event))[0]


def params(mib):
    return pltpu.CompilerParams(vmem_limit_bytes=mib << 20)


def row_mask(block):
    row = lax.broadcasted_iota(jnp.int32, (WIDE, 1), 0) + (block * ROWS - HALO)
    return (row >= 0) & (row < TOKENS)


def joined_rows(parts):
    return jnp.concatenate([part[...].astype(F32) for part in parts], axis=0)


def normed(total):
    scale = lax.rsqrt(jnp.mean(total * total, axis=-1, keepdims=True) + 1e-06)
    return total * scale, scale


def send_pair(core, source, first, second, sems):
    def start(one, two):
        pltpu.make_async_copy(source.at[0], one, sems.at[0]).start()
        pltpu.make_async_copy(source.at[1], two, sems.at[1]).start()

    pl.when(core == 0)(lambda: start(first, second))
    pl.when(core != 0)(lambda: start(second, first))


def wait_pair(source, first, sems):
    for index in range(2):
        pltpu.make_async_copy(source.at[index], first, sems.at[index]).wait()


def hbm(shape, dtype):
    return pltpu.HBM(shape, dtype)


def forward_kernel(tick, info, *refs):
    half = STAGES // 2
    skips = tick >= half
    last = tick == STAGES - 1
    refs = list(refs)
    main, left, right = refs[:3]
    refs = refs[3:]
    own_skip = refs.pop(0) if tick > half else None
    skip_b = [refs.pop(0) for _ in range(2 if tick == half else 1)] if skips else None
    filters, gains = refs[:2]
    refs = refs[4 if skips else 6 :]
    sums_out, keep_out, give_out = refs[:3]
    refs = refs[3:]
    middle_out, whole_out = (refs.pop(0), refs.pop(0)) if not skips else (None, None)
    out, first_rows, last_rows = (refs.pop(0), refs.pop(0), refs.pop(0)) if not last else (None,) * 3
    near = [refs.pop(0), refs.pop(0)] if tick == half - 1 else None
    whole, middle, pad, sums, acts, sems = refs

    @pl.when(info[0] == tick)
    def _():
        core = info[2]
        keep = row_mask(info[1])
        whole[0:HALO, :] = left[...]
        whole[HALO : HALO + ROWS, :] = main[...]
        whole[HALO + ROWS : WIDE, :] = right[...]
        pad[0:8, :] = jnp.zeros((8, C), F32)
        pad[PAD - 8 : PAD, :] = jnp.zeros((8, C), F32)
        copies = []
        if not skips:
            copies = [pltpu.make_async_copy(whole, whole_out, sems.at[4])]
            copies[0].start()
            if near is None:
                copies.append(pltpu.make_async_copy(middle, middle_out, sems.at[5]))
        sum_copies = [
            pltpu.make_async_copy(sums.at[i], sums_out.at[i], sems.at[i]) for i in range(2)
        ]

        def activated(total, which):
            sums[which] = total
            sum_copies[which].start()
            value, _ = normed(total)
            value = jax.nn.gelu(value * gains[which : which + 1, :])
            rounded = jnp.where(keep, value, 0.0).astype(BF16)
            acts[which] = rounded
            pad[8 : 8 + WIDE, :] = rounded.astype(F32)

        def conv(total, which):
            for tap in range(KERNEL):
                start = 6 + tap
                rows = pad[start : start + WIDE, :].astype(BF16)
                total = total + jnp.dot(rows, filters[which, tap], preferred_element_type=F32)
            return total

        total = whole[...].astype(F32)
        if tick == half:
            total = total + total
        elif skips:
            total = total + own_skip[...].astype(F32)
        activated(total, 0)
        value = conv(total, 0).astype(BF16)
        if near is not None:
            near[0][...] = value[: WIDE // 2]
            near[1][...] = value[WIDE // 2 :]
        elif not skips:
            middle[...] = value
            copies[1].start()
        total = value.astype(F32)
        if skips:
            total = total + joined_rows(skip_b)
        activated(total, 1)
        send_pair(core, acts, keep_out, give_out, sems.at[pl.ds(2, 2)])
        if not last:
            value = conv(total, 1)
            out[...] = value[HALO : HALO + ROWS].astype(BF16)
            first_rows[...] = value[HALO : 2 * HALO].astype(BF16)
            last_rows[...] = value[ROWS : HALO + ROWS].astype(BF16)
        for copy in sum_copies + copies:
            copy.wait()
        wait_pair(acts, keep_out, sems.at[pl.ds(2, 2)])


def forward(tick, info, pieces, skip_a, skip_b, filters, gains, kept, passed):
    last = tick == STAGES - 1
    skips = tick >= STAGES // 2
    args = list(pieces)
    if skip_a is not None:
        args.append(skip_a)
    if skip_b is not None:
        args += skip_b
    edge = jax.ShapeDtypeStruct((HALO, C), BF16)
    held = list(kept) + ([] if skips else list(passed))
    shapes = [hbm((2, WIDE, C), F32)] + [hbm(a.shape, a.dtype) for a in held]
    vmem_shapes = [] if last else [jax.ShapeDtypeStruct((ROWS, C), BF16), edge, edge]
    if tick == STAGES // 2 - 1:
        vmem_shapes += [jax.ShapeDtypeStruct((WIDE // 2, C), BF16)] * 2
    count = 3 + len(args)
    return pl.pallas_call(
        functools.partial(forward_kernel, tick),
        out_shape=shapes + vmem_shapes,
        in_specs=[SMEM_SPEC] + [VMEM_SPEC] * (len(args) + 2) + [HBM_SPEC] * len(held),
        out_specs=[HBM_SPEC] * len(shapes) + [VMEM_SPEC] * len(vmem_shapes),
        scratch_shapes=[
            pltpu.VMEM((WIDE, C), BF16),
            pltpu.VMEM((WIDE, C), BF16),
            pltpu.VMEM((PAD, C), F32),
            pltpu.VMEM((2, WIDE, C), F32),
            pltpu.VMEM((2, WIDE, C), BF16),
            pltpu.SemaphoreType.DMA((6,)),
        ],
        input_output_aliases={count + i: 1 + i for i in range(len(held))},
        compiler_params=params(12),
        name="forward_stage",
    )(info, *args, filters, gains, *held)


def backward_kernel(tick, info, *refs):
    half = STAGES // 2
    joined = tick < half
    refs = list(refs)
    main, left, right = refs[:3]
    refs = refs[3:]
    skip_a = refs.pop(0) if tick < half - 1 else None
    skip_b = [refs.pop(0) for _ in range(2 if tick == half - 1 else 1)] if joined else None
    filters, gains, sums_in = refs[:3]
    refs = refs[5 if joined else 7 :]
    keep_out, give_out = refs[:2]
    refs = refs[2:]
    middle_out, whole_out = (refs.pop(0), refs.pop(0)) if not joined else (None, None)
    out, first_rows, last_rows = (refs.pop(0), refs.pop(0), refs.pop(0)) if tick else (None,) * 3
    near = [refs.pop(0), refs.pop(0)] if tick == half else None
    whole, middle, pad, sums, grads, sems = refs

    @pl.when(info[0] == tick)
    def _():
        core = info[2]
        sum_copies = [
            pltpu.make_async_copy(sums_in.at[i], sums.at[i], sems.at[i]) for i in range(2)
        ]
        sum_copies[1].start()
        sum_copies[0].start()
        keep = row_mask(info[1])
        whole[0:HALO, :] = left[...]
        whole[HALO : HALO + ROWS, :] = main[...]
        whole[HALO + ROWS : WIDE, :] = right[...]
        pad[0:8, :] = jnp.zeros((8, C), F32)
        pad[PAD - 8 : PAD, :] = jnp.zeros((8, C), F32)
        copies = []
        if not joined:
            copies = [pltpu.make_async_copy(whole, whole_out, sems.at[4])]
            copies[0].start()
            if near is None:
                copies.append(pltpu.make_async_copy(middle, middle_out, sems.at[5]))

        def pull(grad, which, last):
            grads[which, 0:ROWS, :] = grad[HALO : HALO + ROWS].astype(BF16)
            pad[8 : 8 + WIDE, :] = grad
            grad_act = jnp.zeros((WIDE, C), F32)
            for tap in range(KERNEL):
                start = 10 - tap
                rows = pad[start : start + WIDE, :].astype(BF16)
                grad_act = grad_act + jnp.dot(
                    rows, filters[which, tap], preferred_element_type=F32
                )
            sum_copies[which].wait()
            gain = gains[which : which + 1, :]
            value, scale = normed(sums[which])
            inner = value * gain
            square = inner * inner
            tanh = jnp.tanh(GELU_A * (inner + GELU_B * (square * inner)))
            slope = 0.5 * (1.0 + tanh) + (0.5 * GELU_A) * inner * (1.0 - tanh * tanh) * (
                1.0 + (3.0 * GELU_B) * square
            )
            grad_inner = grad_act * slope
            product = (grad_inner * value)[HALO : HALO + ROWS]
            grad_gain = jnp.sum(product, axis=0, keepdims=True)
            grads[which, ROWS : ROWS + 8, :] = jnp.broadcast_to(grad_gain, (8, C)).astype(BF16)
            if last:
                return None
            grad_value = grad_inner * gain
            mean = jnp.mean(grad_value * value, axis=-1, keepdims=True)
            result = grad + scale * (grad_value - value * mean)
            return jnp.where(keep, result, 0.0).astype(BF16)

        grad = whole[...].astype(F32)
        if tick == half - 1:
            grad = grad + grad
        elif joined:
            grad = grad + skip_a[...].astype(F32)
        grad = grad.astype(BF16).astype(F32)
        value = pull(grad, 1, False)
        if near is not None:
            near[0][...] = value[: WIDE // 2]
            near[1][...] = value[WIDE // 2 :]
        elif not joined:
            middle[...] = value
            copies[1].start()
        grad = value.astype(F32)
        if joined:
            grad = (grad + joined_rows(skip_b)).astype(BF16).astype(F32)
        value = pull(grad, 0, tick == 0)
        send_pair(core, grads, keep_out, give_out, sems.at[pl.ds(2, 2)])
        if tick:
            value = value.astype(F32)
            out[...] = value[HALO : HALO + ROWS].astype(BF16)
            first_rows[...] = value[HALO : 2 * HALO].astype(BF16)
            last_rows[...] = value[ROWS : HALO + ROWS].astype(BF16)
        for copy in copies:
            copy.wait()
        wait_pair(grads, keep_out, sems.at[pl.ds(2, 2)])


def backward(tick, info, pieces, skip_a, skip_b, sums, filters, gains, kept, passed):
    joined = tick < STAGES // 2
    args = list(pieces)
    if skip_a is not None:
        args.append(skip_a)
    if skip_b is not None:
        args += skip_b
    edge = jax.ShapeDtypeStruct((HALO, C), BF16)
    held = list(kept) + ([] if joined else list(passed))
    shapes = [hbm(a.shape, a.dtype) for a in held]
    vmem_shapes = [jax.ShapeDtypeStruct((ROWS, C), BF16), edge, edge] if tick else []
    if tick == STAGES // 2:
        vmem_shapes += [jax.ShapeDtypeStruct((WIDE // 2, C), BF16)] * 2
    count = 4 + len(args)
    return pl.pallas_call(
        functools.partial(backward_kernel, tick),
        out_shape=shapes + vmem_shapes,
        in_specs=[SMEM_SPEC] + [VMEM_SPEC] * (len(args) + 2) + [HBM_SPEC] * (1 + len(held)),
        out_specs=[HBM_SPEC] * len(shapes) + [VMEM_SPEC] * len(vmem_shapes),
        scratch_shapes=[
            pltpu.VMEM((WIDE, C), BF16),
            pltpu.VMEM((WIDE, C), BF16),
            pltpu.VMEM((PAD, C), F32),
            pltpu.VMEM((2, WIDE, C), F32),
            pltpu.VMEM((2, ROWS + 8, C), BF16),
            pltpu.SemaphoreType.DMA((6,)),
        ],
        input_output_aliases={count + i: i for i in range(len(held))},
        compiler_params=params(12),
        name="backward_stage",
    )(info, *args, filters, gains, sums, *held)


def pair_kernel(info, own, other, pair, *refs):
    core, sems = info[2], refs[-1]
    copies = [
        pltpu.make_async_copy(own.at[0], pair.at[core], sems.at[0]),
        pltpu.make_async_copy(other.at[0], pair.at[1 - core], sems.at[1]),
    ]
    for copy in copies:
        copy.start()
    for copy in copies:
        copy.wait()


def transpose_kernel(own, out, source, result, sems_in, sems_out):
    def load(tap, slot):
        return pltpu.make_async_copy(own.at[0, tap], source.at[slot], sems_in.at[slot])

    def save(tap, slot):
        return pltpu.make_async_copy(result.at[slot], out.at[0, tap], sems_out.at[slot])

    load(0, 0).start()
    for tap in range(KERNEL):
        slot = tap % 2
        if tap + 1 < KERNEL:
            load(tap + 1, 1 - slot).start()
        load(tap, slot).wait()
        if tap >= 2:
            save(tap - 2, slot).wait()

        def part(index, _):
            rows = pl.ds(pl.multiple_of(index * 256, 256), 256)
            row = lax.broadcasted_iota(jnp.int32, (256, C), 0) + index * 256
            eye = (row == lax.broadcasted_iota(jnp.int32, (256, C), 1)).astype(BF16)
            result[slot, rows, :] = lax.dot_general(
                eye, source[slot], (((1,), (1,)), ((), ())), preferred_element_type=F32
            ).astype(BF16)
            return 0

        lax.fori_loop(0, C // 256, part, 0)
        save(tap, slot).start()
    for tap in range(KERNEL - 2, KERNEL):
        save(tap, tap % 2).wait()


def transposed(own):
    return pl.pallas_call(
        transpose_kernel,
        out_shape=hbm(own.shape, own.dtype),
        in_specs=[HBM_SPEC],
        out_specs=HBM_SPEC,
        scratch_shapes=[
            pltpu.VMEM((2, C, C), BF16),
            pltpu.VMEM((2, C, C), BF16),
            pltpu.SemaphoreType.DMA((2,)),
            pltpu.SemaphoreType.DMA((2,)),
        ],
        compiler_params=params(12),
        name="turn_filters",
    )(own)


def paired(info, own, other, blanks, mib):
    return pl.pallas_call(
        pair_kernel,
        out_shape=[pltpu.VMEM((2, *own.shape[1:]), own.dtype)]
        + [hbm(shape, BF16) for shape in blanks],
        in_specs=[SMEM_SPEC, HBM_SPEC, HBM_SPEC],
        out_specs=[VMEM_SPEC] + [HBM_SPEC] * len(blanks),
        scratch_shapes=[pltpu.SemaphoreType.DMA((2,))],
        compiler_params=params(mib),
        name="weight_pair",
    )(info, own, other)


def split_kernel(info, keep, got, *outs):
    share = C // BLOCKS
    by_x, by_z = outs[:SPAN], outs[SPAN:]
    for index, array in enumerate((keep, got)):
        rows = array[...]
        for part in range(SPAN):
            one = rows[:, part * SPAN * share : (part + 1) * SPAN * share]
            other = jnp.concatenate(
                [
                    rows[:, (turn * SPAN + part) * share : (turn * SPAN + part + 1) * share]
                    for turn in range(SPAN)
                ],
                axis=1,
            )
            for place_of, piece, targets in ((3, one, by_x), (4, other, by_z)):
                for distance, out in enumerate(targets):

                    @pl.when(lax.rem(info[place_of] + distance, SPAN) == part)
                    def _():
                        out[index] = piece


def split(info, keep, got):
    return pl.pallas_call(
        split_kernel,
        out_shape=[jax.ShapeDtypeStruct((2, WIDE, C // SPAN), BF16)] * (2 * SPAN),
        in_specs=[SMEM_SPEC, VMEM_SPEC, VMEM_SPEC],
        out_specs=[VMEM_SPEC] * (2 * SPAN),
        compiler_params=params(10),
        name="split_rows",
    )(info, keep, got)


def combine_kernel(keep, got, first, second):
    width = C // 2
    for index, array in enumerate((keep, got)):
        rows = slice(index * ROWS, (index + 1) * ROWS)
        first[rows, :] = array[0:ROWS, 0:width]
        second[rows, :] = array[0:ROWS, width:C]
    gain = keep[ROWS : ROWS + 8, :].astype(F32) + got[ROWS : ROWS + 8, :].astype(F32)
    row = lax.broadcasted_iota(jnp.int32, (8, width), 0)
    gain = jnp.where(row == 0, gain[:, 0:width], gain[:, width:C])
    first[2 * ROWS : 2 * ROWS + 8, :] = gain.astype(BF16)


def combined(keep, got):
    return pl.pallas_call(
        combine_kernel,
        out_shape=[
            jax.ShapeDtypeStruct((2 * ROWS + 8, C // 2), BF16),
            jax.ShapeDtypeStruct((2 * ROWS, C // 2), BF16),
        ],
        in_specs=[VMEM_SPEC] * 2,
        out_specs=[VMEM_SPEC] * 2,
        compiler_params=params(8),
        name="combine_rows",
    )(keep, got)


def turn_kernel(*refs):
    pieces, out = refs[:SPAN], refs[SPAN]
    width = C // SPAN
    for index, piece in enumerate(pieces):
        for micro in range(2):
            rows = piece[micro].astype(F32).T
            column = (2 * index + micro) * ROWS
            for tap in range(KERNEL):
                start = HALO - 2 + tap
                out[tap * width : (tap + 1) * width, column : column + ROWS] = rows[
                    :, start : start + ROWS
                ].astype(BF16)


def turned(pieces):
    width = C // SPAN
    return pl.pallas_call(
        turn_kernel,
        out_shape=jax.ShapeDtypeStruct((KERNEL * width, SPAN * 2 * ROWS), BF16),
        in_specs=[VMEM_SPEC] * SPAN,
        out_specs=VMEM_SPEC,
        compiler_params=params(12),
        name="turn_rows",
    )(*pieces)


def product_kernel(place_of, info, rows_t, *refs):
    pieces, outs, total = refs[:SPAN], refs[SPAN : 2 * SPAN], refs[-1]
    count = 2 * ROWS
    for index, piece in enumerate(pieces):
        term = jnp.dot(
            rows_t[:, index * count : (index + 1) * count],
            piece[0:count, :],
            preferred_element_type=F32,
        )
        total[...] = term if index == 0 else total[...] + term
    width = C // SPAN
    share = width // SPAN
    height = KERNEL * share
    extra = pieces[0].shape[0] - count
    if extra:
        gain = sum(piece[count : count + extra, :].astype(F32) for piece in pieces).astype(BF16)
    for distance, out in enumerate(outs):
        target = lax.rem(info[place_of] + distance, SPAN)
        for tap in range(KERNEL):
            start = pl.multiple_of(tap * width + target * share, 8)
            out[tap * share : (tap + 1) * share, :] = total[pl.ds(start, share), :].astype(BF16)
        if extra:
            out[height : height + extra, :] = gain


def product(place_of, info, rows_t, pieces):
    height = rows_t.shape[0] // SPAN + pieces[0].shape[0] - 2 * ROWS
    return pl.pallas_call(
        functools.partial(product_kernel, place_of),
        out_shape=[jax.ShapeDtypeStruct((height, C // 2), BF16)] * SPAN,
        in_specs=[SMEM_SPEC] + [VMEM_SPEC] * (1 + SPAN),
        out_specs=[VMEM_SPEC] * SPAN,
        scratch_shapes=[pltpu.VMEM((rows_t.shape[0], C // 2), F32)],
        compiler_params=params(12),
        name="kernel_grad",
    )(info, rows_t, *pieces)


def mirrored(array, pairs):
    route = [
        (place(source, core, block), place(target, core, block))
        for source, target in pairs
        for core in range(2)
        for block in range(BLOCKS)
    ]
    return lax.ppermute(array, AXES, route)


def nearest(halves):
    half, last = STAGES // 2, STAGES - 1
    outer = mirrored(halves[1], [(half - 1, 0), (half, last)])
    return [
        mirrored(halves[0], [(half - 1, half), (half, half - 1)]),
        mirrored(outer, [(0, half), (last, half - 1)]),
    ]


def shards(base_ids, stem_weight, conv_weight, block_gain, cotangent):
    section = lax.axis_index("section")
    column = lax.axis_index("seq")
    stage, core = section // 2, section % 2
    x, z = column // SPAN, column % SPAN
    late = stage >= STAGES // 2
    block = x * SPAN + jnp.where(late, SPAN - 1 - z, z)
    info = jnp.stack([stage, block, core, x, z]).astype(jnp.int32)
    half = STAGES // 2
    last = STAGES - 1

    wide, own = (WIDE, C), (ROWS + 8, C)
    other_filters = swapped(conv_weight)
    other_gain = swapped(block_gain)
    gains = jnp.where(
        core == 0,
        jnp.concatenate([block_gain, other_gain], 0),
        jnp.concatenate([other_gain, block_gain], 0),
    )

    reach = HALO + STEM_K // 2
    ids = base_ids + 1
    ids = jnp.concatenate(
        [beside(ids[:, -reach:], 1), ids, beside(ids[:, :reach], -1)], 1
    )
    ids = lax.dynamic_index_in_dim(ids, core, 0, keepdims=False)
    letters = jnp.arange(1, BASES + 1, dtype=jnp.int32)
    onehot = jnp.concatenate(
        [ids[offset : offset + WIDE, None] == letters for offset in range(STEM_K)], axis=1
    ).astype(BF16)
    stem = jnp.dot(
        onehot, stem_weight.reshape(STEM_K * BASES, C), preferred_element_type=F32
    ).astype(BF16)
    pieces = (stem[HALO : HALO + ROWS], stem[:HALO], stem[HALO + ROWS :])

    cot = lax.dynamic_index_in_dim(cotangent, core, 0, keepdims=False)

    def cot_moved(rows, shift):
        route = [
            ((2 * last + c) * BLOCKS + b, place(last, c, b + shift))
            for c in range(2)
            for b in range(BLOCKS)
            if 0 <= b + shift < BLOCKS
        ]
        return lax.ppermute(rows, AXES, route)

    cot_pieces = (
        cot_moved(cot, 0),
        cot_moved(cot[ROWS - HALO :], 1),
        cot_moved(cot[:HALO], -1),
    )

    pieces, cot_pieces, gains = lax.optimization_barrier((pieces, cot_pieces, gains))
    info = after(info, (pieces, gains))
    filters, *blanks = paired(info, conv_weight, other_filters, [wide] * 6 + [own] * 2, 44)
    skip_near = skip_far = skip_whole = None
    sums = []
    kept, passed = blanks[0:2], blanks[2:4]
    for tick in range(STAGES):
        results = forward(
            tick,
            info,
            pieces,
            skip_whole if tick > half else None,
            skip_near if tick == half else skip_far,
            filters,
            gains,
            kept,
            passed,
        )
        if tick == half:
            turned_own = transposed(after(conv_weight, results[-1]))
            info = after(info, turned_own)
        elif tick == half + 1:
            turned_other = swapped(after(turned_own, results[-1]))
        elif tick == half + 2:
            turned_pair = after((turned_own, turned_other), results[-1])
            (back_filters,) = paired(info, *turned_pair, [], 12)
            info = after(info, back_filters)
        sums.append(results[0])
        kept = results[1:3]
        if tick < half:
            passed = results[3:5]
        if tick == half - 1:
            skip_near = nearest(results[-2:])
            pieces = hop(results[-5:-2], tick, 1)
            late = after(tuple(passed), pieces)
            skip_whole = mirrored(late[1], [(t, STAGES - t) for t in range(1, half)])
            skip_far = [mirrored(late[0], [(t, last - t) for t in range(half - 1)])]
        elif tick < last:
            pieces = hop(results[-3:], tick, 1)

    acts = kept
    pieces = cot_pieces
    skip_near = skip_far = skip_whole = None
    kept, passed = blanks[6:8], blanks[4:6]
    for tick in reversed(range(STAGES)):
        results = backward(
            tick,
            info,
            pieces,
            skip_whole if tick < half - 1 else None,
            skip_near if tick == half - 1 else skip_far,
            sums[tick],
            back_filters,
            gains,
            kept,
            passed,
        )
        kept = results[:2]
        event = results[-1]
        if tick == last:
            got = swapped(after(acts[1], event))
            info = after(info, got)
        elif tick == last - 1:
            keep, got = after((acts[0], got), event)
            parts = split(info, keep, got)
            by_x, by_z = [parts[0]], [parts[SPAN]]
            by_x.append(turned_x(parts[1], 1))
            info = after(info, by_x)
        elif tick == last - 2:
            later = after(tuple(parts), event)
            by_x += [turned_x(later[d], d) for d in (2, 3)]
            info = after(info, by_x)
        elif tick == half - 2:
            later = after(tuple(parts), event)
            by_z += [turned_z(later[SPAN + d], d) for d in (1, 2)]
            info = after(info, by_z)
        elif tick == half - 3:
            by_x, by_z, later = after((by_x, by_z, tuple(parts)), event)
            by_z = by_z + [turned_z(later[SPAN + 3], 3)]
            rows_x, rows_z = turned(by_x), turned(by_z)
            info = after(info, (rows_x, rows_z))
        if tick >= half:
            passed = results[2:4]
        if tick == half:
            skip_near = nearest(results[-2:])
            pieces = hop(results[-5:-2], tick, -1)
            late = after(tuple(passed), pieces)
            skip_whole = mirrored(late[1], [(t, last - 1 - t) for t in range(half, last)])
            skip_far = [mirrored(late[0], [(t, last - t) for t in range(half + 1, STAGES)])]
        elif tick:
            pieces = hop(results[-3:], tick, -1)

    first, second = combined(kept[0], swapped(kept[1]))
    by_x = [first] + [turned_x(first, d) for d in range(1, SPAN)]
    by_z = [second] + [turned_z(second, d) for d in range(1, SPAN)]
    parts = product(4, info, rows_x, by_x)
    total = parts[0].astype(F32)
    for d in range(1, SPAN):
        total = total + turned_z(parts[d], d).astype(F32)
    parts = product(3, after(info, parts), rows_z, by_z)
    other = parts[0].astype(F32)
    for d in range(1, SPAN):
        other = other + turned_x(parts[d], d).astype(F32)
    share = C // BLOCKS
    height = KERNEL * share
    kernel_grad = jnp.concatenate([total[:height].astype(BF16), other.astype(BF16)], axis=1)
    gain_grad = jnp.concatenate([total[height], total[height + 1]], axis=0)
    gain_grad = lax.dynamic_slice_in_dim(gain_grad, column * share, share)
    return kernel_grad.reshape(1, KERNEL, share, C), gain_grad[None]


def solution(mesh):
    placed = (
        P(None, "seq"),
        P(),
        P("section", None, None, None),
        P("section", None),
        P(None, "seq", None),
    )
    return jax.shard_map(
        shards,
        mesh=mesh,
        in_specs=placed,
        out_specs=(P("section", None, "seq", None), P("section", "seq")),
        check_vma=False,
    )
```

```python
import functools

import jax
import jax.numpy as jnp
from jax import lax
from jax.experimental import pallas as pl
from jax.experimental.pallas import tpu as pltpu
from jax.sharding import PartitionSpec as P

KERNEL = 5
STEM_K = 15
BASES = 4
C = 768
ROWS = 128
HALO = 8
WIDE = ROWS + 2 * HALO
PAD = WIDE + 16
STAGES = 8
BLOCKS = 16
SPAN = 4
TOKENS = BLOCKS * ROWS
AXES = ("section", "seq")
BF16 = jnp.bfloat16
F32 = jnp.float32
GELU_A = 0.7978845608028654
GELU_B = 0.044715
VMEM_SPEC = pl.BlockSpec(memory_space=pltpu.VMEM)
SMEM_SPEC = pl.BlockSpec(memory_space=pltpu.SMEM)
HBM_SPEC = pl.BlockSpec(memory_space=pltpu.HBM)


def place(stage, core, block):
    x, z = block // SPAN, block % SPAN
    column = x * SPAN + (SPAN - 1 - z if stage >= STAGES // 2 else z)
    return (2 * stage + core) * BLOCKS + column


def swapped(array):
    return lax.ppermute(array, "section", [(i, i ^ 1) for i in range(2 * STAGES)])


def beside(array, shift):
    route = [(b, b + shift) for b in range(BLOCKS) if 0 <= b + shift < BLOCKS]
    return lax.ppermute(array, "seq", route)


def turned_x(array, distance):
    route = [
        (x * SPAN + z, (x + distance) % SPAN * SPAN + z) for x in range(SPAN) for z in range(SPAN)
    ]
    return lax.ppermute(array, "seq", route)


def turned_z(array, distance):
    route = [
        (x * SPAN + z, x * SPAN + (z + distance) % SPAN) for x in range(SPAN) for z in range(SPAN)
    ]
    return lax.ppermute(array, "seq", route)


def parity(array, tick, step, shift=0):
    route = [
        (place(stage, core, block), place(stage + step, core, block + shift))
        for stage in range(tick % 2, STAGES, 2)
        for core in range(2)
        for block in range(BLOCKS)
        if 0 <= stage + step < STAGES and 0 <= block + shift < BLOCKS
    ]
    return lax.ppermute(array, AXES, route)


def hop(pieces, tick, step):
    main, first, last = pieces
    return (
        parity(main, tick, step),
        parity(last, tick, step, 1),
        parity(first, tick, step, -1),
    )


def after(array, event):
    return lax.optimization_barrier((array, event))[0]


def params(mib):
    return pltpu.CompilerParams(vmem_limit_bytes=mib << 20)


def row_mask(block):
    row = lax.broadcasted_iota(jnp.int32, (WIDE, 1), 0) + (block * ROWS - HALO)
    return (row >= 0) & (row < TOKENS)


def joined_rows(parts):
    return jnp.concatenate([part[...].astype(F32) for part in parts], axis=0)


def normed(total):
    scale = lax.rsqrt(jnp.mean(total * total, axis=-1, keepdims=True) + 1e-06)
    return total * scale, scale


def send_pair(core, source, first, second, sems):
    def start(one, two):
        pltpu.make_async_copy(source.at[0], one, sems.at[0]).start()
        pltpu.make_async_copy(source.at[1], two, sems.at[1]).start()

    pl.when(core == 0)(lambda: start(first, second))
    pl.when(core != 0)(lambda: start(second, first))


def wait_pair(source, first, sems):
    for index in range(2):
        pltpu.make_async_copy(source.at[index], first, sems.at[index]).wait()


def hbm(shape, dtype):
    return pltpu.HBM(shape, dtype)


def forward_kernel(tick, info, *refs):
    half = STAGES // 2
    skips = tick >= half
    last = tick == STAGES - 1
    refs = list(refs)
    main, left, right = refs[:3]
    refs = refs[3:]
    own_skip = refs.pop(0) if tick > half else None
    skip_b = [refs.pop(0) for _ in range(2 if tick == half else 1)] if skips else None
    filters, gains = refs[:2]
    refs = refs[4 if skips else 6 :]
    sums_out, keep_out, give_out = refs[:3]
    refs = refs[3:]
    middle_out, whole_out = (refs.pop(0), refs.pop(0)) if not skips else (None, None)
    out, first_rows, last_rows = (refs.pop(0), refs.pop(0), refs.pop(0)) if not last else (None,) * 3
    near = [refs.pop(0), refs.pop(0)] if tick == half - 1 else None
    whole, middle, pad, sums, acts, sems = refs

    @pl.when(info[0] == tick)
    def _():
        core = info[2]
        keep = row_mask(info[1])
        whole[0:HALO, :] = left[...]
        whole[HALO : HALO + ROWS, :] = main[...]
        whole[HALO + ROWS : WIDE, :] = right[...]
        pad[0:8, :] = jnp.zeros((8, C), F32)
        pad[PAD - 8 : PAD, :] = jnp.zeros((8, C), F32)
        copies = []
        if not skips:
            copies = [pltpu.make_async_copy(whole, whole_out, sems.at[4])]
            copies[0].start()
            if near is None:
                copies.append(pltpu.make_async_copy(middle, middle_out, sems.at[5]))
        sum_copies = [
            pltpu.make_async_copy(sums.at[i], sums_out.at[i], sems.at[i]) for i in range(2)
        ]

        def activated(total, which):
            sums[which] = total
            sum_copies[which].start()
            value, _ = normed(total)
            value = jax.nn.gelu(value * gains[which : which + 1, :])
            rounded = jnp.where(keep, value, 0.0).astype(BF16)
            acts[which] = rounded
            pad[8 : 8 + WIDE, :] = rounded.astype(F32)

        def conv(total, which):
            for tap in range(KERNEL):
                start = 6 + tap
                rows = pad[start : start + WIDE, :].astype(BF16)
                total = total + jnp.dot(rows, filters[which, tap], preferred_element_type=F32)
            return total

        total = whole[...].astype(F32)
        if tick == half:
            total = total + total
        elif skips:
            total = total + own_skip[...].astype(F32)
        activated(total, 0)
        value = conv(total, 0).astype(BF16)
        if near is not None:
            near[0][...] = value[: WIDE // 2]
            near[1][...] = value[WIDE // 2 :]
        elif not skips:
            middle[...] = value
            copies[1].start()
        total = value.astype(F32)
        if skips:
            total = total + joined_rows(skip_b)
        activated(total, 1)
        send_pair(core, acts, keep_out, give_out, sems.at[pl.ds(2, 2)])
        if not last:
            value = conv(total, 1)
            out[...] = value[HALO : HALO + ROWS].astype(BF16)
            first_rows[...] = value[HALO : 2 * HALO].astype(BF16)
            last_rows[...] = value[ROWS : HALO + ROWS].astype(BF16)
        for copy in sum_copies + copies:
            copy.wait()
        wait_pair(acts, keep_out, sems.at[pl.ds(2, 2)])


def forward(tick, info, pieces, skip_a, skip_b, filters, gains, kept, passed):
    last = tick == STAGES - 1
    skips = tick >= STAGES // 2
    args = list(pieces)
    if skip_a is not None:
        args.append(skip_a)
    if skip_b is not None:
        args += skip_b
    edge = jax.ShapeDtypeStruct((HALO, C), BF16)
    held = list(kept) + ([] if skips else list(passed))
    shapes = [hbm((2, WIDE, C), F32)] + [hbm(a.shape, a.dtype) for a in held]
    vmem_shapes = [] if last else [jax.ShapeDtypeStruct((ROWS, C), BF16), edge, edge]
    if tick == STAGES // 2 - 1:
        vmem_shapes += [jax.ShapeDtypeStruct((WIDE // 2, C), BF16)] * 2
    count = 3 + len(args)
    return pl.pallas_call(
        functools.partial(forward_kernel, tick),
        out_shape=shapes + vmem_shapes,
        in_specs=[SMEM_SPEC] + [VMEM_SPEC] * (len(args) + 2) + [HBM_SPEC] * len(held),
        out_specs=[HBM_SPEC] * len(shapes) + [VMEM_SPEC] * len(vmem_shapes),
        scratch_shapes=[
            pltpu.VMEM((WIDE, C), BF16),
            pltpu.VMEM((WIDE, C), BF16),
            pltpu.VMEM((PAD, C), F32),
            pltpu.VMEM((2, WIDE, C), F32),
            pltpu.VMEM((2, WIDE, C), BF16),
            pltpu.SemaphoreType.DMA((6,)),
        ],
        input_output_aliases={count + i: 1 + i for i in range(len(held))},
        compiler_params=params(12),
        name="forward_stage",
    )(info, *args, filters, gains, *held)


def backward_kernel(tick, info, *refs):
    half = STAGES // 2
    joined = tick < half
    refs = list(refs)
    main, left, right = refs[:3]
    refs = refs[3:]
    skip_a = refs.pop(0) if tick < half - 1 else None
    skip_b = [refs.pop(0) for _ in range(2 if tick == half - 1 else 1)] if joined else None
    filters, gains, sums_in = refs[:3]
    refs = refs[5 if joined else 7 :]
    keep_out, give_out = refs[:2]
    refs = refs[2:]
    middle_out, whole_out = (refs.pop(0), refs.pop(0)) if not joined else (None, None)
    out, first_rows, last_rows = (refs.pop(0), refs.pop(0), refs.pop(0)) if tick else (None,) * 3
    near = [refs.pop(0), refs.pop(0)] if tick == half else None
    whole, middle, pad, sums, grads, sems = refs

    @pl.when(info[0] == tick)
    def _():
        core = info[2]
        sum_copies = [
            pltpu.make_async_copy(sums_in.at[i], sums.at[i], sems.at[i]) for i in range(2)
        ]
        sum_copies[1].start()
        sum_copies[0].start()
        keep = row_mask(info[1])
        whole[0:HALO, :] = left[...]
        whole[HALO : HALO + ROWS, :] = main[...]
        whole[HALO + ROWS : WIDE, :] = right[...]
        pad[0:8, :] = jnp.zeros((8, C), F32)
        pad[PAD - 8 : PAD, :] = jnp.zeros((8, C), F32)
        copies = []
        if not joined:
            copies = [pltpu.make_async_copy(whole, whole_out, sems.at[4])]
            copies[0].start()
            if near is None:
                copies.append(pltpu.make_async_copy(middle, middle_out, sems.at[5]))

        def pull(grad, which, last):
            grads[which, 0:ROWS, :] = grad[HALO : HALO + ROWS].astype(BF16)
            pad[8 : 8 + WIDE, :] = grad
            grad_act = jnp.zeros((WIDE, C), F32)
            for tap in range(KERNEL):
                start = 10 - tap
                rows = pad[start : start + WIDE, :].astype(BF16)
                grad_act = grad_act + jnp.dot(
                    rows, filters[which, tap], preferred_element_type=F32
                )
            sum_copies[which].wait()
            gain = gains[which : which + 1, :]
            value, scale = normed(sums[which])
            inner = value * gain
            square = inner * inner
            tanh = jnp.tanh(GELU_A * (inner + GELU_B * (square * inner)))
            slope = 0.5 * (1.0 + tanh) + (0.5 * GELU_A) * inner * (1.0 - tanh * tanh) * (
                1.0 + (3.0 * GELU_B) * square
            )
            grad_inner = grad_act * slope
            product = (grad_inner * value)[HALO : HALO + ROWS]
            grad_gain = jnp.sum(product, axis=0, keepdims=True)
            grads[which, ROWS : ROWS + 8, :] = jnp.broadcast_to(grad_gain, (8, C)).astype(BF16)
            if last:
                return None
            grad_value = grad_inner * gain
            mean = jnp.mean(grad_value * value, axis=-1, keepdims=True)
            result = grad + scale * (grad_value - value * mean)
            return jnp.where(keep, result, 0.0).astype(BF16)

        grad = whole[...].astype(F32)
        if tick == half - 1:
            grad = grad + grad
        elif joined:
            grad = grad + skip_a[...].astype(F32)
        grad = grad.astype(BF16).astype(F32)
        value = pull(grad, 1, False)
        if near is not None:
            near[0][...] = value[: WIDE // 2]
            near[1][...] = value[WIDE // 2 :]
        elif not joined:
            middle[...] = value
            copies[1].start()
        grad = value.astype(F32)
        if joined:
            grad = (grad + joined_rows(skip_b)).astype(BF16).astype(F32)
        value = pull(grad, 0, tick == 0)
        send_pair(core, grads, keep_out, give_out, sems.at[pl.ds(2, 2)])
        if tick:
            value = value.astype(F32)
            out[...] = value[HALO : HALO + ROWS].astype(BF16)
            first_rows[...] = value[HALO : 2 * HALO].astype(BF16)
            last_rows[...] = value[ROWS : HALO + ROWS].astype(BF16)
        for copy in copies:
            copy.wait()
        wait_pair(grads, keep_out, sems.at[pl.ds(2, 2)])


def backward(tick, info, pieces, skip_a, skip_b, sums, filters, gains, kept, passed):
    joined = tick < STAGES // 2
    args = list(pieces)
    if skip_a is not None:
        args.append(skip_a)
    if skip_b is not None:
        args += skip_b
    edge = jax.ShapeDtypeStruct((HALO, C), BF16)
    held = list(kept) + ([] if joined else list(passed))
    shapes = [hbm(a.shape, a.dtype) for a in held]
    vmem_shapes = [jax.ShapeDtypeStruct((ROWS, C), BF16), edge, edge] if tick else []
    if tick == STAGES // 2:
        vmem_shapes += [jax.ShapeDtypeStruct((WIDE // 2, C), BF16)] * 2
    count = 4 + len(args)
    return pl.pallas_call(
        functools.partial(backward_kernel, tick),
        out_shape=shapes + vmem_shapes,
        in_specs=[SMEM_SPEC] + [VMEM_SPEC] * (len(args) + 2) + [HBM_SPEC] * (1 + len(held)),
        out_specs=[HBM_SPEC] * len(shapes) + [VMEM_SPEC] * len(vmem_shapes),
        scratch_shapes=[
            pltpu.VMEM((WIDE, C), BF16),
            pltpu.VMEM((WIDE, C), BF16),
            pltpu.VMEM((PAD, C), F32),
            pltpu.VMEM((2, WIDE, C), F32),
            pltpu.VMEM((2, ROWS + 8, C), BF16),
            pltpu.SemaphoreType.DMA((6,)),
        ],
        input_output_aliases={count + i: i for i in range(len(held))},
        compiler_params=params(12),
        name="backward_stage",
    )(info, *args, filters, gains, sums, *held)


def pair_kernel(info, own, other, pair, *refs):
    core, sems = info[2], refs[-1]
    copies = [
        pltpu.make_async_copy(own.at[0], pair.at[core], sems.at[0]),
        pltpu.make_async_copy(other.at[0], pair.at[1 - core], sems.at[1]),
    ]
    for copy in copies:
        copy.start()
    for copy in copies:
        copy.wait()


def transpose_kernel(own, out, source, result, sems_in, sems_out):
    def load(tap, slot):
        return pltpu.make_async_copy(own.at[0, tap], source.at[slot], sems_in.at[slot])

    def save(tap, slot):
        return pltpu.make_async_copy(result.at[slot], out.at[0, tap], sems_out.at[slot])

    load(0, 0).start()
    for tap in range(KERNEL):
        slot = tap % 2
        if tap + 1 < KERNEL:
            load(tap + 1, 1 - slot).start()
        load(tap, slot).wait()
        if tap >= 2:
            save(tap - 2, slot).wait()

        def part(index, _):
            rows = pl.ds(pl.multiple_of(index * 256, 256), 256)
            row = lax.broadcasted_iota(jnp.int32, (256, C), 0) + index * 256
            eye = (row == lax.broadcasted_iota(jnp.int32, (256, C), 1)).astype(BF16)
            result[slot, rows, :] = lax.dot_general(
                eye, source[slot], (((1,), (1,)), ((), ())), preferred_element_type=F32
            ).astype(BF16)
            return 0

        lax.fori_loop(0, C // 256, part, 0)
        save(tap, slot).start()
    for tap in range(KERNEL - 2, KERNEL):
        save(tap, tap % 2).wait()


def transposed(own):
    return pl.pallas_call(
        transpose_kernel,
        out_shape=hbm(own.shape, own.dtype),
        in_specs=[HBM_SPEC],
        out_specs=HBM_SPEC,
        scratch_shapes=[
            pltpu.VMEM((2, C, C), BF16),
            pltpu.VMEM((2, C, C), BF16),
            pltpu.SemaphoreType.DMA((2,)),
            pltpu.SemaphoreType.DMA((2,)),
        ],
        compiler_params=params(12),
        name="turn_filters",
    )(own)


def paired(info, own, other, blanks, mib):
    return pl.pallas_call(
        pair_kernel,
        out_shape=[pltpu.VMEM((2, *own.shape[1:]), own.dtype)]
        + [hbm(shape, BF16) for shape in blanks],
        in_specs=[SMEM_SPEC, HBM_SPEC, HBM_SPEC],
        out_specs=[VMEM_SPEC] + [HBM_SPEC] * len(blanks),
        scratch_shapes=[pltpu.SemaphoreType.DMA((2,))],
        compiler_params=params(mib),
        name="weight_pair",
    )(info, own, other)


def split_kernel(info, keep, got, *outs):
    share = C // BLOCKS
    by_x, by_z = outs[:SPAN], outs[SPAN:]
    for index, array in enumerate((keep, got)):
        rows = array[...]
        for part in range(SPAN):
            one = rows[:, part * SPAN * share : (part + 1) * SPAN * share]
            other = jnp.concatenate(
                [
                    rows[:, (turn * SPAN + part) * share : (turn * SPAN + part + 1) * share]
                    for turn in range(SPAN)
                ],
                axis=1,
            )
            for place_of, piece, targets in ((3, one, by_x), (4, other, by_z)):
                for distance, out in enumerate(targets):

                    @pl.when(lax.rem(info[place_of] + distance, SPAN) == part)
                    def _():
                        out[index] = piece


def split(info, keep, got):
    return pl.pallas_call(
        split_kernel,
        out_shape=[jax.ShapeDtypeStruct((2, WIDE, C // SPAN), BF16)] * (2 * SPAN),
        in_specs=[SMEM_SPEC, VMEM_SPEC, VMEM_SPEC],
        out_specs=[VMEM_SPEC] * (2 * SPAN),
        compiler_params=params(10),
        name="split_rows",
    )(info, keep, got)


def combine_kernel(keep, got, first, second):
    width = C // 2
    for index, array in enumerate((keep, got)):
        rows = slice(index * ROWS, (index + 1) * ROWS)
        first[rows, :] = array[0:ROWS, 0:width]
        second[rows, :] = array[0:ROWS, width:C]
    gain = keep[ROWS : ROWS + 8, :].astype(F32) + got[ROWS : ROWS + 8, :].astype(F32)
    row = lax.broadcasted_iota(jnp.int32, (8, width), 0)
    gain = jnp.where(row == 0, gain[:, 0:width], gain[:, width:C])
    first[2 * ROWS : 2 * ROWS + 8, :] = gain.astype(BF16)


def combined(keep, got):
    return pl.pallas_call(
        combine_kernel,
        out_shape=[
            jax.ShapeDtypeStruct((2 * ROWS + 8, C // 2), BF16),
            jax.ShapeDtypeStruct((2 * ROWS, C // 2), BF16),
        ],
        in_specs=[VMEM_SPEC] * 2,
        out_specs=[VMEM_SPEC] * 2,
        compiler_params=params(8),
        name="combine_rows",
    )(keep, got)


def turn_kernel(*refs):
    pieces, out = refs[:SPAN], refs[SPAN]
    width = C // SPAN
    for index, piece in enumerate(pieces):
        for micro in range(2):
            rows = piece[micro].astype(F32).T
            column = (2 * index + micro) * ROWS
            for tap in range(KERNEL):
                start = HALO - 2 + tap
                out[tap * width : (tap + 1) * width, column : column + ROWS] = rows[
                    :, start : start + ROWS
                ].astype(BF16)


def turned(pieces):
    width = C // SPAN
    return pl.pallas_call(
        turn_kernel,
        out_shape=jax.ShapeDtypeStruct((KERNEL * width, SPAN * 2 * ROWS), BF16),
        in_specs=[VMEM_SPEC] * SPAN,
        out_specs=VMEM_SPEC,
        compiler_params=params(12),
        name="turn_rows",
    )(*pieces)


def product_kernel(place_of, info, rows_t, *refs):
    pieces, outs, total = refs[:SPAN], refs[SPAN : 2 * SPAN], refs[-1]
    count = 2 * ROWS
    for index, piece in enumerate(pieces):
        term = jnp.dot(
            rows_t[:, index * count : (index + 1) * count],
            piece[0:count, :],
            preferred_element_type=F32,
        )
        total[...] = term if index == 0 else total[...] + term
    width = C // SPAN
    share = width // SPAN
    height = KERNEL * share
    extra = pieces[0].shape[0] - count
    if extra:
        gain = sum(piece[count : count + extra, :].astype(F32) for piece in pieces).astype(BF16)
    for distance, out in enumerate(outs):
        target = lax.rem(info[place_of] + distance, SPAN)
        for tap in range(KERNEL):
            start = pl.multiple_of(tap * width + target * share, 8)
            out[tap * share : (tap + 1) * share, :] = total[pl.ds(start, share), :].astype(BF16)
        if extra:
            out[height : height + extra, :] = gain


def product(place_of, info, rows_t, pieces):
    height = rows_t.shape[0] // SPAN + pieces[0].shape[0] - 2 * ROWS
    return pl.pallas_call(
        functools.partial(product_kernel, place_of),
        out_shape=[jax.ShapeDtypeStruct((height, C // 2), BF16)] * SPAN,
        in_specs=[SMEM_SPEC] + [VMEM_SPEC] * (1 + SPAN),
        out_specs=[VMEM_SPEC] * SPAN,
        scratch_shapes=[pltpu.VMEM((rows_t.shape[0], C // 2), F32)],
        compiler_params=params(12),
        name="kernel_grad",
    )(info, rows_t, *pieces)


def mirrored(array, pairs):
    route = [
        (place(source, core, block), place(target, core, block))
        for source, target in pairs
        for core in range(2)
        for block in range(BLOCKS)
    ]
    return lax.ppermute(array, AXES, route)


def nearest(halves, source, outer, target):
    return [
        mirrored(halves[0], [(source, target)]),
        mirrored(mirrored(halves[1], [(source, outer)]), [(outer, target)]),
    ]


def shards(base_ids, stem_weight, conv_weight, block_gain, cotangent):
    section = lax.axis_index("section")
    column = lax.axis_index("seq")
    stage, core = section // 2, section % 2
    x, z = column // SPAN, column % SPAN
    late = stage >= STAGES // 2
    block = x * SPAN + jnp.where(late, SPAN - 1 - z, z)
    info = jnp.stack([stage, block, core, x, z]).astype(jnp.int32)
    half = STAGES // 2
    last = STAGES - 1

    wide, own = (WIDE, C), (ROWS + 8, C)
    other_filters = swapped(conv_weight)
    other_gain = swapped(block_gain)
    gains = jnp.where(
        core == 0,
        jnp.concatenate([block_gain, other_gain], 0),
        jnp.concatenate([other_gain, block_gain], 0),
    )

    reach = HALO + STEM_K // 2
    ids = base_ids + 1
    ids = jnp.concatenate(
        [beside(ids[:, -reach:], 1), ids, beside(ids[:, :reach], -1)], 1
    )
    ids = lax.dynamic_index_in_dim(ids, core, 0, keepdims=False)
    letters = jnp.arange(1, BASES + 1, dtype=jnp.int32)
    onehot = jnp.concatenate(
        [ids[offset : offset + WIDE, None] == letters for offset in range(STEM_K)], axis=1
    ).astype(BF16)
    stem = jnp.dot(
        onehot, stem_weight.reshape(STEM_K * BASES, C), preferred_element_type=F32
    ).astype(BF16)
    pieces = (stem[HALO : HALO + ROWS], stem[:HALO], stem[HALO + ROWS :])

    cot = lax.dynamic_index_in_dim(cotangent, core, 0, keepdims=False)

    def cot_moved(rows, shift):
        route = [
            ((2 * last + c) * BLOCKS + b, place(last, c, b + shift))
            for c in range(2)
            for b in range(BLOCKS)
            if 0 <= b + shift < BLOCKS
        ]
        return lax.ppermute(rows, AXES, route)

    cot_pieces = (
        cot_moved(cot, 0),
        cot_moved(cot[ROWS - HALO :], 1),
        cot_moved(cot[:HALO], -1),
    )

    pieces, cot_pieces, gains = lax.optimization_barrier((pieces, cot_pieces, gains))
    info = after(info, (pieces, gains))
    filters, *blanks = paired(info, conv_weight, other_filters, [wide] * 6 + [own] * 2, 44)
    skip_near = skip_far = skip_whole = None
    sums = []
    kept, passed = blanks[0:2], blanks[2:4]
    for tick in range(STAGES):
        results = forward(
            tick,
            info,
            pieces,
            skip_whole if tick > half else None,
            skip_near if tick == half else skip_far,
            filters,
            gains,
            kept,
            passed,
        )
        if tick == half:
            turned_own = transposed(after(conv_weight, results[-1]))
            info = after(info, turned_own)
        elif tick == half + 1:
            turned_other = swapped(after(turned_own, results[-1]))
        elif tick == half + 2:
            turned_pair = after((turned_own, turned_other), results[-1])
            (back_filters,) = paired(info, *turned_pair, [], 12)
            info = after(info, back_filters)
        sums.append(results[0])
        kept = results[1:3]
        if tick < half:
            passed = results[3:5]
        if tick == half - 1:
            skip_near = nearest(results[-2:], tick, 0, tick + 1)
            pieces = hop(results[-5:-2], tick, 1)
            late = after(tuple(passed), pieces)
            skip_whole = mirrored(late[1], [(t, STAGES - t) for t in range(1, half)])
            skip_far = [mirrored(late[0], [(t, last - t) for t in range(half - 1)])]
        elif tick < last:
            pieces = hop(results[-3:], tick, 1)

    acts = kept
    pieces = cot_pieces
    skip_near = skip_far = skip_whole = None
    kept, passed = blanks[6:8], blanks[4:6]
    for tick in reversed(range(STAGES)):
        results = backward(
            tick,
            info,
            pieces,
            skip_whole if tick < half - 1 else None,
            skip_near if tick == half - 1 else skip_far,
            sums[tick],
            back_filters,
            gains,
            kept,
            passed,
        )
        kept = results[:2]
        event = results[-1]
        if tick == last:
            got = swapped(after(acts[1], event))
            info = after(info, got)
        elif tick == last - 1:
            keep, got = after((acts[0], got), event)
            parts = split(info, keep, got)
            by_x, by_z = [parts[0]], [parts[SPAN]]
            by_x.append(turned_x(parts[1], 1))
            info = after(info, by_x)
        elif tick == last - 2:
            later = after(tuple(parts), event)
            by_x += [turned_x(later[d], d) for d in (2, 3)]
            info = after(info, by_x)
        elif tick == half - 2:
            later = after(tuple(parts), event)
            by_z += [turned_z(later[SPAN + d], d) for d in (1, 2)]
            info = after(info, by_z)
        elif tick == half - 3:
            by_x, by_z, later = after((by_x, by_z, tuple(parts)), event)
            by_z = by_z + [turned_z(later[SPAN + 3], 3)]
            rows_x, rows_z = turned(by_x), turned(by_z)
            info = after(info, (rows_x, rows_z))
        if tick >= half:
            passed = results[2:4]
        if tick == half:
            skip_near = nearest(results[-2:], tick, last, tick - 1)
            pieces = hop(results[-5:-2], tick, -1)
            late = after(tuple(passed), pieces)
            skip_whole = mirrored(late[1], [(t, last - 1 - t) for t in range(half, last)])
            skip_far = [mirrored(late[0], [(t, last - t) for t in range(half + 1, STAGES)])]
        elif tick:
            pieces = hop(results[-3:], tick, -1)

    first, second = combined(kept[0], swapped(kept[1]))
    by_x = [first] + [turned_x(first, d) for d in range(1, SPAN)]
    by_z = [second] + [turned_z(second, d) for d in range(1, SPAN)]
    parts = product(4, info, rows_x, by_x)
    total = parts[0].astype(F32)
    for d in range(1, SPAN):
        total = total + turned_z(parts[d], d).astype(F32)
    parts = product(3, after(info, parts), rows_z, by_z)
    other = parts[0].astype(F32)
    for d in range(1, SPAN):
        other = other + turned_x(parts[d], d).astype(F32)
    share = C // BLOCKS
    height = KERNEL * share
    kernel_grad = jnp.concatenate([total[:height].astype(BF16), other.astype(BF16)], axis=1)
    gain_grad = jnp.concatenate([total[height], total[height + 1]], axis=0)
    gain_grad = lax.dynamic_slice_in_dim(gain_grad, column * share, share)
    return kernel_grad.reshape(1, KERNEL, share, C), gain_grad[None]


def solution(mesh):
    placed = (
        P(None, "seq"),
        P(),
        P("section", None, None, None),
        P("section", None),
        P(None, "seq", None),
    )
    return jax.shard_map(
        shards,
        mesh=mesh,
        in_specs=placed,
        out_specs=(P("section", None, "seq", None), P("section", "seq")),
        check_vma=False,
    )
```

```python
import functools

import jax
import jax.numpy as jnp
from jax import lax
from jax.experimental import pallas as pl
from jax.experimental.pallas import tpu as pltpu
from jax.sharding import PartitionSpec as P

KERNEL = 5
STEM_K = 15
BASES = 4
C = 768
ROWS = 128
HALO = 8
WIDE = ROWS + 2 * HALO
PAD = WIDE + 16
NEAR = 32
STAGES = 8
BLOCKS = 16
SPAN = 4
TOKENS = BLOCKS * ROWS
AXES = ("section", "seq")
BF16 = jnp.bfloat16
F32 = jnp.float32
GELU_A = 0.7978845608028654
GELU_B = 0.044715
VMEM_SPEC = pl.BlockSpec(memory_space=pltpu.VMEM)
SMEM_SPEC = pl.BlockSpec(memory_space=pltpu.SMEM)
HBM_SPEC = pl.BlockSpec(memory_space=pltpu.HBM)


def place(stage, core, block):
    x, z = block // SPAN, block % SPAN
    column = x * SPAN + (SPAN - 1 - z if stage >= STAGES // 2 else z)
    return (2 * stage + core) * BLOCKS + column


def swapped(array):
    return lax.ppermute(array, "section", [(i, i ^ 1) for i in range(2 * STAGES)])


def beside(array, shift):
    route = [(b, b + shift) for b in range(BLOCKS) if 0 <= b + shift < BLOCKS]
    return lax.ppermute(array, "seq", route)


def turned_x(array, distance):
    route = [
        (x * SPAN + z, (x + distance) % SPAN * SPAN + z) for x in range(SPAN) for z in range(SPAN)
    ]
    return lax.ppermute(array, "seq", route)


def turned_z(array, distance):
    route = [
        (x * SPAN + z, x * SPAN + (z + distance) % SPAN) for x in range(SPAN) for z in range(SPAN)
    ]
    return lax.ppermute(array, "seq", route)


def parity(array, tick, step, shift=0):
    route = [
        (place(stage, core, block), place(stage + step, core, block + shift))
        for stage in range(tick % 2, STAGES, 2)
        for core in range(2)
        for block in range(BLOCKS)
        if 0 <= stage + step < STAGES and 0 <= block + shift < BLOCKS
    ]
    return lax.ppermute(array, AXES, route)


def hop(pieces, tick, step):
    main, first, last = pieces
    return (
        parity(main, tick, step),
        parity(last, tick, step, 1),
        parity(first, tick, step, -1),
    )


def after(array, event):
    return lax.optimization_barrier((array, event))[0]


def params(mib):
    return pltpu.CompilerParams(vmem_limit_bytes=mib << 20)


def row_mask(block):
    row = lax.broadcasted_iota(jnp.int32, (WIDE, 1), 0) + (block * ROWS - HALO)
    return (row >= 0) & (row < TOKENS)


def joined_rows(parts):
    return jnp.concatenate([part[...].astype(F32) for part in parts], axis=0)


def normed(total):
    scale = lax.rsqrt(jnp.mean(total * total, axis=-1, keepdims=True) + 1e-06)
    return total * scale, scale


def send_pair(core, source, first, second, sems):
    def start(one, two):
        pltpu.make_async_copy(source.at[0], one, sems.at[0]).start()
        pltpu.make_async_copy(source.at[1], two, sems.at[1]).start()

    pl.when(core == 0)(lambda: start(first, second))
    pl.when(core != 0)(lambda: start(second, first))


def wait_pair(source, first, sems):
    for index in range(2):
        pltpu.make_async_copy(source.at[index], first, sems.at[index]).wait()


def hbm(shape, dtype):
    return pltpu.HBM(shape, dtype)


def forward_kernel(tick, info, *refs):
    half = STAGES // 2
    skips = tick >= half
    last = tick == STAGES - 1
    refs = list(refs)
    main, left, right = refs[:3]
    refs = refs[3:]
    own_skip = refs.pop(0) if tick > half else None
    skip_b = [refs.pop(0) for _ in range(2 if tick == half else 1)] if skips else None
    filters, gains = refs[:2]
    refs = refs[4 if skips else 6 :]
    sums_out, keep_out, give_out = refs[:3]
    refs = refs[3:]
    middle_out, whole_out = (refs.pop(0), refs.pop(0)) if not skips else (None, None)
    out, first_rows, last_rows = (refs.pop(0), refs.pop(0), refs.pop(0)) if not last else (None,) * 3
    near = [refs.pop(0), refs.pop(0)] if tick == half - 1 else None
    whole, middle, pad, sums, acts, sems = refs

    @pl.when(info[0] == tick)
    def _():
        core = info[2]
        keep = row_mask(info[1])
        whole[0:HALO, :] = left[...]
        whole[HALO : HALO + ROWS, :] = main[...]
        whole[HALO + ROWS : WIDE, :] = right[...]
        pad[0:8, :] = jnp.zeros((8, C), F32)
        pad[PAD - 8 : PAD, :] = jnp.zeros((8, C), F32)
        copies = []
        if not skips:
            copies = [pltpu.make_async_copy(whole, whole_out, sems.at[4])]
            copies[0].start()
            if near is None:
                copies.append(pltpu.make_async_copy(middle, middle_out, sems.at[5]))
        sum_copies = [
            pltpu.make_async_copy(sums.at[i], sums_out.at[i], sems.at[i]) for i in range(2)
        ]

        def activated(total, which):
            sums[which] = total
            sum_copies[which].start()
            value, _ = normed(total)
            value = jax.nn.gelu(value * gains[which : which + 1, :])
            rounded = jnp.where(keep, value, 0.0).astype(BF16)
            acts[which] = rounded
            pad[8 : 8 + WIDE, :] = rounded.astype(F32)

        def conv(total, which):
            for tap in range(KERNEL):
                start = 6 + tap
                rows = pad[start : start + WIDE, :].astype(BF16)
                total = total + jnp.dot(rows, filters[which, tap], preferred_element_type=F32)
            return total

        total = whole[...].astype(F32)
        if tick == half:
            total = total + total
        elif skips:
            total = total + own_skip[...].astype(F32)
        activated(total, 0)
        value = conv(total, 0).astype(BF16)
        if near is not None:
            near[0][...] = value[:NEAR]
            near[1][...] = value[NEAR:]
        elif not skips:
            middle[...] = value
            copies[1].start()
        total = value.astype(F32)
        if skips:
            total = total + joined_rows(skip_b)
        activated(total, 1)
        send_pair(core, acts, keep_out, give_out, sems.at[pl.ds(2, 2)])
        if not last:
            value = conv(total, 1)
            out[...] = value[HALO : HALO + ROWS].astype(BF16)
            first_rows[...] = value[HALO : 2 * HALO].astype(BF16)
            last_rows[...] = value[ROWS : HALO + ROWS].astype(BF16)
        for copy in sum_copies + copies:
            copy.wait()
        wait_pair(acts, keep_out, sems.at[pl.ds(2, 2)])


def forward(tick, info, pieces, skip_a, skip_b, filters, gains, kept, passed):
    last = tick == STAGES - 1
    skips = tick >= STAGES // 2
    args = list(pieces)
    if skip_a is not None:
        args.append(skip_a)
    if skip_b is not None:
        args += skip_b
    edge = jax.ShapeDtypeStruct((HALO, C), BF16)
    held = list(kept) + ([] if skips else list(passed))
    shapes = [hbm((2, WIDE, C), F32)] + [hbm(a.shape, a.dtype) for a in held]
    vmem_shapes = [] if last else [jax.ShapeDtypeStruct((ROWS, C), BF16), edge, edge]
    if tick == STAGES // 2 - 1:
        vmem_shapes += [jax.ShapeDtypeStruct((n, C), BF16) for n in (NEAR, WIDE - NEAR)]
    count = 3 + len(args)
    return pl.pallas_call(
        functools.partial(forward_kernel, tick),
        out_shape=shapes + vmem_shapes,
        in_specs=[SMEM_SPEC] + [VMEM_SPEC] * (len(args) + 2) + [HBM_SPEC] * len(held),
        out_specs=[HBM_SPEC] * len(shapes) + [VMEM_SPEC] * len(vmem_shapes),
        scratch_shapes=[
            pltpu.VMEM((WIDE, C), BF16),
            pltpu.VMEM((WIDE, C), BF16),
            pltpu.VMEM((PAD, C), F32),
            pltpu.VMEM((2, WIDE, C), F32),
            pltpu.VMEM((2, WIDE, C), BF16),
            pltpu.SemaphoreType.DMA((6,)),
        ],
        input_output_aliases={count + i: 1 + i for i in range(len(held))},
        compiler_params=params(12),
        name="forward_stage",
    )(info, *args, filters, gains, *held)


def backward_kernel(tick, info, *refs):
    half = STAGES // 2
    joined = tick < half
    refs = list(refs)
    main, left, right = refs[:3]
    refs = refs[3:]
    skip_a = refs.pop(0) if tick < half - 1 else None
    skip_b = [refs.pop(0) for _ in range(2 if tick == half - 1 else 1)] if joined else None
    filters, gains, sums_in = refs[:3]
    refs = refs[5 if joined else 7 :]
    keep_out, give_out = refs[:2]
    refs = refs[2:]
    middle_out, whole_out = (refs.pop(0), refs.pop(0)) if not joined else (None, None)
    out, first_rows, last_rows = (refs.pop(0), refs.pop(0), refs.pop(0)) if tick else (None,) * 3
    near = [refs.pop(0), refs.pop(0)] if tick == half else None
    whole, middle, pad, sums, grads, sems = refs

    @pl.when(info[0] == tick)
    def _():
        core = info[2]
        sum_copies = [
            pltpu.make_async_copy(sums_in.at[i], sums.at[i], sems.at[i]) for i in range(2)
        ]
        sum_copies[1].start()
        sum_copies[0].start()
        keep = row_mask(info[1])
        whole[0:HALO, :] = left[...]
        whole[HALO : HALO + ROWS, :] = main[...]
        whole[HALO + ROWS : WIDE, :] = right[...]
        pad[0:8, :] = jnp.zeros((8, C), F32)
        pad[PAD - 8 : PAD, :] = jnp.zeros((8, C), F32)
        copies = []
        if not joined:
            copies = [pltpu.make_async_copy(whole, whole_out, sems.at[4])]
            copies[0].start()
            if near is None:
                copies.append(pltpu.make_async_copy(middle, middle_out, sems.at[5]))

        def pull(grad, which, last):
            grads[which, 0:ROWS, :] = grad[HALO : HALO + ROWS].astype(BF16)
            pad[8 : 8 + WIDE, :] = grad
            grad_act = jnp.zeros((WIDE, C), F32)
            for tap in range(KERNEL):
                start = 10 - tap
                rows = pad[start : start + WIDE, :].astype(BF16)
                grad_act = grad_act + jnp.dot(
                    rows, filters[which, tap], preferred_element_type=F32
                )
            sum_copies[which].wait()
            gain = gains[which : which + 1, :]
            value, scale = normed(sums[which])
            inner = value * gain
            square = inner * inner
            tanh = jnp.tanh(GELU_A * (inner + GELU_B * (square * inner)))
            slope = 0.5 * (1.0 + tanh) + (0.5 * GELU_A) * inner * (1.0 - tanh * tanh) * (
                1.0 + (3.0 * GELU_B) * square
            )
            grad_inner = grad_act * slope
            product = (grad_inner * value)[HALO : HALO + ROWS]
            grad_gain = jnp.sum(product, axis=0, keepdims=True)
            grads[which, ROWS : ROWS + 8, :] = jnp.broadcast_to(grad_gain, (8, C)).astype(BF16)
            if last:
                return None
            grad_value = grad_inner * gain
            mean = jnp.mean(grad_value * value, axis=-1, keepdims=True)
            result = grad + scale * (grad_value - value * mean)
            return jnp.where(keep, result, 0.0).astype(BF16)

        grad = whole[...].astype(F32)
        if tick == half - 1:
            grad = grad + grad
        elif joined:
            grad = grad + skip_a[...].astype(F32)
        grad = grad.astype(BF16).astype(F32)
        value = pull(grad, 1, False)
        if near is not None:
            near[0][...] = value[:NEAR]
            near[1][...] = value[NEAR:]
        elif not joined:
            middle[...] = value
            copies[1].start()
        grad = value.astype(F32)
        if joined:
            grad = (grad + joined_rows(skip_b)).astype(BF16).astype(F32)
        value = pull(grad, 0, tick == 0)
        send_pair(core, grads, keep_out, give_out, sems.at[pl.ds(2, 2)])
        if tick:
            value = value.astype(F32)
            out[...] = value[HALO : HALO + ROWS].astype(BF16)
            first_rows[...] = value[HALO : 2 * HALO].astype(BF16)
            last_rows[...] = value[ROWS : HALO + ROWS].astype(BF16)
        for copy in copies:
            copy.wait()
        wait_pair(grads, keep_out, sems.at[pl.ds(2, 2)])


def backward(tick, info, pieces, skip_a, skip_b, sums, filters, gains, kept, passed):
    joined = tick < STAGES // 2
    args = list(pieces)
    if skip_a is not None:
        args.append(skip_a)
    if skip_b is not None:
        args += skip_b
    edge = jax.ShapeDtypeStruct((HALO, C), BF16)
    held = list(kept) + ([] if joined else list(passed))
    shapes = [hbm(a.shape, a.dtype) for a in held]
    vmem_shapes = [jax.ShapeDtypeStruct((ROWS, C), BF16), edge, edge] if tick else []
    if tick == STAGES // 2:
        vmem_shapes += [jax.ShapeDtypeStruct((n, C), BF16) for n in (NEAR, WIDE - NEAR)]
    count = 4 + len(args)
    return pl.pallas_call(
        functools.partial(backward_kernel, tick),
        out_shape=shapes + vmem_shapes,
        in_specs=[SMEM_SPEC] + [VMEM_SPEC] * (len(args) + 2) + [HBM_SPEC] * (1 + len(held)),
        out_specs=[HBM_SPEC] * len(shapes) + [VMEM_SPEC] * len(vmem_shapes),
        scratch_shapes=[
            pltpu.VMEM((WIDE, C), BF16),
            pltpu.VMEM((WIDE, C), BF16),
            pltpu.VMEM((PAD, C), F32),
            pltpu.VMEM((2, WIDE, C), F32),
            pltpu.VMEM((2, ROWS + 8, C), BF16),
            pltpu.SemaphoreType.DMA((6,)),
        ],
        input_output_aliases={count + i: i for i in range(len(held))},
        compiler_params=params(12),
        name="backward_stage",
    )(info, *args, filters, gains, sums, *held)


def pair_kernel(info, own, other, pair, *refs):
    core, sems = info[2], refs[-1]
    copies = [
        pltpu.make_async_copy(own.at[0], pair.at[core], sems.at[0]),
        pltpu.make_async_copy(other.at[0], pair.at[1 - core], sems.at[1]),
    ]
    for copy in copies:
        copy.start()
    for copy in copies:
        copy.wait()


def transpose_kernel(own, out, source, result, sems_in, sems_out):
    def load(tap, slot):
        return pltpu.make_async_copy(own.at[0, tap], source.at[slot], sems_in.at[slot])

    def save(tap, slot):
        return pltpu.make_async_copy(result.at[slot], out.at[0, tap], sems_out.at[slot])

    load(0, 0).start()
    for tap in range(KERNEL):
        slot = tap % 2
        if tap + 1 < KERNEL:
            load(tap + 1, 1 - slot).start()
        load(tap, slot).wait()
        if tap >= 2:
            save(tap - 2, slot).wait()

        def part(index, _):
            rows = pl.ds(pl.multiple_of(index * 256, 256), 256)
            row = lax.broadcasted_iota(jnp.int32, (256, C), 0) + index * 256
            eye = (row == lax.broadcasted_iota(jnp.int32, (256, C), 1)).astype(BF16)
            result[slot, rows, :] = lax.dot_general(
                eye, source[slot], (((1,), (1,)), ((), ())), preferred_element_type=F32
            ).astype(BF16)
            return 0

        lax.fori_loop(0, C // 256, part, 0)
        save(tap, slot).start()
    for tap in range(KERNEL - 2, KERNEL):
        save(tap, tap % 2).wait()


def transposed(own):
    return pl.pallas_call(
        transpose_kernel,
        out_shape=hbm(own.shape, own.dtype),
        in_specs=[HBM_SPEC],
        out_specs=HBM_SPEC,
        scratch_shapes=[
            pltpu.VMEM((2, C, C), BF16),
            pltpu.VMEM((2, C, C), BF16),
            pltpu.SemaphoreType.DMA((2,)),
            pltpu.SemaphoreType.DMA((2,)),
        ],
        compiler_params=params(12),
        name="turn_filters",
    )(own)


def paired(info, own, other, blanks, mib):
    return pl.pallas_call(
        pair_kernel,
        out_shape=[pltpu.VMEM((2, *own.shape[1:]), own.dtype)]
        + [hbm(shape, BF16) for shape in blanks],
        in_specs=[SMEM_SPEC, HBM_SPEC, HBM_SPEC],
        out_specs=[VMEM_SPEC] + [HBM_SPEC] * len(blanks),
        scratch_shapes=[pltpu.SemaphoreType.DMA((2,))],
        compiler_params=params(mib),
        name="weight_pair",
    )(info, own, other)


def split_kernel(info, keep, got, *outs):
    share = C // BLOCKS
    by_x, by_z = outs[:SPAN], outs[SPAN:]
    for index, array in enumerate((keep, got)):
        rows = array[...]
        for part in range(SPAN):
            one = rows[:, part * SPAN * share : (part + 1) * SPAN * share]
            other = jnp.concatenate(
                [
                    rows[:, (turn * SPAN + part) * share : (turn * SPAN + part + 1) * share]
                    for turn in range(SPAN)
                ],
                axis=1,
            )
            for place_of, piece, targets in ((3, one, by_x), (4, other, by_z)):
                for distance, out in enumerate(targets):

                    @pl.when(lax.rem(info[place_of] + distance, SPAN) == part)
                    def _():
                        out[index] = piece


def split(info, keep, got):
    return pl.pallas_call(
        split_kernel,
        out_shape=[jax.ShapeDtypeStruct((2, WIDE, C // SPAN), BF16)] * (2 * SPAN),
        in_specs=[SMEM_SPEC, VMEM_SPEC, VMEM_SPEC],
        out_specs=[VMEM_SPEC] * (2 * SPAN),
        compiler_params=params(10),
        name="split_rows",
    )(info, keep, got)


def combine_kernel(keep, got, first, second):
    width = C // 2
    for index, array in enumerate((keep, got)):
        rows = slice(index * ROWS, (index + 1) * ROWS)
        first[rows, :] = array[0:ROWS, 0:width]
        second[rows, :] = array[0:ROWS, width:C]
    gain = keep[ROWS : ROWS + 8, :].astype(F32) + got[ROWS : ROWS + 8, :].astype(F32)
    row = lax.broadcasted_iota(jnp.int32, (8, width), 0)
    gain = jnp.where(row == 0, gain[:, 0:width], gain[:, width:C])
    first[2 * ROWS : 2 * ROWS + 8, :] = gain.astype(BF16)


def combined(keep, got):
    return pl.pallas_call(
        combine_kernel,
        out_shape=[
            jax.ShapeDtypeStruct((2 * ROWS + 8, C // 2), BF16),
            jax.ShapeDtypeStruct((2 * ROWS, C // 2), BF16),
        ],
        in_specs=[VMEM_SPEC] * 2,
        out_specs=[VMEM_SPEC] * 2,
        compiler_params=params(8),
        name="combine_rows",
    )(keep, got)


def turn_kernel(*refs):
    pieces, out = refs[:SPAN], refs[SPAN]
    width = C // SPAN
    for index, piece in enumerate(pieces):
        for micro in range(2):
            rows = piece[micro].astype(F32).T
            column = (2 * index + micro) * ROWS
            for tap in range(KERNEL):
                start = HALO - 2 + tap
                out[tap * width : (tap + 1) * width, column : column + ROWS] = rows[
                    :, start : start + ROWS
                ].astype(BF16)


def turned(pieces):
    width = C // SPAN
    return pl.pallas_call(
        turn_kernel,
        out_shape=jax.ShapeDtypeStruct((KERNEL * width, SPAN * 2 * ROWS), BF16),
        in_specs=[VMEM_SPEC] * SPAN,
        out_specs=VMEM_SPEC,
        compiler_params=params(12),
        name="turn_rows",
    )(*pieces)


def product_kernel(place_of, info, rows_t, *refs):
    pieces, outs, total = refs[:SPAN], refs[SPAN : 2 * SPAN], refs[-1]
    count = 2 * ROWS
    for index, piece in enumerate(pieces):
        term = jnp.dot(
            rows_t[:, index * count : (index + 1) * count],
            piece[0:count, :],
            preferred_element_type=F32,
        )
        total[...] = term if index == 0 else total[...] + term
    width = C // SPAN
    share = width // SPAN
    height = KERNEL * share
    extra = pieces[0].shape[0] - count
    if extra:
        gain = sum(piece[count : count + extra, :].astype(F32) for piece in pieces).astype(BF16)
    for distance, out in enumerate(outs):
        target = lax.rem(info[place_of] + distance, SPAN)
        for tap in range(KERNEL):
            start = pl.multiple_of(tap * width + target * share, 8)
            out[tap * share : (tap + 1) * share, :] = total[pl.ds(start, share), :].astype(BF16)
        if extra:
            out[height : height + extra, :] = gain


def product(place_of, info, rows_t, pieces):
    height = rows_t.shape[0] // SPAN + pieces[0].shape[0] - 2 * ROWS
    return pl.pallas_call(
        functools.partial(product_kernel, place_of),
        out_shape=[jax.ShapeDtypeStruct((height, C // 2), BF16)] * SPAN,
        in_specs=[SMEM_SPEC] + [VMEM_SPEC] * (1 + SPAN),
        out_specs=[VMEM_SPEC] * SPAN,
        scratch_shapes=[pltpu.VMEM((rows_t.shape[0], C // 2), F32)],
        compiler_params=params(12),
        name="kernel_grad",
    )(info, rows_t, *pieces)


def mirrored(array, pairs):
    route = [
        (place(source, core, block), place(target, core, block))
        for source, target in pairs
        for core in range(2)
        for block in range(BLOCKS)
    ]
    return lax.ppermute(array, AXES, route)


def nearest(halves, source, outer, target):
    return [
        mirrored(halves[0], [(source, target)]),
        mirrored(mirrored(halves[1], [(source, outer)]), [(outer, target)]),
    ]


def shards(base_ids, stem_weight, conv_weight, block_gain, cotangent):
    section = lax.axis_index("section")
    column = lax.axis_index("seq")
    stage, core = section // 2, section % 2
    x, z = column // SPAN, column % SPAN
    late = stage >= STAGES // 2
    block = x * SPAN + jnp.where(late, SPAN - 1 - z, z)
    info = jnp.stack([stage, block, core, x, z]).astype(jnp.int32)
    half = STAGES // 2
    last = STAGES - 1

    wide, own = (WIDE, C), (ROWS + 8, C)
    other_filters = swapped(conv_weight)
    other_gain = swapped(block_gain)
    gains = jnp.where(
        core == 0,
        jnp.concatenate([block_gain, other_gain], 0),
        jnp.concatenate([other_gain, block_gain], 0),
    )

    reach = HALO + STEM_K // 2
    ids = base_ids + 1
    ids = jnp.concatenate(
        [beside(ids[:, -reach:], 1), ids, beside(ids[:, :reach], -1)], 1
    )
    ids = lax.dynamic_index_in_dim(ids, core, 0, keepdims=False)
    letters = jnp.arange(1, BASES + 1, dtype=jnp.int32)
    onehot = jnp.concatenate(
        [ids[offset : offset + WIDE, None] == letters for offset in range(STEM_K)], axis=1
    ).astype(BF16)
    stem = jnp.dot(
        onehot, stem_weight.reshape(STEM_K * BASES, C), preferred_element_type=F32
    ).astype(BF16)
    pieces = (stem[HALO : HALO + ROWS], stem[:HALO], stem[HALO + ROWS :])

    cot = lax.dynamic_index_in_dim(cotangent, core, 0, keepdims=False)

    def cot_moved(rows, shift):
        route = [
            ((2 * last + c) * BLOCKS + b, place(last, c, b + shift))
            for c in range(2)
            for b in range(BLOCKS)
            if 0 <= b + shift < BLOCKS
        ]
        return lax.ppermute(rows, AXES, route)

    cot_pieces = (
        cot_moved(cot, 0),
        cot_moved(cot[ROWS - HALO :], 1),
        cot_moved(cot[:HALO], -1),
    )

    pieces, cot_pieces, gains = lax.optimization_barrier((pieces, cot_pieces, gains))
    info = after(info, (pieces, gains))
    filters, *blanks = paired(info, conv_weight, other_filters, [wide] * 6 + [own] * 2, 44)
    skip_near = skip_far = skip_whole = None
    sums = []
    kept, passed = blanks[0:2], blanks[2:4]
    for tick in range(STAGES):
        results = forward(
            tick,
            info,
            pieces,
            skip_whole if tick > half else None,
            skip_near if tick == half else skip_far,
            filters,
            gains,
            kept,
            passed,
        )
        if tick == half:
            turned_own = transposed(after(conv_weight, results[-1]))
            info = after(info, turned_own)
        elif tick == half + 1:
            turned_other = swapped(after(turned_own, results[-1]))
        elif tick == half + 2:
            turned_pair = after((turned_own, turned_other), results[-1])
            (back_filters,) = paired(info, *turned_pair, [], 12)
            info = after(info, back_filters)
        sums.append(results[0])
        kept = results[1:3]
        if tick < half:
            passed = results[3:5]
        if tick == half - 1:
            skip_near = nearest(results[-2:], tick, 0, tick + 1)
            pieces = hop(results[-5:-2], tick, 1)
            late = after(tuple(passed), pieces)
            skip_whole = mirrored(late[1], [(t, STAGES - t) for t in range(1, half)])
            skip_far = [mirrored(late[0], [(t, last - t) for t in range(half - 1)])]
        elif tick < last:
            pieces = hop(results[-3:], tick, 1)

    acts = kept
    pieces = cot_pieces
    skip_near = skip_far = skip_whole = None
    kept, passed = blanks[6:8], blanks[4:6]
    for tick in reversed(range(STAGES)):
        results = backward(
            tick,
            info,
            pieces,
            skip_whole if tick < half - 1 else None,
            skip_near if tick == half - 1 else skip_far,
            sums[tick],
            back_filters,
            gains,
            kept,
            passed,
        )
        kept = results[:2]
        event = results[-1]
        if tick == last:
            got = swapped(after(acts[1], event))
            info = after(info, got)
        elif tick == last - 1:
            keep, got = after((acts[0], got), event)
            parts = split(info, keep, got)
            by_x, by_z = [parts[0]], [parts[SPAN]]
            by_x.append(turned_x(parts[1], 1))
            info = after(info, by_x)
        elif tick == last - 2:
            later = after(tuple(parts), event)
            by_x += [turned_x(later[d], d) for d in (2, 3)]
            info = after(info, by_x)
        elif tick == half - 2:
            later = after(tuple(parts), event)
            by_z += [turned_z(later[SPAN + d], d) for d in (1, 2)]
            info = after(info, by_z)
        elif tick == half - 3:
            by_x, by_z, later = after((by_x, by_z, tuple(parts)), event)
            by_z = by_z + [turned_z(later[SPAN + 3], 3)]
            rows_x, rows_z = turned(by_x), turned(by_z)
            info = after(info, (rows_x, rows_z))
        if tick >= half:
            passed = results[2:4]
        if tick == half:
            skip_near = nearest(results[-2:], tick, last, tick - 1)
            pieces = hop(results[-5:-2], tick, -1)
            late = after(tuple(passed), pieces)
            skip_whole = mirrored(late[1], [(t, last - 1 - t) for t in range(half, last)])
            skip_far = [mirrored(late[0], [(t, last - t) for t in range(half + 1, STAGES)])]
        elif tick:
            pieces = hop(results[-3:], tick, -1)

    first, second = combined(kept[0], swapped(kept[1]))
    by_x = [first] + [turned_x(first, d) for d in range(1, SPAN)]
    by_z = [second] + [turned_z(second, d) for d in range(1, SPAN)]
    parts = product(4, info, rows_x, by_x)
    total = parts[0].astype(F32)
    for d in range(1, SPAN):
        total = total + turned_z(parts[d], d).astype(F32)
    parts = product(3, after(info, parts), rows_z, by_z)
    other = parts[0].astype(F32)
    for d in range(1, SPAN):
        other = other + turned_x(parts[d], d).astype(F32)
    share = C // BLOCKS
    height = KERNEL * share
    kernel_grad = jnp.concatenate([total[:height].astype(BF16), other.astype(BF16)], axis=1)
    gain_grad = jnp.concatenate([total[height], total[height + 1]], axis=0)
    gain_grad = lax.dynamic_slice_in_dim(gain_grad, column * share, share)
    return kernel_grad.reshape(1, KERNEL, share, C), gain_grad[None]


def solution(mesh):
    placed = (
        P(None, "seq"),
        P(),
        P("section", None, None, None),
        P("section", None),
        P(None, "seq", None),
    )
    return jax.shard_map(
        shards,
        mesh=mesh,
        in_specs=placed,
        out_specs=(P("section", None, "seq", None), P("section", "seq")),
        check_vma=False,
    )
```
